32 devices in a mesh: seq: 8 (over z, y), head: 4 (over x, core).
Axes of the slice: x: 2, y: 2, z: 4, core: 2. Of those that a mesh axis runs over, the one named last changes fastest.
Arguments:
- tokens: bfloat16 [2048, 2048], P('seq'), may hold values from -6 to 6
- first_gain: float32 [2048], replicated, may hold values from 0.5 to 1.5
- query_weight: bfloat16 [2048, 2048], P(None, 'head'), may hold values from -0.125 to 0.125
- key_weight: bfloat16 [2048, 2048], P(None, 'head'), may hold values from -0.125 to 0.125
- value_weight: bfloat16 [2048, 4096], P(None, 'head'), may hold values from -0.125 to 0.125
- gate_weight: bfloat16 [2048, 4096], P(None, 'head'), may hold values from -0.125 to 0.125
- output_weight: bfloat16 [4096, 2048], P('head'), may hold values from -0.125 to 0.125
- second_gain: float32 [2048], replicated, may hold values from 0.5 to 1.5
- gelu_weight: bfloat16 [2048, 4096], P(None, 'head'), may hold values from -0.125 to 0.125
- linear_weight: bfloat16 [2048, 4096], P(None, 'head'), may hold values from -0.125 to 0.125
- down_weight: bfloat16 [4096, 2048], P('head'), may hold values from -0.09375 to 0.09375
- log_decay: float32 [8, 2048], P('head', 'seq'), may hold values from -1 to 0, as said below
- first_start: int32 [8], P('seq'), may hold values from 0 to 256, as said below
- cotangent: bfloat16 [2048, 2048], P('seq'), may hold values from -6 to 6
Outputs:
- output: bfloat16 [2048, 2048], P('seq')
- grad_tokens: bfloat16 [2048, 2048], P('seq')
- grad_first_gain: float32 [2048], P('seq')
- grad_query: float32 [2048, 2048], P('seq', 'head')
- grad_key: float32 [2048, 2048], P('seq', 'head')
- grad_value: float32 [2048, 4096], P('seq', 'head')
- grad_gate: float32 [2048, 4096], P('seq', 'head')
- grad_output: float32 [4096, 2048], P('head', 'seq')
- grad_second_gain: float32 [2048], P('seq')
- grad_gelu: float32 [2048, 4096], P('seq', 'head')
- grad_linear: float32 [2048, 4096], P('seq', 'head')
- grad_down: float32 [4096, 2048], P('head', 'seq')
The draws below stay inside these ranges and needn't reach their ends.
Inputs may be any that keep to these rules, and one draw needn't show every extreme that they name: `first_start`: each shard of 256 tokens holds at most one sequence start; the value 256 means that no sequence starts in the shard; the first shard's value is 0. `log_decay`: every entry is negative.
All inputs are finite; a program needn't handle non-finite values.
Results may differ from the reference program's by a relative error of at most 0.011.
The reference program's roundings to bfloat16 on the way count: a program that leaves them out, or rounds other values in their place, can miss the bound.
Values sent between devices are 32-bit elements; how exact they have to be, the bound alone decides.
No kernel may reach another device: no remote copies, remote signals or barrier semaphores. Data moves between devices by JAX's collectives and lax.ppermute only.
A program may use at most 256 MiB of HBM per device.

```python
import math
import jax
import jax.numpy as jnp
from jax import lax

D = 2048
RETENTION_HEADS = 8
DK = 256
DV = 512
FF = 4096
TOK_DEV = 256
BLK = 256
SEQS = 2
QK = 2048
VW = 4096
TOTAL_TOKENS = 2048


def draw_log_decay(key, part):
    every_key = jax.random.split(key, 7)
    sequence_length = TOTAL_TOKENS // SEQS
    chosen = jax.random.uniform(every_key[0], (RETENTION_HEADS, 1))
    fast_head = chosen < 0.5
    fast_rate = jax.random.uniform(every_key[1], (RETENTION_HEADS, 1), minval=1.0 / 50.0, maxval=1.0 / 30.0)
    slow_rate = jax.random.uniform(every_key[2], (RETENTION_HEADS, 1), minval=0.05, maxval=0.5) / sequence_length
    baseline_decay = jnp.where(fast_head, fast_rate, slow_rate)
    jitter_level = jnp.exp(jax.random.uniform(every_key[3], (RETENTION_HEADS, TOTAL_TOKENS), minval=-0.7, maxval=0.7))
    split_factor = jnp.exp(jax.random.uniform(every_key[4], (RETENTION_HEADS, TOTAL_TOKENS // TOK_DEV, 1), minval=-0.5, maxval=0.5))
    split_factor = jnp.broadcast_to(split_factor, (RETENTION_HEADS, TOTAL_TOKENS // TOK_DEV, TOK_DEV)).reshape(RETENTION_HEADS, TOTAL_TOKENS)
    spike_position = jax.random.uniform(every_key[5], (RETENTION_HEADS, TOTAL_TOKENS)) < 2.0 / sequence_length
    spike_length = jax.random.uniform(every_key[6], (RETENTION_HEADS, TOTAL_TOKENS), minval=0.22, maxval=0.69)
    decay_rates = -(baseline_decay * jitter_level * split_factor) - jnp.where(spike_position, spike_length, 0.0)
    return decay_rates.astype(jnp.float32)


def draw_first_start(key, part):
    sequence_length = TOTAL_TOKENS // SEQS
    spread = sequence_length // 4
    shifts = jax.random.randint(key, (SEQS - 1,), -spread, spread + 1)
    bounds = jnp.arange(1, SEQS, dtype=jnp.int32) * sequence_length + shifts
    shard_begin = jnp.arange(TOTAL_TOKENS // TOK_DEV, dtype=jnp.int32) * TOK_DEV
    inside = (bounds[None, :] >= shard_begin[:, None]) & (bounds[None, :] < shard_begin[:, None] + TOK_DEV)
    offset = jnp.min(jnp.where(inside, bounds[None, :] - shard_begin[:, None], TOK_DEV), axis=1)
    offset = jnp.where(shard_begin == 0, 0, offset)
    return offset.astype(jnp.int32)


def raised(entries, own_key, source, target, shards_of, factor):
    owner, partner = [(jnp.arange(entries.shape[dim]) // (entries.shape[dim] // shards_of)).reshape([-1 if axis == dim else 1 for axis in range(entries.ndim)]) for dim in (source, target)]
    chosen = jax.random.permutation(own_key, shards_of)[partner]
    strong = (owner == chosen) | (owner == (partner + shards_of // 2) % shards_of)
    return jnp.where(strong, factor * entries, entries)


def block_levels(stream_key, shape, cuts, least, top_value):
    def one(dim, blocks):
        heights = jax.random.uniform(jax.random.fold_in(jax.random.fold_in(stream_key, 6), dim), (blocks,), jnp.float32, least / len(cuts), top_value / len(cuts))
        return jnp.repeat(jnp.exp(heights), shape[dim] // blocks).reshape((-1,) + (1,) * (len(shape) - dim - 1))

    factor_of = one(*cuts[0])
    for cut in cuts[1:]:
        factor_of = factor_of * one(*cut)
    return factor_of


def normal_values(own_key, dims, deviation, bound, cuts=(), held_as=jnp.bfloat16):
    values = deviation * jax.random.normal(own_key, dims, jnp.float32)
    if cuts:
        values = values * block_levels(own_key, dims, cuts, -0.22, 0.18)
    return jnp.clip(values, -bound, bound).astype(held_as)


def bell_draw_with(own_key, shape, deviation, bound, pieces, heavy, kind=jnp.bfloat16):
    values = deviation * jax.random.normal(own_key, shape, jnp.float32)
    if pieces:
        values = values * block_levels(own_key, shape, pieces, -0.22, 0.18)
    return jnp.clip(raised(values, jax.random.fold_in(own_key, 3), *heavy), -bound, bound).astype(kind)


def setup_inputs(seed: int = 0) -> dict:
    key_of = jax.random.split(jax.random.key(seed), 15)
    tokens = normal_values(key_of[0], (TOTAL_TOKENS, D), 1.0, 6.0, ((0, 8),))
    first_gain = jnp.clip(1.0 + 0.1 * jax.random.normal(key_of[1], (D,), jnp.float32), 0.5, 1.5)
    query_weight = normal_values(key_of[2], (D, QK), D ** -0.5, 0.125, ((1, 4),))
    key_weight = normal_values(key_of[3], (D, QK), D ** -0.5, 0.125, ((1, 4),))
    value_weight = normal_values(key_of[4], (D, VW), D ** -0.5, 0.125, ((1, 4),))
    gate_weight = normal_values(key_of[5], (D, VW), D ** -0.5, 0.125, ((1, 4),))
    output_weight = normal_values(key_of[6], (VW, D), (VW // 2) ** -0.5, 0.125, ((0, 4),))
    second_gain = jnp.clip(1.0 + 0.1 * jax.random.normal(key_of[7], (D,), jnp.float32), 0.5, 1.5)
    gelu_weight = normal_values(key_of[8], (D, FF), D ** -0.5, 0.125, ((1, 4),))
    linear_weight = normal_values(key_of[9], (D, FF), D ** -0.5, 0.125, ((1, 4),))
    down_weight = normal_values(key_of[10], (FF, D), FF ** -0.5, 0.09375, ((0, 4),))
    log_decay = draw_log_decay(jax.random.fold_in(key_of[14], 71), 0)
    first_start = draw_first_start(jax.random.fold_in(key_of[14], 71), 0)
    cotangent = bell_draw_with(key_of[13], (TOTAL_TOKENS, D), 1.0, 6.0, ((0, 8),), (0, 1, 8, 2.0))
    return dict(tokens=tokens, first_gain=first_gain, query_weight=query_weight, key_weight=key_weight, value_weight=value_weight, gate_weight=gate_weight, output_weight=output_weight, second_gain=second_gain, gelu_weight=gelu_weight, linear_weight=linear_weight, down_weight=down_weight, log_decay=log_decay, first_start=first_start, cotangent=cotangent)


maximum_precision = lax.Precision.HIGHEST
eps_norm = 1e-05

@jax.custom_vjp
def low(v):
    return lax.optimization_barrier(v.astype(jnp.bfloat16)).astype(jnp.float32)

@jax.custom_vjp
def low_back(v):
    return v

def low_keep(v):
    return (low(v), None)

def low_pass(kept, grad):
    return (grad,)

def back_keep(v):
    return (v, None)

def back_low(kept, grad):
    return (low(grad),)
low.defvjp(low_keep, low_pass)
low_back.defvjp(back_keep, back_low)

def matmul(left_side, right_side):
    return jnp.dot(left_side, right_side, precision=maximum_precision, preferred_element_type=jnp.float32)

def layer_norm(activity, gain_row):
    centre = lax.optimization_barrier(jnp.mean(activity, axis=-1, keepdims=True))
    centred = activity - centre
    spread = lax.optimization_barrier(jnp.mean(centred * centred, axis=-1, keepdims=True))
    return centred * lax.rsqrt(spread + eps_norm) * gain_row

def group_norm(activity):
    centre = lax.optimization_barrier(jnp.mean(activity, axis=-1, keepdims=True))
    centred = activity - centre
    spread = lax.optimization_barrier(jnp.mean(centred * centred, axis=-1, keepdims=True))
    return centred * lax.rsqrt(spread + eps_norm)

def retain_block(carried, query_slice, key_slice, value_slice, rate_part, flag_part):
    cumulative = jnp.cumsum(rate_part, axis=1)
    started = jnp.cumsum(flag_part)
    block_len = flag_part.shape[0]
    position = jnp.arange(block_len)
    causal_same = (started[:, None] == started[None, :]) & (position[:, None] >= position[None, :])
    log_gap = cumulative[:, :, None] - cumulative[:, None, :]
    weight_matrix = jnp.where(causal_same[None], jnp.exp(jnp.where(causal_same[None], log_gap, 0.0)), 0.0)
    attention_scores = jnp.einsum('keu,reu->ekr', query_slice, key_slice, precision=maximum_precision) * weight_matrix
    within = jnp.einsum('hnm,mhe->nhe', attention_scores, value_slice, precision=maximum_precision)
    before = (started == 0).astype(jnp.float32)
    reach_in = jnp.exp(cumulative) * before[None, :]
    across = jnp.einsum('nhd,hde->nhe', query_slice * reach_in.T[:, :, None], carried, precision=maximum_precision)
    last_count = started[-1]
    trailing_weight = jnp.exp(cumulative[:, -1:] - cumulative) * (started == last_count).astype(jnp.float32)[None, :]
    keep_factor = jnp.exp(cumulative[:, -1]) * (last_count == 0).astype(jnp.float32)
    zeroed_state = jnp.einsum('ygc,ygs->gcs', key_slice * trailing_weight.T[:, :, None], value_slice, precision=maximum_precision)
    return (keep_factor[:, None, None] * carried + zeroed_state, within + across)

def retain(queries, key_heads, value_heads, log_rates, start_flag, initial):
    block_count = queries.shape[0] // BLK
    head_count = queries.shape[1]
    query_blocks = queries.reshape(block_count, BLK, head_count, queries.shape[2])
    key_blocks = key_heads.reshape(block_count, BLK, head_count, key_heads.shape[2])
    value_blocks = value_heads.reshape(block_count, BLK, head_count, value_heads.shape[2])
    rate_blocks = log_rates.reshape(head_count, block_count, BLK).transpose(1, 0, 2)
    flag_blocks = start_flag.reshape(block_count, BLK)

    def scan_step(carried, block_items):
        return retain_block(carried, *block_items)
    final_state, block_outputs = lax.scan(jax.checkpoint(scan_step), initial, (query_blocks, key_blocks, value_blocks, rate_blocks, flag_blocks))
    return (block_outputs.reshape(block_count * BLK, head_count, value_heads.shape[2]), final_state)

def reference(tokens, first_gain, query_weight, key_weight, value_weight, gate_weight, output_weight, second_gain, gelu_weight, linear_weight, down_weight, log_decay, first_start, cotangent):
    position = jnp.arange(TOTAL_TOKENS).astype(jnp.int32)
    shard_of = (position // TOK_DEV).astype(jnp.int32)
    start_flag = (position - shard_of * TOK_DEV == first_start[shard_of]).astype(jnp.float32)
    log_rates = log_decay.astype(jnp.float32)
    key_scale = 1.0 / math.sqrt(DK)

    def forward(inputs, gain_one, weight_query, weight_key, weight_value, weight_gate, weight_output, gain_two, weight_gelu, weight_linear, weight_down):
        normed_in = low(layer_norm(inputs, gain_one))
        queries = low_back(matmul(normed_in, weight_query))
        key_rows = low_back(matmul(normed_in, weight_key)) * key_scale
        value_rows = low_back(matmul(normed_in, weight_value))
        gate_pre = low_back(matmul(normed_in, weight_gate))
        initial = jnp.zeros((RETENTION_HEADS, DK, DV), jnp.float32)
        retained, final_state = retain(queries.reshape(TOTAL_TOKENS, RETENTION_HEADS, DK), key_rows.reshape(TOTAL_TOKENS, RETENTION_HEADS, DK), value_rows.reshape(TOTAL_TOKENS, RETENTION_HEADS, DV), log_rates, start_flag, initial)
        normed = group_norm(retained).reshape(TOTAL_TOKENS, VW)
        gated_rows = low(jax.nn.silu(gate_pre) * normed)
        residual = inputs + low_back(matmul(gated_rows, weight_output))
        normed_mid = low(layer_norm(residual, gain_two))
        up_gate = low_back(matmul(normed_mid, weight_gelu))
        up_proj = low_back(matmul(normed_mid, weight_linear))
        hidden = low(jax.nn.gelu(up_gate, approximate=False) * up_proj)
        return residual + low_back(matmul(hidden, weight_down))
    primals = tuple((item.astype(jnp.float32) for item in (tokens, first_gain, query_weight, key_weight, value_weight, gate_weight, output_weight, second_gain, gelu_weight, linear_weight, down_weight)))
    result, pullback = jax.vjp(forward, *primals)
    grads = pullback(cotangent.astype(jnp.float32))
    return (result.astype(jnp.bfloat16), grads[0].astype(jnp.bfloat16), grads[1], grads[2], grads[3], grads[4], grads[5], grads[6], grads[7], grads[8], grads[9], grads[10])
```

```python
import math

import jax
import jax.numpy as jnp
from jax import lax
from jax.experimental import pallas as pl
from jax.experimental.pallas import tpu as pltpu
from jax.sharding import PartitionSpec as P


DK = 256
DV = 512
BLK = 256


maximum_precision = lax.Precision.HIGHEST
eps_norm = 1e-05


def carried_in(part, axis, combine, identity, reverse):
    count = lax.axis_size(axis)
    place = lax.axis_index(axis)
    ahead = count - 1 - place if reverse else place
    gathered = jax.tree.map(lambda a: lax.all_gather(a, axis), part)
    state = jax.tree.map(lambda a, e: jnp.zeros_like(a) + jnp.asarray(e, a.dtype), part, identity)

    def one(hop, state):
        source = count - 1 - hop if reverse else hop
        return combine(
            state, jax.tree.map(lambda a: lax.dynamic_index_in_dim(a, source, 0, False), gathered)
        )

    return lax.fori_loop(0, ahead, one, state)


def matmul(left_side, right_side):
    return jnp.dot(left_side, right_side, preferred_element_type=jnp.float32)


def transpose_left(left_side, right_side):
    return lax.dot_general(
        left_side, right_side, (((0,), (0,)), ((), ())), preferred_element_type=jnp.float32
    )


def transpose_right(left_side, right_side):
    return lax.dot_general(
        left_side, right_side, (((1,), (1,)), ((), ())), preferred_element_type=jnp.float32
    )


def layer_norm(activity, gain_row):
    centre = jnp.mean(activity, axis=-1, keepdims=True)
    centred = activity - centre
    spread = jnp.mean(centred * centred, axis=-1, keepdims=True)
    return centred * lax.rsqrt(spread + eps_norm) * gain_row


def group_norm(activity):
    centre = jnp.mean(activity, axis=-1, keepdims=True)
    centred = activity - centre
    spread = jnp.mean(centred * centred, axis=-1, keepdims=True)
    return centred * lax.rsqrt(spread + eps_norm)


def retain_block(carried, query_slice, key_slice, value_slice, rate_part, flag_part):
    cumulative = jnp.cumsum(rate_part, axis=1)
    started = jnp.cumsum(flag_part)
    block_len = flag_part.shape[0]
    position = jnp.arange(block_len)
    causal_same = (started[:, None] == started[None, :]) & (position[:, None] >= position[None, :])
    log_gap = cumulative[:, :, None] - cumulative[:, None, :]
    weight_matrix = jnp.where(
        causal_same[None], jnp.exp(jnp.where(causal_same[None], log_gap, 0.0)), 0.0
    )
    attention_scores = (
        jnp.einsum("keu,reu->ekr", query_slice, key_slice, precision=maximum_precision)
        * weight_matrix
    )
    within = jnp.einsum("hnm,mhe->nhe", attention_scores, value_slice, precision=maximum_precision)
    before = (started == 0).astype(jnp.float32)
    reach_in = jnp.exp(cumulative) * before[None, :]
    across = jnp.einsum(
        "nhd,hde->nhe", query_slice * reach_in.T[:, :, None], carried, precision=maximum_precision
    )
    last_count = started[-1]
    trailing_weight = (
        jnp.exp(cumulative[:, -1:] - cumulative)
        * (started == last_count).astype(jnp.float32)[None, :]
    )
    keep_factor = jnp.exp(cumulative[:, -1]) * (last_count == 0).astype(jnp.float32)
    zeroed_state = jnp.einsum(
        "ygc,ygs->gcs",
        key_slice * trailing_weight.T[:, :, None],
        value_slice,
        precision=maximum_precision,
    )
    return (keep_factor[:, None, None] * carried + zeroed_state, within + across)


def retain(queries, key_heads, value_heads, log_rates, start_flag, initial):
    block_count = queries.shape[0] // BLK
    head_count = queries.shape[1]
    query_blocks = queries.reshape(block_count, BLK, head_count, queries.shape[2])
    key_blocks = key_heads.reshape(block_count, BLK, head_count, key_heads.shape[2])
    value_blocks = value_heads.reshape(block_count, BLK, head_count, value_heads.shape[2])
    rate_blocks = log_rates.reshape(head_count, block_count, BLK).transpose(1, 0, 2)
    flag_blocks = start_flag.reshape(block_count, BLK)

    def scan_step(carried, block_items):
        return retain_block(carried, *block_items)

    final_state, block_outputs = lax.scan(
        jax.checkpoint(scan_step),
        initial,
        (query_blocks, key_blocks, value_blocks, rate_blocks, flag_blocks),
    )
    return (block_outputs.reshape(block_count * BLK, head_count, value_heads.shape[2]), final_state)


def link_maps(earlier, later):
    return (earlier[0] * later[0], later[0][:, None, None] * earlier[1] + later[1])


def local_scatter(
    tokens,
    first_gain,
    query_weight,
    key_weight,
    value_weight,
    gate_weight,
    output_weight,
    second_gain,
    gelu_weight,
    linear_weight,
    down_weight,
    log_decay,
    first_start,
    cotangent,
):
    token_rows = tokens.shape[0]
    head_count = query_weight.shape[1] // DK
    key_scale = 1.0 / math.sqrt(DK)
    position = jnp.arange(token_rows, dtype=jnp.int32)
    start_flag = (position == first_start[0]).astype(jnp.float32)
    before = (position < first_start[0]).astype(jnp.float32)
    reach_in = jnp.exp(jnp.cumsum(log_decay, axis=1)) * before[None, :]
    shard_keep = jnp.exp(jnp.sum(log_decay, axis=1)) * (first_start[0] == token_rows).astype(
        jnp.float32
    )
    empty_state = jnp.zeros((head_count, DK, DV), jnp.float32)
    inputs = tokens.astype(jnp.float32)
    normed_in = layer_norm(inputs, first_gain).astype(jnp.bfloat16)
    queries = matmul(normed_in, query_weight)
    scaled_keys = matmul(normed_in, key_weight) * key_scale
    values = matmul(normed_in, value_weight)
    gate_pre = matmul(normed_in, gate_weight)
    query_heads = queries.reshape(token_rows, head_count, DK)
    key_heads = scaled_keys.reshape(token_rows, head_count, DK)
    value_heads = values.reshape(token_rows, head_count, DV)
    local_out, local_end = retain(
        query_heads, key_heads, value_heads, log_decay, start_flag, empty_state
    )
    weighted_query = query_heads * reach_in.T[:, :, None]
    incoming = carried_in(
        (shard_keep, local_end), "seq", link_maps, (jnp.ones_like(shard_keep), empty_state), False
    )[1]
    retained = local_out + jnp.einsum(
        "nhd,hde->nhe", weighted_query, incoming, precision=maximum_precision
    )

    def gate_mix(gate_in, retained_in):
        return jax.nn.silu(gate_in) * group_norm(retained_in).reshape(token_rows, head_count * DV)

    gated_rows = gate_mix(gate_pre, retained).astype(jnp.bfloat16)
    residual = inputs + lax.psum(matmul(gated_rows, output_weight), "head")
    normed_mid = layer_norm(residual, second_gain).astype(jnp.bfloat16)
    up_gate = matmul(normed_mid, gelu_weight)
    up_proj = matmul(normed_mid, linear_weight)

    def hidden_mix(pre_gate, up_branch):
        return jax.nn.gelu(pre_gate, approximate=False) * up_branch

    hidden = hidden_mix(up_gate, up_proj).astype(jnp.bfloat16)
    result = residual + lax.psum(matmul(hidden, down_weight), "head")
    output_rows = result.astype(jnp.bfloat16)
    grad_hidden = transpose_right(cotangent, down_weight)
    wgrad_down = transpose_left(hidden, cotangent)
    _, hidden_back = jax.vjp(hidden_mix, up_gate, up_proj)
    grad_up_gate, grad_up = hidden_back(grad_hidden)
    grad_up_gate = grad_up_gate.astype(jnp.bfloat16)
    grad_up = grad_up.astype(jnp.bfloat16)
    grad_mid_in = lax.psum(
        transpose_right(grad_up_gate, gelu_weight) + transpose_right(grad_up, linear_weight), "head"
    )
    wgrad_gelu = transpose_left(normed_mid, grad_up_gate)
    wgrad_linear = transpose_left(normed_mid, grad_up)
    _, second_back = jax.vjp(layer_norm, residual, second_gain)
    grad_mid_norm, wgrad_second = second_back(grad_mid_in)
    grad_residual = cotangent.astype(jnp.float32) + grad_mid_norm
    grad_branch = grad_residual.astype(jnp.bfloat16)
    grad_gated = transpose_right(grad_branch, output_weight)
    wgrad_output = transpose_left(gated_rows, grad_branch)
    _, gate_back = jax.vjp(gate_mix, gate_pre, retained)
    grad_gate_pre, grad_retained = gate_back(grad_gated)
    grad_gate_pre = grad_gate_pre.astype(jnp.bfloat16)
    local_in = jnp.einsum(
        "nhd,nhe->hde", weighted_query, grad_retained, precision=maximum_precision
    )
    beyond = carried_in(
        (shard_keep, local_in), "seq", link_maps, (jnp.ones_like(shard_keep), empty_state), True
    )[1]

    def local_retain(query_in, key_in, value_in):
        return retain(query_in, key_in, value_in, log_decay, start_flag, incoming)

    _, retain_back = jax.vjp(local_retain, query_heads, key_heads, value_heads)
    grad_q, grad_k, grad_v = retain_back((grad_retained, beyond))
    grad_queries = grad_q.reshape(token_rows, head_count * DK).astype(jnp.bfloat16)
    grad_keys = (grad_k * key_scale).reshape(token_rows, head_count * DK).astype(jnp.bfloat16)
    grad_values = grad_v.reshape(token_rows, head_count * DV).astype(jnp.bfloat16)
    grad_in = lax.psum(
        transpose_right(grad_queries, query_weight)
        + transpose_right(grad_keys, key_weight)
        + transpose_right(grad_values, value_weight)
        + transpose_right(grad_gate_pre, gate_weight),
        "head",
    )
    wgrad_query = transpose_left(normed_in, grad_queries)
    wgrad_key = transpose_left(normed_in, grad_keys)
    wgrad_value = transpose_left(normed_in, grad_values)
    wgrad_gate = transpose_left(normed_in, grad_gate_pre)
    _, first_back = jax.vjp(layer_norm, inputs, first_gain)
    grad_in_norm, wgrad_first = first_back(grad_in)
    grad_tokens = (grad_residual + grad_in_norm).astype(jnp.bfloat16)
    summed = tuple(
        (
            lax.psum_scatter(wgrad_first, "seq", scatter_dimension=0, tiled=True),
            lax.psum_scatter(wgrad_query, "seq", scatter_dimension=0, tiled=True),
            lax.psum_scatter(wgrad_key, "seq", scatter_dimension=0, tiled=True),
            lax.psum_scatter(wgrad_value, "seq", scatter_dimension=0, tiled=True),
            lax.psum_scatter(wgrad_gate, "seq", scatter_dimension=0, tiled=True),
            lax.psum_scatter(wgrad_output, "seq", scatter_dimension=1, tiled=True),
            lax.psum_scatter(wgrad_second, "seq", scatter_dimension=0, tiled=True),
            lax.psum_scatter(wgrad_gelu, "seq", scatter_dimension=0, tiled=True),
            lax.psum_scatter(wgrad_linear, "seq", scatter_dimension=0, tiled=True),
            lax.psum_scatter(wgrad_down, "seq", scatter_dimension=1, tiled=True),
        )
    )
    return (output_rows, grad_tokens) + summed


def exchange_gather(rows, axis):
    count = lax.axis_size(axis)
    place = lax.axis_index(axis)
    bit = 1
    while bit < count:
        other = lax.ppermute(rows, axis, [(i, i ^ bit) for i in range(count)])
        upper = (place & bit) != 0
        rows = jnp.concatenate([jnp.where(upper, other, rows), jnp.where(upper, rows, other)], axis=0)
        bit *= 2
    return rows


def exchange_sum(rows, axis):
    count = lax.axis_size(axis)
    bit = 1
    while bit < count:
        rows = rows + lax.ppermute(rows, axis, [(i, i ^ bit) for i in range(count)])
        bit *= 2
    return rows


def head_scatter(part):
    count = lax.axis_size("head")
    place = lax.axis_index("head")
    width = part.shape[1]
    low = 2 if count % 2 == 0 else 1
    split = part.reshape(count // low, low, part.shape[0] // count, width)
    if low == 2:
        pairs = [(i, i ^ 1) for i in range(count)]
        sent = lax.dynamic_index_in_dim(split, 1 - place % 2, 1, False)
        split = lax.dynamic_index_in_dim(split, place % 2, 1, False) + lax.ppermute(sent, "head", pairs)
    else:
        split = split[:, 0]
    total = lax.dynamic_index_in_dim(split, place // low, 0, False)
    for hop in range(1, count // low):
        ring = [(i, (i + hop * low) % count) for i in range(count)]
        sent = lax.dynamic_index_in_dim(split, (place // low + hop) % (count // low), 0, False)
        total = total + lax.ppermute(sent, "head", ring)
    return total


def place_parts(parts, positions):
    rows = parts[0].shape[0]
    whole = jnp.zeros((rows * len(parts),) + parts[0].shape[1:], parts[0].dtype)
    for item, position in zip(parts, positions):
        whole = lax.dynamic_update_slice_in_dim(whole, item, position * rows, 0)
    return whole


def head_parts(piece):
    count = lax.axis_size("head")
    place = lax.axis_index("head")
    low = 2 if count % 2 == 0 else 1
    parts, places = [piece], [place]
    for hop in range(1, count // low):
        parts.append(lax.ppermute(piece, "head", [(i, (i + hop * low) % count) for i in range(count)]))
        places.append((place - hop * low) % count)
    if low == 2:
        pairs = [(i, i ^ 1) for i in range(count)]
        parts += [lax.ppermute(item, "head", pairs) for item in parts]
        places += [other ^ 1 for other in places]
    return parts, places


def dot_nt(left, right):
    return lax.dot_general(left, right, (((1,), (1,)), ((), ())), preferred_element_type=jnp.float32)


def dot_tn(left, right):
    return lax.dot_general(left, right, (((0,), (0,)), ((), ())), preferred_element_type=jnp.float32)


def dot_nn(left, right):
    return lax.dot_general(left, right, (((1,), (0,)), ((), ())), preferred_element_type=jnp.float32)


def split_dot(left, right, dot):
    left_high, right_high = left.astype(jnp.bfloat16), right.astype(jnp.bfloat16)
    left_low = (left - left_high.astype(jnp.float32)).astype(jnp.bfloat16)
    right_low = (right - right_high.astype(jnp.float32)).astype(jnp.bfloat16)
    return dot(left_high, right_high) + (dot(left_low, right_high) + dot(left_high, right_low))


def half_split_dot(left, right, dot):
    left_high = left.astype(jnp.bfloat16)
    left_low = (left - left_high.astype(jnp.float32)).astype(jnp.bfloat16)
    return dot(left_high, right) + dot(left_low, right)


def block_decay(first, cumulative):
    size = cumulative.shape[1]
    across = jnp.broadcast_to(cumulative, (size, size))
    down = across.T
    row = lax.broadcasted_iota(jnp.int32, (size, size), 0)
    column = lax.broadcasted_iota(jnp.int32, (size, size), 1)
    seen = (row >= column) & ((column >= first) | (row < first))
    weights = jnp.where(seen, jnp.exp(jnp.where(seen, down - across, 0.0)), 0.0)
    per_row = down[:, :1]
    place = lax.broadcasted_iota(jnp.int32, (size, 1), 0)
    last = cumulative[:, size - 1 :]
    whole = first >= size
    reach = jnp.where(place < first, jnp.exp(per_row), 0.0)
    trail = jnp.where((place >= first) | whole, jnp.exp(last - per_row), 0.0)
    keep = jnp.where(whole, jnp.exp(last), 0.0)
    return weights, reach, trail, keep


def norm_parts(retained):
    centre = jnp.mean(retained, axis=-1, keepdims=True)
    centred = retained - centre
    inverse = lax.rsqrt(jnp.mean(centred * centred, axis=-1, keepdims=True) + eps_norm)
    return centred * inverse, inverse


def retain_forward_kernel(first_ref, cum_ref, q_ref, k_ref, v_ref, gate_ref, retained_ref, gated_ref, state_ref, state):
    block = pl.program_id(1)

    @pl.when(block == 0)
    def _():
        state[...] = jnp.zeros_like(state)

    weights, reach, trail, keep = block_decay(first_ref[block], cum_ref[0, 0])
    q, k, v = q_ref[...], k_ref[...], v_ref[...]
    held = state[...].astype(jnp.bfloat16)
    state_ref[0, 0] = held
    scores = (split_dot(q, k, dot_nt) * weights).astype(jnp.bfloat16)
    retained = dot_nn(scores, v) + reach * dot_nn(q.astype(jnp.bfloat16), held)
    state[...] = keep * state[...] + dot_tn((k * trail).astype(jnp.bfloat16), v)
    retained_ref[...] = retained
    normed, _ = norm_parts(retained)
    gate = gate_ref[...]
    gated_ref[...] = (gate * jax.nn.sigmoid(gate) * normed).astype(jnp.bfloat16)


def retain_backward_kernel(
    first_ref, cum_ref, q_ref, k_ref, v_ref, gate_ref, retained_ref, state_ref, up_ref,
    dq_ref, dk_ref, dv_ref, dgate_ref, beyond,
):
    block = pl.num_programs(1) - 1 - pl.program_id(1)

    @pl.when(pl.program_id(1) == 0)
    def _():
        beyond[...] = jnp.zeros_like(beyond)

    weights, reach, trail, keep = block_decay(first_ref[block], cum_ref[0, 0])
    q, k, v = q_ref[...], k_ref[...], v_ref[...]
    gate, up = gate_ref[...], up_ref[...]
    normed, inverse = norm_parts(retained_ref[...])
    sig = jax.nn.sigmoid(gate)
    silu = gate * sig
    dgate_ref[...] = (up * normed * (sig + silu * (1.0 - sig))).astype(jnp.bfloat16)
    g = up * silu
    mean_g = jnp.mean(g, axis=-1, keepdims=True)
    mean_gn = jnp.mean(g * normed, axis=-1, keepdims=True)
    grad = (g - mean_g - normed * mean_gn) * inverse
    after = beyond[...].astype(jnp.bfloat16)
    scores = (split_dot(q, k, dot_nt) * weights).astype(jnp.bfloat16)
    dscores = (half_split_dot(grad, v, dot_nt) * weights).astype(jnp.bfloat16)
    grad = grad.astype(jnp.bfloat16)
    q_reach = (q * reach).astype(jnp.bfloat16)
    q, k = q.astype(jnp.bfloat16), k.astype(jnp.bfloat16)
    dq_ref[...] = (dot_nn(dscores, k) + reach * dot_nt(grad, state_ref[0, 0])).astype(jnp.bfloat16)
    dk = dot_tn(dscores, q) + trail * dot_nt(v, after)
    dk_ref[...] = (dk * (1.0 / math.sqrt(DK))).astype(jnp.bfloat16)
    dv_ref[...] = (dot_tn(scores, grad) + trail * dot_nn(k, after)).astype(jnp.bfloat16)
    beyond[...] = keep * beyond[...] + dot_tn(q_reach, grad)


def retain_specs(blocks, reverse):
    at = (lambda b: blocks - 1 - b) if reverse else (lambda b: b)
    cum = pl.BlockSpec((1, 1, 1, BLK), lambda h, b, *_: (h, at(b), 0, 0))
    key = pl.BlockSpec((BLK, DK), lambda h, b, *_: (at(b), h))
    val = pl.BlockSpec((BLK, DV), lambda h, b, *_: (at(b), h))
    state = pl.BlockSpec((1, 1, DK, DV), lambda h, b, *_: (h, at(b), 0, 0))
    return cum, key, val, state


def retain_forward(first, cumulative, q, k, v, gate):
    heads, blocks = cumulative.shape[:2]
    rows = q.shape[0]
    cum, key, val, state = retain_specs(blocks, False)
    return pl.pallas_call(
        retain_forward_kernel,
        grid_spec=pltpu.PrefetchScalarGridSpec(
            num_scalar_prefetch=1,
            grid=(heads, blocks),
            in_specs=[cum, key, key, val, val],
            out_specs=[val, val, state],
            scratch_shapes=[pltpu.VMEM((DK, DV), jnp.float32)],
        ),
        out_shape=[
            jax.ShapeDtypeStruct((rows, heads * DV), jnp.float32),
            jax.ShapeDtypeStruct((rows, heads * DV), jnp.bfloat16),
            jax.ShapeDtypeStruct((heads, blocks, DK, DV), jnp.bfloat16),
        ],
        cost_estimate=pl.CostEstimate(
            flops=2 * heads * rows * (BLK * (DK + DV) + 2 * DK * DV),
            bytes_accessed=rows * heads * (4 * DK + 12 * DV),
            transcendentals=rows * heads * (BLK + DV),
        ),
        name="retain_forward",
    )(first, cumulative, q, k, v, gate)


def retain_backward(first, cumulative, q, k, v, gate, retained, states, up):
    heads, blocks = cumulative.shape[:2]
    rows = q.shape[0]
    cum, key, val, state = retain_specs(blocks, True)
    return pl.pallas_call(
        retain_backward_kernel,
        grid_spec=pltpu.PrefetchScalarGridSpec(
            num_scalar_prefetch=1,
            grid=(heads, blocks),
            in_specs=[cum, key, key, val, val, val, state, val],
            out_specs=[key, key, val, val],
            scratch_shapes=[pltpu.VMEM((DK, DV), jnp.float32)],
        ),
        out_shape=[
            jax.ShapeDtypeStruct((rows, heads * DK), jnp.bfloat16),
            jax.ShapeDtypeStruct((rows, heads * DK), jnp.bfloat16),
            jax.ShapeDtypeStruct((rows, heads * DV), jnp.bfloat16),
            jax.ShapeDtypeStruct((rows, heads * DV), jnp.bfloat16),
        ],
        cost_estimate=pl.CostEstimate(
            flops=2 * heads * rows * (BLK * (3 * DK + 2 * DV) + 4 * DK * DV),
            bytes_accessed=rows * heads * (8 * DK + 20 * DV),
            transcendentals=rows * heads * (BLK + DV),
        ),
        name="retain_backward",
    )(first, cumulative, q, k, v, gate, retained, states, up)


def norm_grad(grad, gain, centred_unit, inverse):
    e = grad * gain
    mean_e = jnp.mean(e, axis=-1, keepdims=True)
    mean_en = jnp.mean(e * centred_unit, axis=-1, keepdims=True)
    return (e - mean_e - centred_unit * mean_en) * inverse


def local_gather(
    tokens,
    first_gain,
    query_weight,
    key_weight,
    value_weight,
    gate_weight,
    output_weight,
    second_gain,
    gelu_weight,
    linear_weight,
    down_weight,
    log_decay,
    first_start,
    cotangent,
):
    bf16, f32 = jnp.bfloat16, jnp.float32
    shards, groups = lax.axis_size("seq"), lax.axis_size("head")
    shard, group = lax.axis_index("seq"), lax.axis_index("head")
    rows, width = tokens.shape
    heads = query_weight.shape[1] // DK
    part = rows // groups
    slab = width // shards
    key_scale = 1.0 / math.sqrt(DK)

    def piece_of(a):
        return lax.dynamic_slice_in_dim(a, group * part, part, 0)

    def own_rows(a):
        return lax.dynamic_slice_in_dim(a, shard * rows, rows, 0)

    def own_slab(a):
        return lax.dynamic_slice_in_dim(a, shard * slab, slab, 1)

    def gather(piece, axes):
        return (2.0 * lax.all_gather(0.5 * piece, axes, axis=0, tiled=True)).astype(bf16)

    def gather_all(piece):
        return gather(piece, ("seq", "head"))

    small = jnp.concatenate(
        [log_decay, jnp.broadcast_to(first_start.astype(f32)[:, None], (1, rows))], axis=0
    )
    small = exchange_gather(small[None], "seq")
    cumulative = jnp.cumsum(small[:, :heads].transpose(1, 0, 2), axis=2)[:, :, None, :]
    first = small[:, heads, 0].astype(jnp.int32)

    def widen(a):
        return 0.5 * a.astype(f32)

    def narrow(a):
        return (2.0 * a).astype(bf16)

    def head_gather(piece):
        return place_parts(*head_parts(piece))

    def pair_group(piece):
        parts = []
        for hop in range(2, shards, 2):
            moved = lax.ppermute(piece, "seq", [(i, (i + hop) % shards) for i in range(shards)])
            parts += head_parts(moved)[0]
        return narrow(jnp.concatenate(parts, axis=0))

    def pair_sum(product):
        sent = product(lax.bitwise_xor(shard, 1))
        return product(shard) + lax.ppermute(sent, "seq", [(i, i ^ 1) for i in range(shards)])

    token_piece = piece_of(tokens).astype(f32)
    first_unit, first_inverse = norm_parts(token_piece)
    normed_in = gather_all((first_unit * first_gain).astype(bf16).astype(f32))
    cotangent_piece = piece_of(cotangent).astype(f32)
    cotangent_far = pair_group(0.5 * cotangent_piece)

    queries = matmul(normed_in, query_weight)
    keys = matmul(normed_in, key_weight) * key_scale
    values = matmul(normed_in, value_weight).astype(bf16)
    gate_pre = matmul(normed_in, gate_weight)
    retained, gated, states = retain_forward(first, cumulative, queries, keys, values, gate_pre)

    residual = token_piece + head_scatter(matmul(own_rows(gated), output_weight))
    mid_unit, mid_inverse = norm_parts(residual)
    normed_mid_piece = widen((mid_unit * second_gain).astype(bf16))
    normed_mid_own = narrow(head_gather(normed_mid_piece))
    normed_mid_far = pair_group(normed_mid_piece)

    def hidden_mix(pre_gate, up_branch):
        return jax.nn.gelu(pre_gate, approximate=False) * up_branch

    def feed_forward(normed, above):
        up_gate = matmul(normed, gelu_weight)
        up_proj = matmul(normed, linear_weight)
        hidden, back = jax.vjp(hidden_mix, up_gate, up_proj)
        grad_up_gate, grad_up = back(transpose_right(above, down_weight))
        return hidden.astype(bf16), grad_up_gate.astype(bf16), grad_up.astype(bf16)

    hidden, grad_up_gate, grad_up = feed_forward(normed_mid_own, cotangent)
    grad_mid = head_scatter(transpose_right(grad_up_gate, gelu_weight) + transpose_right(grad_up, linear_weight))
    grad_residual = cotangent_piece + norm_grad(grad_mid, second_gain, mid_unit, mid_inverse)
    second_part = jnp.sum(grad_mid * mid_unit, axis=0)
    grad_branch = gather_all(grad_residual.astype(bf16).astype(f32))

    result = residual + head_scatter(matmul(hidden, down_weight))
    output_rows = narrow(head_gather(0.5 * result))

    hidden_far, grad_up_gate_far, grad_up_far = feed_forward(normed_mid_far, cotangent_far)

    def slab_of(a, place):
        return lax.dynamic_slice_in_dim(a, place * slab, slab, 1)

    wgrad_down = pair_sum(
        lambda place: transpose_left(hidden, slab_of(cotangent, place))
        + transpose_left(hidden_far, slab_of(cotangent_far, place)),
    )
    wgrad_gelu = pair_sum(
        lambda place: transpose_left(slab_of(normed_mid_own, place), grad_up_gate)
        + transpose_left(slab_of(normed_mid_far, place), grad_up_gate_far),
    )
    wgrad_linear = pair_sum(
        lambda place: transpose_left(slab_of(normed_mid_own, place), grad_up)
        + transpose_left(slab_of(normed_mid_far, place), grad_up_far),
    )

    grad_gated = transpose_right(grad_branch, output_weight)
    wgrad_output = transpose_left(gated, own_slab(grad_branch))
    grad_queries, grad_keys, grad_values, grad_gate_pre = retain_backward(
        first, cumulative, queries, keys, values, gate_pre, retained, states, grad_gated
    )
    grad_in = head_scatter(
        transpose_right(own_rows(grad_queries), query_weight)
        + transpose_right(own_rows(grad_keys), key_weight)
        + transpose_right(own_rows(grad_values), value_weight)
        + transpose_right(own_rows(grad_gate_pre), gate_weight)
    )
    in_slab = own_slab(normed_in)
    wgrad_query = transpose_left(in_slab, grad_queries)
    wgrad_key = transpose_left(in_slab, grad_keys)
    wgrad_value = transpose_left(in_slab, grad_values)
    wgrad_gate = transpose_left(in_slab, grad_gate_pre)
    first_part = jnp.sum(grad_in * first_unit, axis=0)
    grad_piece = grad_residual + norm_grad(grad_in, first_gain, first_unit, first_inverse)
    grad_tokens = narrow(head_gather(0.5 * grad_piece))
    gains = exchange_sum(exchange_sum(jnp.stack([first_part, second_part]), "head"), "seq")
    gains = own_slab(gains)
    return (
        output_rows,
        grad_tokens,
        gains[0],
        wgrad_query,
        wgrad_key,
        wgrad_value,
        wgrad_gate,
        wgrad_output,
        gains[1],
        wgrad_gelu,
        wgrad_linear,
        wgrad_down,
    )


def local(*arrays):
    tokens = lax.axis_size("seq") * arrays[0].shape[0]
    columns = sum(w.shape[1] for w in (*arrays[2:6], *arrays[8:10])) + arrays[6].shape[0] + arrays[10].shape[0]
    if 4 * tokens <= lax.axis_size("head") * columns:
        return local_gather(*arrays)
    return local_scatter(*arrays)


def solution(mesh):
    return jax.shard_map(
        local,
        mesh=mesh,
        in_specs=(
            P("seq", None),
            P(),
            P(None, "head"),
            P(None, "head"),
            P(None, "head"),
            P(None, "head"),
            P("head", None),
            P(),
            P(None, "head"),
            P(None, "head"),
            P("head", None),
            P("head", "seq"),
            P("seq"),
            P("seq", None),
        ),
        out_specs=(
            P("seq", None),
            P("seq", None),
            P("seq"),
            P("seq", "head"),
            P("seq", "head"),
            P("seq", "head"),
            P("seq", "head"),
            P("head", "seq"),
            P("seq"),
            P("seq", "head"),
            P("seq", "head"),
            P("head", "seq"),
        ),
        check_vma=False,
    )
```

```python
import functools
import math

import jax
import jax.numpy as jnp
from jax import lax
from jax.experimental import pallas as pl
from jax.experimental.pallas import tpu as pltpu
from jax.sharding import PartitionSpec as P


SEQ = "seq"
HEAD = "head"
DK = 256
DV = 512
BLK = 256


maximum_precision = lax.Precision.HIGHEST
eps_norm = 1e-05


def carried_in(part, axis, combine, identity, reverse):
    count = lax.axis_size(axis)
    place = lax.axis_index(axis)
    ahead = count - 1 - place if reverse else place
    gathered = jax.tree.map(lambda a: lax.all_gather(a, axis), part)
    state = jax.tree.map(lambda a, e: jnp.zeros_like(a) + jnp.asarray(e, a.dtype), part, identity)

    def one(hop, state):
        source = count - 1 - hop if reverse else hop
        return combine(
            state, jax.tree.map(lambda a: lax.dynamic_index_in_dim(a, source, 0, False), gathered)
        )

    return lax.fori_loop(0, ahead, one, state)


def matmul(left_side, right_side):
    return jnp.dot(left_side, right_side, preferred_element_type=jnp.float32)


def transpose_left(left_side, right_side):
    return lax.dot_general(
        left_side, right_side, (((0,), (0,)), ((), ())), preferred_element_type=jnp.float32
    )


def transpose_right(left_side, right_side):
    return lax.dot_general(
        left_side, right_side, (((1,), (1,)), ((), ())), preferred_element_type=jnp.float32
    )


def layer_norm(activity, gain_row):
    centre = jnp.mean(activity, axis=-1, keepdims=True)
    centred = activity - centre
    spread = jnp.mean(centred * centred, axis=-1, keepdims=True)
    return centred * lax.rsqrt(spread + eps_norm) * gain_row


def group_norm(activity):
    centre = jnp.mean(activity, axis=-1, keepdims=True)
    centred = activity - centre
    spread = jnp.mean(centred * centred, axis=-1, keepdims=True)
    return centred * lax.rsqrt(spread + eps_norm)


def retain_block(carried, query_slice, key_slice, value_slice, rate_part, flag_part):
    cumulative = jnp.cumsum(rate_part, axis=1)
    started = jnp.cumsum(flag_part)
    block_len = flag_part.shape[0]
    position = jnp.arange(block_len)
    causal_same = (started[:, None] == started[None, :]) & (position[:, None] >= position[None, :])
    log_gap = cumulative[:, :, None] - cumulative[:, None, :]
    weight_matrix = jnp.where(
        causal_same[None], jnp.exp(jnp.where(causal_same[None], log_gap, 0.0)), 0.0
    )
    attention_scores = (
        jnp.einsum("keu,reu->ekr", query_slice, key_slice, precision=maximum_precision)
        * weight_matrix
    )
    within = jnp.einsum("hnm,mhe->nhe", attention_scores, value_slice, precision=maximum_precision)
    before = (started == 0).astype(jnp.float32)
    reach_in = jnp.exp(cumulative) * before[None, :]
    across = jnp.einsum(
        "nhd,hde->nhe", query_slice * reach_in.T[:, :, None], carried, precision=maximum_precision
    )
    last_count = started[-1]
    trailing_weight = (
        jnp.exp(cumulative[:, -1:] - cumulative)
        * (started == last_count).astype(jnp.float32)[None, :]
    )
    keep_factor = jnp.exp(cumulative[:, -1]) * (last_count == 0).astype(jnp.float32)
    zeroed_state = jnp.einsum(
        "ygc,ygs->gcs",
        key_slice * trailing_weight.T[:, :, None],
        value_slice,
        precision=maximum_precision,
    )
    return (keep_factor[:, None, None] * carried + zeroed_state, within + across)


def retain(queries, key_heads, value_heads, log_rates, start_flag, initial):
    block_count = queries.shape[0] // BLK
    head_count = queries.shape[1]
    query_blocks = queries.reshape(block_count, BLK, head_count, queries.shape[2])
    key_blocks = key_heads.reshape(block_count, BLK, head_count, key_heads.shape[2])
    value_blocks = value_heads.reshape(block_count, BLK, head_count, value_heads.shape[2])
    rate_blocks = log_rates.reshape(head_count, block_count, BLK).transpose(1, 0, 2)
    flag_blocks = start_flag.reshape(block_count, BLK)

    def scan_step(carried, block_items):
        return retain_block(carried, *block_items)

    final_state, block_outputs = lax.scan(
        jax.checkpoint(scan_step),
        initial,
        (query_blocks, key_blocks, value_blocks, rate_blocks, flag_blocks),
    )
    return (block_outputs.reshape(block_count * BLK, head_count, value_heads.shape[2]), final_state)


def link_maps(earlier, later):
    return (earlier[0] * later[0], later[0][:, None, None] * earlier[1] + later[1])


def local_scatter(
    tokens,
    first_gain,
    query_weight,
    key_weight,
    value_weight,
    gate_weight,
    output_weight,
    second_gain,
    gelu_weight,
    linear_weight,
    down_weight,
    log_decay,
    first_start,
    cotangent,
):
    token_rows = tokens.shape[0]
    head_count = query_weight.shape[1] // DK
    key_scale = 1.0 / math.sqrt(DK)
    position = jnp.arange(token_rows, dtype=jnp.int32)
    start_flag = (position == first_start[0]).astype(jnp.float32)
    before = (position < first_start[0]).astype(jnp.float32)
    reach_in = jnp.exp(jnp.cumsum(log_decay, axis=1)) * before[None, :]
    shard_keep = jnp.exp(jnp.sum(log_decay, axis=1)) * (first_start[0] == token_rows).astype(
        jnp.float32
    )
    empty_state = jnp.zeros((head_count, DK, DV), jnp.float32)
    inputs = tokens.astype(jnp.float32)
    normed_in = layer_norm(inputs, first_gain).astype(jnp.bfloat16)
    queries = matmul(normed_in, query_weight)
    scaled_keys = matmul(normed_in, key_weight) * key_scale
    values = matmul(normed_in, value_weight)
    gate_pre = matmul(normed_in, gate_weight)
    query_heads = queries.reshape(token_rows, head_count, DK)
    key_heads = scaled_keys.reshape(token_rows, head_count, DK)
    value_heads = values.reshape(token_rows, head_count, DV)
    local_out, local_end = retain(
        query_heads, key_heads, value_heads, log_decay, start_flag, empty_state
    )
    weighted_query = query_heads * reach_in.T[:, :, None]
    incoming = carried_in(
        (shard_keep, local_end), SEQ, link_maps, (jnp.ones_like(shard_keep), empty_state), False
    )[1]
    retained = local_out + jnp.einsum(
        "nhd,hde->nhe", weighted_query, incoming, precision=maximum_precision
    )

    def gate_mix(gate_in, retained_in):
        return jax.nn.silu(gate_in) * group_norm(retained_in).reshape(token_rows, head_count * DV)

    gated_rows = gate_mix(gate_pre, retained).astype(jnp.bfloat16)
    residual = inputs + lax.psum(matmul(gated_rows, output_weight), HEAD)
    normed_mid = layer_norm(residual, second_gain).astype(jnp.bfloat16)
    up_gate = matmul(normed_mid, gelu_weight)
    up_proj = matmul(normed_mid, linear_weight)

    def hidden_mix(pre_gate, up_branch):
        return jax.nn.gelu(pre_gate, approximate=False) * up_branch

    hidden = hidden_mix(up_gate, up_proj).astype(jnp.bfloat16)
    result = residual + lax.psum(matmul(hidden, down_weight), HEAD)
    output_rows = result.astype(jnp.bfloat16)
    grad_hidden = transpose_right(cotangent, down_weight)
    wgrad_down = transpose_left(hidden, cotangent)
    _, hidden_back = jax.vjp(hidden_mix, up_gate, up_proj)
    grad_up_gate, grad_up = hidden_back(grad_hidden)
    grad_up_gate = grad_up_gate.astype(jnp.bfloat16)
    grad_up = grad_up.astype(jnp.bfloat16)
    grad_mid_in = lax.psum(
        transpose_right(grad_up_gate, gelu_weight) + transpose_right(grad_up, linear_weight), HEAD
    )
    wgrad_gelu = transpose_left(normed_mid, grad_up_gate)
    wgrad_linear = transpose_left(normed_mid, grad_up)
    _, second_back = jax.vjp(layer_norm, residual, second_gain)
    grad_mid_norm, wgrad_second = second_back(grad_mid_in)
    grad_residual = cotangent.astype(jnp.float32) + grad_mid_norm
    grad_branch = grad_residual.astype(jnp.bfloat16)
    grad_gated = transpose_right(grad_branch, output_weight)
    wgrad_output = transpose_left(gated_rows, grad_branch)
    _, gate_back = jax.vjp(gate_mix, gate_pre, retained)
    grad_gate_pre, grad_retained = gate_back(grad_gated)
    grad_gate_pre = grad_gate_pre.astype(jnp.bfloat16)
    local_in = jnp.einsum(
        "nhd,nhe->hde", weighted_query, grad_retained, precision=maximum_precision
    )
    beyond = carried_in(
        (shard_keep, local_in), SEQ, link_maps, (jnp.ones_like(shard_keep), empty_state), True
    )[1]

    def local_retain(query_in, key_in, value_in):
        return retain(query_in, key_in, value_in, log_decay, start_flag, incoming)

    _, retain_back = jax.vjp(local_retain, query_heads, key_heads, value_heads)
    grad_q, grad_k, grad_v = retain_back((grad_retained, beyond))
    grad_queries = grad_q.reshape(token_rows, head_count * DK).astype(jnp.bfloat16)
    grad_keys = (grad_k * key_scale).reshape(token_rows, head_count * DK).astype(jnp.bfloat16)
    grad_values = grad_v.reshape(token_rows, head_count * DV).astype(jnp.bfloat16)
    grad_in = lax.psum(
        transpose_right(grad_queries, query_weight)
        + transpose_right(grad_keys, key_weight)
        + transpose_right(grad_values, value_weight)
        + transpose_right(grad_gate_pre, gate_weight),
        HEAD,
    )
    wgrad_query = transpose_left(normed_in, grad_queries)
    wgrad_key = transpose_left(normed_in, grad_keys)
    wgrad_value = transpose_left(normed_in, grad_values)
    wgrad_gate = transpose_left(normed_in, grad_gate_pre)
    _, first_back = jax.vjp(layer_norm, inputs, first_gain)
    grad_in_norm, wgrad_first = first_back(grad_in)
    grad_tokens = (grad_residual + grad_in_norm).astype(jnp.bfloat16)
    summed = tuple(
        (
            lax.psum_scatter(wgrad_first, SEQ, scatter_dimension=0, tiled=True),
            lax.psum_scatter(wgrad_query, SEQ, scatter_dimension=0, tiled=True),
            lax.psum_scatter(wgrad_key, SEQ, scatter_dimension=0, tiled=True),
            lax.psum_scatter(wgrad_value, SEQ, scatter_dimension=0, tiled=True),
            lax.psum_scatter(wgrad_gate, SEQ, scatter_dimension=0, tiled=True),
            lax.psum_scatter(wgrad_output, SEQ, scatter_dimension=1, tiled=True),
            lax.psum_scatter(wgrad_second, SEQ, scatter_dimension=0, tiled=True),
            lax.psum_scatter(wgrad_gelu, SEQ, scatter_dimension=0, tiled=True),
            lax.psum_scatter(wgrad_linear, SEQ, scatter_dimension=0, tiled=True),
            lax.psum_scatter(wgrad_down, SEQ, scatter_dimension=1, tiled=True),
        )
    )
    return (output_rows, grad_tokens) + summed


def exchange_sum(rows, axis):
    count = lax.axis_size(axis)
    bit = count // 2
    while bit:
        rows = rows + lax.ppermute(rows, axis, [(i, i ^ bit) for i in range(count)])
        bit //= 2
    return rows


CHIP = [(0, 1), (1, 0), (2, 3), (3, 2)]
ACROSS = [(0, 2), (2, 0), (1, 3), (3, 1)]


def of_rows(a, start, size):
    return lax.dynamic_slice_in_dim(a, start, size, 0)


def after(a, *others):
    return lax.optimization_barrier((a, *others))[0]


def head_total(mine, other):
    other = lax.ppermute(other, HEAD, CHIP)
    both = mine + other
    return both + lax.ppermute(both, HEAD, ACROSS)


def other_core(a):
    return lax.ppermute(a, HEAD, CHIP)


def ring_order(count):
    return list(range(0, count, 2)) + list(range(count - 1, 0, -2))


def ring_gather(half, split):
    count = lax.axis_size(SEQ)
    order = ring_order(count)
    up = [(order[i], order[(i + 1) % count]) for i in range(count)]
    down = [(target, source) for source, target in up]
    steps = []
    rising = falling = half
    for hop in range(1, count // 2 + 1):
        if hop == count // 2:
            rising, falling = rising[:split], falling[split:]
        rising, falling = lax.ppermute(rising, SEQ, up), lax.ppermute(falling, SEQ, down)
        others = other_core(rising), other_core(falling)
        if hop == count // 2:
            steps.append([rising, falling, *others])
        else:
            steps.append([rising, others[0], falling, others[1]])
    return steps


def ring_slots():
    count = lax.axis_size(SEQ)
    index = jnp.arange(count, dtype=jnp.int32)

    def position(shard):
        return jnp.where(shard % 2 == 0, shard // 2, count - 1 - shard // 2)

    behind = (position(lax.axis_index(SEQ).astype(jnp.int32)) - position(index)) % count
    steps = jnp.where(behind < count // 2, 2 * behind - 2, 2 * (count - behind) - 1)
    return jnp.where(behind == 0, count - 2, jnp.where(behind == count // 2, count - 1, steps))


def dot_nt(left, right):
    return lax.dot_general(left, right, (((1,), (1,)), ((), ())), preferred_element_type=jnp.float32)


def dot_tn(left, right):
    return lax.dot_general(left, right, (((0,), (0,)), ((), ())), preferred_element_type=jnp.float32)


def dot_nn(left, right):
    return lax.dot_general(left, right, (((1,), (0,)), ((), ())), preferred_element_type=jnp.float32)


def split_dot(left, right, dot):
    left_high, right_high = left.astype(jnp.bfloat16), right.astype(jnp.bfloat16)
    left_low = (left - left_high.astype(jnp.float32)).astype(jnp.bfloat16)
    right_low = (right - right_high.astype(jnp.float32)).astype(jnp.bfloat16)
    return dot(left_high, right_high) + (dot(left_low, right_high) + dot(left_high, right_low))


def half_split_dot(left, right, dot):
    left_high = left.astype(jnp.bfloat16)
    left_low = (left - left_high.astype(jnp.float32)).astype(jnp.bfloat16)
    return dot(left_high, right) + dot(left_low, right)


def norm_parts(retained):
    centre = jnp.mean(retained, axis=-1, keepdims=True)
    centred = retained - centre
    inverse = lax.rsqrt(jnp.mean(centred * centred, axis=-1, keepdims=True) + eps_norm)
    return centred * inverse, inverse


def norm_start_kernel(core_ref, first_ref, tokens_ref, gain_ref, rates_ref, normed_ref, half_ref):
    half = tokens_ref.shape[0] // 2
    for index, core in enumerate((core_ref[0], 1 - core_ref[0])):
        rows = tokens_ref[pl.ds(pl.multiple_of(core * half, half), half), :].astype(jnp.float32)
        normed = (norm_parts(rows)[0] * gain_ref[...]).astype(jnp.bfloat16)
        normed_ref[index * half : (index + 1) * half, :] = normed
        if index == 0:
            half_ref[:half, :] = normed.astype(jnp.float32)
    heads, size = rates_ref.shape
    half_ref[half:, :] = jnp.full((8, half_ref.shape[1]), first_ref[0], jnp.int32).astype(jnp.float32)
    for head in range(heads):
        half_ref[half : half + 1, head * size : (head + 1) * size] = rates_ref[head : head + 1, :]


def norm_start(core, first_start, tokens, gain, log_decay):
    rows, width = tokens.shape
    vmem, smem = pl.BlockSpec(memory_space=pltpu.VMEM), pl.BlockSpec(memory_space=pltpu.SMEM)
    return pl.pallas_call(
        norm_start_kernel,
        in_specs=[smem, smem, vmem, vmem, vmem],
        out_specs=[vmem, vmem],
        out_shape=[
            jax.ShapeDtypeStruct((rows, width), jnp.bfloat16),
            jax.ShapeDtypeStruct((rows // 2 + 8, width), jnp.float32),
        ],
        name="norm_start",
    )(core[None], first_start, tokens, gain[None], log_decay)


def gain_part_kernel(core_ref, tokens_ref, mine_ref, other_ref, out_ref):
    half = mine_ref.shape[0]
    total = jnp.zeros(out_ref.shape, jnp.float32)
    for grad_ref, core in ((mine_ref, core_ref[0]), (other_ref, 1 - core_ref[0])):
        rows = tokens_ref[pl.ds(pl.multiple_of(core * half, half), half), :].astype(jnp.float32)
        total = total + jnp.sum(grad_ref[...] * norm_parts(rows)[0], axis=0, keepdims=True)
    out_ref[...] = total


def gain_part(core, tokens, mine, other):
    vmem, smem = pl.BlockSpec(memory_space=pltpu.VMEM), pl.BlockSpec(memory_space=pltpu.SMEM)
    return pl.pallas_call(
        gain_part_kernel,
        in_specs=[smem, vmem, vmem, vmem],
        out_specs=vmem,
        out_shape=jax.ShapeDtypeStruct((1, tokens.shape[1]), jnp.float32),
        cost_estimate=pl.CostEstimate(flops=10 * tokens.size, bytes_accessed=6 * tokens.size, transcendentals=0),
        name="gain_part",
    )(core[None], tokens, mine, other)


def rows_product_kernel(parts, weights, tiles, scales, turned, shard_ref, *refs):
    part_refs, slab_refs = refs[:parts], refs[parts : 2 * parts]
    weight_refs = refs[2 * parts : 2 * parts + weights]
    outs = refs[len(refs) - weights - 2 : len(refs) - 1]
    x = refs[-1]
    step = pl.program_id(0)
    size = x.shape[0] // parts

    @pl.when(step == 0)
    def _():
        for index in range(parts):
            at = slice(index * size, (index + 1) * size)
            x[at, :] = part_refs[index][...].astype(jnp.bfloat16)
            outs[0][at, :] = slab_refs[index][...].astype(jnp.bfloat16)

    start = 0
    for weight, out, count, scale in zip(weight_refs, outs[1:], tiles, scales):

        @pl.when((step >= start) & (step < start + count))
        def _(weight=weight, out=out, scale=scale):
            found = (dot_nt if turned else dot_nn)(x[...], weight[...])
            out[...] = (found * scale if scale != 1.0 else found).astype(out.dtype)

        start += count


def rows_product(parts, size, weights, kinds, scales, turned, shard, block, total, buffers=None):
    count, width = len(parts), parts[0].shape[1]
    rows = count * size
    tile = 512
    columns = [w.shape[0] if turned else w.shape[1] for w in weights]
    tiles = [c // tile for c in columns]
    starts = [sum(tiles[:i]) for i in range(len(tiles))]
    slab = width // lax.axis_size(SEQ)

    def at(j, start, number):
        return jnp.clip(j - start, 0, number - 1)

    in_specs = [pl.BlockSpec((size, width), lambda j, s: (0, 0)) for _ in parts]
    in_specs += [pl.BlockSpec((size, slab), lambda j, s: (0, s[0])) for _ in parts]
    for start, number in zip(starts, tiles):
        if turned:
            in_specs.append(pl.BlockSpec((tile, width), lambda j, s, a=start, n=number: (at(j, a, n), 0)))
        else:
            in_specs.append(pl.BlockSpec((width, tile), lambda j, s, a=start, n=number: (0, at(j, a, n))))
    out_specs = [pl.BlockSpec((rows, slab), lambda j, s: (block, 0))]
    for start, number in zip(starts, tiles):
        out_specs.append(pl.BlockSpec((rows, tile), lambda j, s, a=start, n=number: (block, at(j, a, n))))
    out_shape = [jax.ShapeDtypeStruct((total, slab), jnp.bfloat16)]
    out_shape += [jax.ShapeDtypeStruct((total, c), kind) for c, kind in zip(columns, kinds)]
    operands = [*parts, *parts, *weights]
    aliases = {}
    if buffers is not None:
        aliases = {1 + len(operands) + i: i for i in range(len(buffers))}
        in_specs += [pl.BlockSpec(memory_space=pl.ANY)] * len(buffers)
        operands += buffers
    return pl.pallas_call(
        functools.partial(rows_product_kernel, count, len(weights), tiles, scales, turned),
        grid_spec=pltpu.PrefetchScalarGridSpec(
            num_scalar_prefetch=1,
            grid=(sum(tiles),),
            in_specs=in_specs,
            out_specs=out_specs,
            scratch_shapes=[pltpu.VMEM((rows, width), jnp.bfloat16)],
        ),
        out_shape=out_shape,
        input_output_aliases=aliases,
        cost_estimate=pl.CostEstimate(
            flops=2 * rows * width * sum(columns),
            bytes_accessed=4 * rows * width + 2 * width * sum(columns) + 4 * rows * sum(columns),
            transcendentals=0,
        ),
        name="rows_product",
    )(shard[None], *operands)


def round_rows_kernel(*refs):
    out = refs[-1]
    at = 0
    for part in refs[:-1]:
        size = part.shape[0]
        out[at : at + size, :] = (2.0 * part[...]).astype(jnp.bfloat16)
        at += size


def round_rows(parts):
    vmem = pl.BlockSpec(memory_space=pltpu.VMEM)
    rows, width = sum(part.shape[0] for part in parts), parts[0].shape[1]
    return pl.pallas_call(
        round_rows_kernel,
        in_specs=[vmem] * len(parts),
        out_specs=vmem,
        out_shape=jax.ShapeDtypeStruct((rows, width), jnp.bfloat16),
        cost_estimate=pl.CostEstimate(flops=rows * width, bytes_accessed=6 * rows * width, transcendentals=0),
        name="round_rows",
    )(*parts)


def causal(first, places):
    size = places.shape[1]
    column = jnp.broadcast_to(places, (size, size))
    row = column.T
    return (row >= column) & ((column >= first) | (row < first)), row


def block_decay(rates, first, seen, row):
    size = rates.shape[1]
    nth = lax.broadcasted_iota(jnp.int32, (size, size), 1).astype(jnp.float32)
    per_row = jnp.sum(jnp.where(nth <= row, rates, 0.0), axis=1, keepdims=True)
    down = jnp.broadcast_to(per_row, (size, size))
    weights = jnp.exp(jnp.where(seen, down - down.T, -jnp.inf))
    place = row[:, :1]
    last = jnp.sum(rates, axis=1, keepdims=True)
    whole = first >= size
    reach = jnp.where(place < first, jnp.exp(per_row), 0.0)
    trail = jnp.where((place >= first) | whole, jnp.exp(last - per_row), 0.0)
    keep = jnp.where(whole, jnp.exp(last), 0.0)
    return weights, reach, trail, keep


def head_lanes(head):
    return slice(head * DK, (head + 1) * DK), slice(head * DV, (head + 1) * DV), slice(head * BLK, (head + 1) * BLK)


def retain_forward_kernel(
    slot_ref, info_ref, places_ref, q_ref, k_ref, v_ref, gate_ref, retained_ref, gated_ref, state_ref, state
):
    @pl.when(pl.program_id(0) == 0)
    def _():
        state[...] = jnp.zeros_like(state)

    first = info_ref[0, 1:2, :1]
    seen, row = causal(first, places_ref[...])
    for head in range(state.shape[0]):
        key, val, lane = head_lanes(head)
        weights, reach, trail, keep = block_decay(info_ref[0, 0:1, lane], first, seen, row)
        q, k, v = q_ref[:, key], k_ref[:, key], v_ref[:, val]
        held = state[head].astype(jnp.bfloat16)
        state_ref[head, 0] = held
        scores = (split_dot(q, k, dot_nt) * weights).astype(jnp.bfloat16)
        retained = dot_nn(scores, v) + reach * dot_nn(q.astype(jnp.bfloat16), held)
        state[head] = keep * state[head] + dot_tn((k * trail).astype(jnp.bfloat16), v)
        retained_ref[:, val] = retained
        normed, _ = norm_parts(retained)
        gate = gate_ref[:, val]
        gated_ref[:, val] = (gate * jax.nn.sigmoid(gate) * normed).astype(jnp.bfloat16)


def retain_backward_kernel(
    slot_ref, info_ref, places_ref, q_ref, k_ref, v_ref, gate_ref, retained_ref, state_ref, up_ref,
    dq_ref, dk_ref, dv_ref, dgate_ref, beyond,
):
    @pl.when(pl.program_id(0) == 0)
    def _():
        beyond[...] = jnp.zeros_like(beyond)

    first = info_ref[0, 1:2, :1]
    seen, row = causal(first, places_ref[...])
    for head in range(beyond.shape[0]):
        key, val, lane = head_lanes(head)
        weights, reach, trail, keep = block_decay(info_ref[0, 0:1, lane], first, seen, row)
        q, k, v = q_ref[:, key], k_ref[:, key], v_ref[:, val]
        gate, up = gate_ref[:, val], up_ref[:, val]
        normed, inverse = norm_parts(retained_ref[:, val])
        sig = jax.nn.sigmoid(gate)
        silu = gate * sig
        dgate_ref[:, val] = (up * normed * (sig + silu * (1.0 - sig))).astype(jnp.bfloat16)
        g = up * silu
        mean_g = jnp.mean(g, axis=-1, keepdims=True)
        mean_gn = jnp.mean(g * normed, axis=-1, keepdims=True)
        grad = (g - mean_g - normed * mean_gn) * inverse
        after_block = beyond[head].astype(jnp.bfloat16)
        scores = (split_dot(q, k, dot_nt) * weights).astype(jnp.bfloat16)
        dscores = (half_split_dot(grad, v, dot_nt) * weights).astype(jnp.bfloat16)
        grad = grad.astype(jnp.bfloat16)
        q_reach = (q * reach).astype(jnp.bfloat16)
        q, k = q.astype(jnp.bfloat16), k.astype(jnp.bfloat16)
        dq_ref[:, key] = (dot_nn(dscores, k) + reach * dot_nt(grad, state_ref[head, 0])).astype(jnp.bfloat16)
        dk = dot_tn(dscores, q) + trail * dot_nt(v, after_block)
        dk_ref[:, key] = (dk * (1.0 / math.sqrt(DK))).astype(jnp.bfloat16)
        dv_ref[:, val] = (dot_tn(scores, grad) + trail * dot_nn(k, after_block)).astype(jnp.bfloat16)
        beyond[head] = keep * beyond[head] + dot_tn(q_reach, grad)


def retain_specs(heads, blocks, width, reverse):
    at = (lambda b: blocks - 1 - b) if reverse else (lambda b: b)
    info = pl.BlockSpec((1, 8, width), lambda b, slot: (slot[at(b)], 0, 0))
    places = pl.BlockSpec((1, BLK), lambda b, slot: (0, 0))
    key = pl.BlockSpec((BLK, heads * DK), lambda b, slot: (slot[at(b)], 0))
    val = pl.BlockSpec((BLK, heads * DV), lambda b, slot: (slot[at(b)], 0))
    state = pl.BlockSpec((heads, 1, DK, DV), lambda b, slot: (0, at(b), 0, 0))
    return info, places, key, val, state


def retain_forward(slot, info, places, q, k, v, gate):
    rows, heads = q.shape[0], q.shape[1] // DK
    blocks = rows // BLK
    info_at, places_at, key, val, state = retain_specs(heads, blocks, info.shape[2], False)
    return pl.pallas_call(
        retain_forward_kernel,
        grid_spec=pltpu.PrefetchScalarGridSpec(
            num_scalar_prefetch=1,
            grid=(blocks,),
            in_specs=[info_at, places_at, key, key, val, val],
            out_specs=[val, val, state],
            scratch_shapes=[pltpu.VMEM((heads, DK, DV), jnp.float32)],
        ),
        out_shape=[
            jax.ShapeDtypeStruct((rows, heads * DV), jnp.float32),
            jax.ShapeDtypeStruct((rows, heads * DV), jnp.bfloat16),
            jax.ShapeDtypeStruct((heads, blocks, DK, DV), jnp.bfloat16),
        ],
        cost_estimate=pl.CostEstimate(
            flops=2 * heads * rows * (BLK * (3 * DK + DV) + 2 * DK * DV),
            bytes_accessed=rows * heads * (8 * DK + 12 * DV),
            transcendentals=rows * heads * (BLK + DV),
        ),
        name="retain_forward",
    )(slot, info, places, q, k, v, gate)


def retain_backward(slot, info, places, q, k, v, gate, retained, states, up):
    rows, heads = q.shape[0], q.shape[1] // DK
    blocks = rows // BLK
    info_at, places_at, key, val, state = retain_specs(heads, blocks, info.shape[2], True)
    return pl.pallas_call(
        retain_backward_kernel,
        grid_spec=pltpu.PrefetchScalarGridSpec(
            num_scalar_prefetch=1,
            grid=(blocks,),
            in_specs=[info_at, places_at, key, key, val, val, val, state, val],
            out_specs=[key, key, val, val],
            scratch_shapes=[pltpu.VMEM((heads, DK, DV), jnp.float32)],
        ),
        out_shape=[
            jax.ShapeDtypeStruct((rows, heads * DK), jnp.bfloat16),
            jax.ShapeDtypeStruct((rows, heads * DK), jnp.bfloat16),
            jax.ShapeDtypeStruct((rows, heads * DV), jnp.bfloat16),
            jax.ShapeDtypeStruct((rows, heads * DV), jnp.bfloat16),
        ],
        cost_estimate=pl.CostEstimate(
            flops=2 * heads * rows * (BLK * (5 * DK + 3 * DV) + 4 * DK * DV),
            bytes_accessed=rows * heads * (12 * DK + 20 * DV),
            transcendentals=rows * heads * (BLK + DV),
        ),
        name="retain_backward",
    )(slot, info, places, q, k, v, gate, retained, states, up)


def norm_grad(grad, gain, centred_unit, inverse):
    e = grad * gain
    mean_e = jnp.mean(e, axis=-1, keepdims=True)
    mean_en = jnp.mean(e * centred_unit, axis=-1, keepdims=True)
    return (e - mean_e - centred_unit * mean_en) * inverse


def local_gather(
    tokens,
    first_gain,
    query_weight,
    key_weight,
    value_weight,
    gate_weight,
    output_weight,
    second_gain,
    gelu_weight,
    linear_weight,
    down_weight,
    log_decay,
    first_start,
    cotangent,
):
    bf16, f32 = jnp.bfloat16, jnp.float32
    shards = lax.axis_size(SEQ)
    shard, group = lax.axis_index(SEQ), lax.axis_index(HEAD)
    rows, width = tokens.shape
    half = rows // 2
    total = shards * rows
    own = (shards - 2) * rows
    quarter = half // 2
    slab = width // shards
    key_scale = 1.0 / math.sqrt(DK)
    chip, core = (group // 2).astype(jnp.int32), (group % 2).astype(jnp.int32)
    place = shard.astype(jnp.int32)

    def narrow(a):
        return (2.0 * a).astype(bf16)

    def slab_of(a, at):
        return lax.dynamic_slice_in_dim(a, at * slab, slab, 1)

    def in_order(mine, other):
        return jnp.where(core == 0, jnp.concatenate([mine, other]), jnp.concatenate([other, mine]))

    def far_hops():
        return [[(i, (i + hop) % shards) for i in range(shards)] for hop in range(2, shards, 2)]

    def over_steps(own_rows, steps, weights, kinds, scales, turned):
        common = (weights, kinds, scales, turned, place)
        found = rows_product([own_rows], rows, *common, shards - 2, total)
        for index, parts in enumerate(steps):
            last = index + 1 == len(steps)
            found = rows_product(parts, quarter if last else half, *common, shards - 1 if last else index, total, found)
        return found

    normed_own, normed_half = norm_start(core, first_start, tokens, first_gain, log_decay)
    came = ring_gather(normed_half, quarter)
    info = [item[half:] for step in came[:-1] for item in (step[0], step[2])]
    info = jnp.stack(info + [normed_half[half:], came[-1][1][quarter:]])
    slot = ring_slots()
    lanes = jnp.arange(half)
    places = jnp.concatenate([core * half + lanes, (1 - core) * half + lanes]).astype(f32)[None]

    cotangent_half = of_rows(cotangent, core * half, half)
    cotangent_own = jnp.concatenate([cotangent_half, of_rows(cotangent, (1 - core) * half, half)], axis=0)
    cotangent_half = cotangent_half.astype(f32)
    token_half = of_rows(tokens, core * half, half).astype(f32)
    first_unit, first_inverse = norm_parts(token_half)

    def far_start(share):
        share = of_rows(share, chip * quarter, quarter)
        return [lax.ppermute(share, SEQ, hop) for hop in far_hops()]

    def far_parts(came):
        parts = []
        for item in came:
            both = [item, lax.ppermute(item, HEAD, ACROSS)]
            parts += both + [other_core(part) for part in both]
        return parts

    cotangent_far = far_start(after(0.5 * cotangent_half, came[-1][0]))
    cotangent_far = far_parts(cotangent_far)
    cotangent_far = round_rows(cotangent_far)

    in_slab, queries, keys, values, gate_pre = over_steps(
        normed_own,
        came,
        [query_weight, key_weight, value_weight, gate_weight],
        [f32, f32, bf16, f32],
        [1.0, key_scale, 1.0, 1.0],
        False,
    )
    retained, gated, states = retain_forward(slot, info, places, queries, keys, values, gate_pre)

    out_other = matmul(gated[own + half : own + rows], output_weight)
    out_mine = matmul(gated[own : own + half], output_weight)
    residual = token_half + head_total(out_mine, out_other)
    mid_unit, mid_inverse = norm_parts(residual)
    normed_mid_half = 0.5 * (mid_unit * second_gain)
    normed_mid_own = narrow(jnp.concatenate([normed_mid_half, other_core(normed_mid_half)], axis=0))
    mid_far = far_start(normed_mid_half)

    def hidden_mix(pre_gate, up_branch):
        return jax.nn.gelu(pre_gate, approximate=False) * up_branch

    def feed_forward(normed, grad_hidden):
        up_gate = matmul(normed, gelu_weight)
        up_proj = matmul(normed, linear_weight)
        hidden, back = jax.vjp(hidden_mix, up_gate, up_proj)
        grad_up_gate, grad_up = back(grad_hidden)
        return hidden.astype(bf16), grad_up_gate.astype(bf16), grad_up.astype(bf16)

    hidden, grad_up_gate, grad_up = feed_forward(normed_mid_own, transpose_right(cotangent_own, down_weight))

    def mid_part(at):
        return transpose_right(grad_up_gate[at : at + half], gelu_weight) + transpose_right(
            grad_up[at : at + half], linear_weight
        )

    mid_other = mid_part(half)
    mid_mine = mid_part(0)
    grad_mid = head_total(mid_mine, mid_other)
    grad_residual = cotangent_half + norm_grad(grad_mid, second_gain, mid_unit, mid_inverse)
    second_part = 0.5 * jnp.sum(grad_mid * mid_unit, axis=0)
    branch_came = ring_gather(grad_residual, quarter)
    branch_slab, grad_gated = over_steps(
        jnp.concatenate([grad_residual, other_core(grad_residual)], axis=0), branch_came, [output_weight], [f32], [1.0], True
    )

    mid_far = far_parts(mid_far)
    grad_hidden_far = transpose_right(cotangent_far, down_weight)
    normed_mid_far = round_rows(mid_far)
    hidden_far, grad_up_gate_far, grad_up_far = feed_forward(normed_mid_far, grad_hidden_far)

    res_other = matmul(hidden[half:], down_weight)
    res_mine = matmul(hidden[:half], down_weight)
    result = 0.5 * (after(residual, branch_came[1][0]) + head_total(res_mine, res_other))
    output_rows = narrow(in_order(result, other_core(result)))

    def pair_slab(a):
        return lax.dynamic_slice_in_dim(a, shard // 2 * (2 * slab), 2 * slab, 1)

    def pair_sum(left, right, left_far, right_far, dim):
        found = transpose_left(left, right)
        found = found + transpose_left(left_far, right_far)
        kept = lax.dynamic_slice_in_dim(found, shard % 2 * slab, slab, dim)
        sent = lax.dynamic_slice_in_dim(found, (1 - shard % 2) * slab, slab, dim)
        sent = lax.ppermute(after(sent, branch_came[-1][0]), SEQ, [(i, i ^ 1) for i in range(shards)])
        return kept + sent

    mid_slab, mid_slab_far = pair_slab(normed_mid_own), pair_slab(normed_mid_far)
    wgrad_down = pair_sum(hidden, pair_slab(cotangent_own), hidden_far, pair_slab(cotangent_far), 1)
    wgrad_gelu = pair_sum(mid_slab, grad_up_gate, mid_slab_far, grad_up_gate_far, 0)
    wgrad_linear = pair_sum(mid_slab, grad_up, mid_slab_far, grad_up_far, 0)

    wgrad_output = transpose_left(gated, branch_slab)
    grad_queries, grad_keys, grad_values, grad_gate_pre = retain_backward(
        slot, info, places, queries, keys, values, gate_pre, retained, states, grad_gated
    )

    def in_part(at):
        at = slice(own + at, own + at + half)
        return (
            transpose_right(grad_queries[at], query_weight)
            + transpose_right(grad_keys[at], key_weight)
            + transpose_right(grad_values[at], value_weight)
            + transpose_right(grad_gate_pre[at], gate_weight)
        )

    in_other = in_part(half)
    in_mine = in_part(0)
    grad_in = head_total(in_mine, in_other)
    wgrad_query = transpose_left(in_slab, grad_queries)
    wgrad_key = transpose_left(in_slab, grad_keys)
    wgrad_value = transpose_left(in_slab, grad_values)
    wgrad_gate = transpose_left(in_slab, grad_gate_pre)
    first_part = gain_part(core, tokens, in_mine, in_other)
    gains = exchange_sum(jnp.concatenate([first_part, second_part[None]]), SEQ)
    gains = gains + other_core(gains)
    grad_half = 0.5 * (grad_residual + norm_grad(grad_in, first_gain, first_unit, first_inverse))
    grad_tokens = narrow(in_order(grad_half, other_core(grad_half)))
    gains = after(gains, grad_in)
    gains = slab_of(gains + lax.ppermute(gains, HEAD, ACROSS), shard)
    return (
        output_rows,
        grad_tokens,
        gains[0],
        wgrad_query,
        wgrad_key,
        wgrad_value,
        wgrad_gate,
        wgrad_output,
        gains[1],
        wgrad_gelu,
        wgrad_linear,
        wgrad_down,
    )


def local(*arrays):
    tokens = lax.axis_size(SEQ) * arrays[0].shape[0]
    columns = sum(w.shape[1] for w in (*arrays[2:6], *arrays[8:10])) + arrays[6].shape[0] + arrays[10].shape[0]
    shards, groups = lax.axis_size(SEQ), lax.axis_size(HEAD)
    if groups == 4 and shards % 2 == 0 and arrays[0].shape[0] == BLK and 4 * tokens <= groups * columns:
        return local_gather(*arrays)
    return local_scatter(*arrays)


def solution(mesh):
    return jax.shard_map(
        local,
        mesh=mesh,
        in_specs=(
            P(SEQ, None),
            P(),
            P(None, HEAD),
            P(None, HEAD),
            P(None, HEAD),
            P(None, HEAD),
            P(HEAD, None),
            P(),
            P(None, HEAD),
            P(None, HEAD),
            P(HEAD, None),
            P(HEAD, SEQ),
            P(SEQ),
            P(SEQ, None),
        ),
        out_specs=(
            P(SEQ, None),
            P(SEQ, None),
            P(SEQ),
            P(SEQ, HEAD),
            P(SEQ, HEAD),
            P(SEQ, HEAD),
            P(SEQ, HEAD),
            P(HEAD, SEQ),
            P(SEQ),
            P(SEQ, HEAD),
            P(SEQ, HEAD),
            P(HEAD, SEQ),
        ),
        check_vma=False,
    )
```

```python
import functools
import math

import jax
import jax.numpy as jnp
from jax import lax
from jax.experimental import pallas as pl
from jax.experimental.pallas import tpu as pltpu
from jax.sharding import PartitionSpec as P


SEQ = "seq"
HEAD = "head"
DK = 256
DV = 512
BLK = 256


maximum_precision = lax.Precision.HIGHEST
eps_norm = 1e-05


def carried_in(part, axis, combine, identity, reverse):
    count = lax.axis_size(axis)
    place = lax.axis_index(axis)
    ahead = count - 1 - place if reverse else place
    gathered = jax.tree.map(lambda a: lax.all_gather(a, axis), part)
    state = jax.tree.map(lambda a, e: jnp.zeros_like(a) + jnp.asarray(e, a.dtype), part, identity)

    def one(hop, state):
        source = count - 1 - hop if reverse else hop
        return combine(
            state, jax.tree.map(lambda a: lax.dynamic_index_in_dim(a, source, 0, False), gathered)
        )

    return lax.fori_loop(0, ahead, one, state)


def matmul(left_side, right_side):
    return jnp.dot(left_side, right_side, preferred_element_type=jnp.float32)


def transpose_left(left_side, right_side):
    return lax.dot_general(
        left_side, right_side, (((0,), (0,)), ((), ())), preferred_element_type=jnp.float32
    )


def transpose_right(left_side, right_side):
    return lax.dot_general(
        left_side, right_side, (((1,), (1,)), ((), ())), preferred_element_type=jnp.float32
    )


def layer_norm(activity, gain_row):
    centre = jnp.mean(activity, axis=-1, keepdims=True)
    centred = activity - centre
    spread = jnp.mean(centred * centred, axis=-1, keepdims=True)
    return centred * lax.rsqrt(spread + eps_norm) * gain_row


def group_norm(activity):
    centre = jnp.mean(activity, axis=-1, keepdims=True)
    centred = activity - centre
    spread = jnp.mean(centred * centred, axis=-1, keepdims=True)
    return centred * lax.rsqrt(spread + eps_norm)


def retain_block(carried, query_slice, key_slice, value_slice, rate_part, flag_part):
    cumulative = jnp.cumsum(rate_part, axis=1)
    started = jnp.cumsum(flag_part)
    block_len = flag_part.shape[0]
    position = jnp.arange(block_len)
    causal_same = (started[:, None] == started[None, :]) & (position[:, None] >= position[None, :])
    log_gap = cumulative[:, :, None] - cumulative[:, None, :]
    weight_matrix = jnp.where(
        causal_same[None], jnp.exp(jnp.where(causal_same[None], log_gap, 0.0)), 0.0
    )
    attention_scores = (
        jnp.einsum("keu,reu->ekr", query_slice, key_slice, precision=maximum_precision)
        * weight_matrix
    )
    within = jnp.einsum("hnm,mhe->nhe", attention_scores, value_slice, precision=maximum_precision)
    before = (started == 0).astype(jnp.float32)
    reach_in = jnp.exp(cumulative) * before[None, :]
    across = jnp.einsum(
        "nhd,hde->nhe", query_slice * reach_in.T[:, :, None], carried, precision=maximum_precision
    )
    last_count = started[-1]
    trailing_weight = (
        jnp.exp(cumulative[:, -1:] - cumulative)
        * (started == last_count).astype(jnp.float32)[None, :]
    )
    keep_factor = jnp.exp(cumulative[:, -1]) * (last_count == 0).astype(jnp.float32)
    zeroed_state = jnp.einsum(
        "ygc,ygs->gcs",
        key_slice * trailing_weight.T[:, :, None],
        value_slice,
        precision=maximum_precision,
    )
    return (keep_factor[:, None, None] * carried + zeroed_state, within + across)


def retain(queries, key_heads, value_heads, log_rates, start_flag, initial):
    block_count = queries.shape[0] // BLK
    head_count = queries.shape[1]
    query_blocks = queries.reshape(block_count, BLK, head_count, queries.shape[2])
    key_blocks = key_heads.reshape(block_count, BLK, head_count, key_heads.shape[2])
    value_blocks = value_heads.reshape(block_count, BLK, head_count, value_heads.shape[2])
    rate_blocks = log_rates.reshape(head_count, block_count, BLK).transpose(1, 0, 2)
    flag_blocks = start_flag.reshape(block_count, BLK)

    def scan_step(carried, block_items):
        return retain_block(carried, *block_items)

    final_state, block_outputs = lax.scan(
        jax.checkpoint(scan_step),
        initial,
        (query_blocks, key_blocks, value_blocks, rate_blocks, flag_blocks),
    )
    return (block_outputs.reshape(block_count * BLK, head_count, value_heads.shape[2]), final_state)


def link_maps(earlier, later):
    return (earlier[0] * later[0], later[0][:, None, None] * earlier[1] + later[1])


def local_scatter(
    tokens,
    first_gain,
    query_weight,
    key_weight,
    value_weight,
    gate_weight,
    output_weight,
    second_gain,
    gelu_weight,
    linear_weight,
    down_weight,
    log_decay,
    first_start,
    cotangent,
):
    token_rows = tokens.shape[0]
    head_count = query_weight.shape[1] // DK
    key_scale = 1.0 / math.sqrt(DK)
    position = jnp.arange(token_rows, dtype=jnp.int32)
    start_flag = (position == first_start[0]).astype(jnp.float32)
    before = (position < first_start[0]).astype(jnp.float32)
    reach_in = jnp.exp(jnp.cumsum(log_decay, axis=1)) * before[None, :]
    shard_keep = jnp.exp(jnp.sum(log_decay, axis=1)) * (first_start[0] == token_rows).astype(
        jnp.float32
    )
    empty_state = jnp.zeros((head_count, DK, DV), jnp.float32)
    inputs = tokens.astype(jnp.float32)
    normed_in = layer_norm(inputs, first_gain).astype(jnp.bfloat16)
    queries = matmul(normed_in, query_weight)
    scaled_keys = matmul(normed_in, key_weight) * key_scale
    values = matmul(normed_in, value_weight)
    gate_pre = matmul(normed_in, gate_weight)
    query_heads = queries.reshape(token_rows, head_count, DK)
    key_heads = scaled_keys.reshape(token_rows, head_count, DK)
    value_heads = values.reshape(token_rows, head_count, DV)
    local_out, local_end = retain(
        query_heads, key_heads, value_heads, log_decay, start_flag, empty_state
    )
    weighted_query = query_heads * reach_in.T[:, :, None]
    incoming = carried_in(
        (shard_keep, local_end), SEQ, link_maps, (jnp.ones_like(shard_keep), empty_state), False
    )[1]
    retained = local_out + jnp.einsum(
        "nhd,hde->nhe", weighted_query, incoming, precision=maximum_precision
    )

    def gate_mix(gate_in, retained_in):
        return jax.nn.silu(gate_in) * group_norm(retained_in).reshape(token_rows, head_count * DV)

    gated_rows = gate_mix(gate_pre, retained).astype(jnp.bfloat16)
    residual = inputs + lax.psum(matmul(gated_rows, output_weight), HEAD)
    normed_mid = layer_norm(residual, second_gain).astype(jnp.bfloat16)
    up_gate = matmul(normed_mid, gelu_weight)
    up_proj = matmul(normed_mid, linear_weight)

    def hidden_mix(pre_gate, up_branch):
        return jax.nn.gelu(pre_gate, approximate=False) * up_branch

    hidden = hidden_mix(up_gate, up_proj).astype(jnp.bfloat16)
    result = residual + lax.psum(matmul(hidden, down_weight), HEAD)
    output_rows = result.astype(jnp.bfloat16)
    grad_hidden = transpose_right(cotangent, down_weight)
    wgrad_down = transpose_left(hidden, cotangent)
    _, hidden_back = jax.vjp(hidden_mix, up_gate, up_proj)
    grad_up_gate, grad_up = hidden_back(grad_hidden)
    grad_up_gate = grad_up_gate.astype(jnp.bfloat16)
    grad_up = grad_up.astype(jnp.bfloat16)
    grad_mid_in = lax.psum(
        transpose_right(grad_up_gate, gelu_weight) + transpose_right(grad_up, linear_weight), HEAD
    )
    wgrad_gelu = transpose_left(normed_mid, grad_up_gate)
    wgrad_linear = transpose_left(normed_mid, grad_up)
    _, second_back = jax.vjp(layer_norm, residual, second_gain)
    grad_mid_norm, wgrad_second = second_back(grad_mid_in)
    grad_residual = cotangent.astype(jnp.float32) + grad_mid_norm
    grad_branch = grad_residual.astype(jnp.bfloat16)
    grad_gated = transpose_right(grad_branch, output_weight)
    wgrad_output = transpose_left(gated_rows, grad_branch)
    _, gate_back = jax.vjp(gate_mix, gate_pre, retained)
    grad_gate_pre, grad_retained = gate_back(grad_gated)
    grad_gate_pre = grad_gate_pre.astype(jnp.bfloat16)
    local_in = jnp.einsum(
        "nhd,nhe->hde", weighted_query, grad_retained, precision=maximum_precision
    )
    beyond = carried_in(
        (shard_keep, local_in), SEQ, link_maps, (jnp.ones_like(shard_keep), empty_state), True
    )[1]

    def local_retain(query_in, key_in, value_in):
        return retain(query_in, key_in, value_in, log_decay, start_flag, incoming)

    _, retain_back = jax.vjp(local_retain, query_heads, key_heads, value_heads)
    grad_q, grad_k, grad_v = retain_back((grad_retained, beyond))
    grad_queries = grad_q.reshape(token_rows, head_count * DK).astype(jnp.bfloat16)
    grad_keys = (grad_k * key_scale).reshape(token_rows, head_count * DK).astype(jnp.bfloat16)
    grad_values = grad_v.reshape(token_rows, head_count * DV).astype(jnp.bfloat16)
    grad_in = lax.psum(
        transpose_right(grad_queries, query_weight)
        + transpose_right(grad_keys, key_weight)
        + transpose_right(grad_values, value_weight)
        + transpose_right(grad_gate_pre, gate_weight),
        HEAD,
    )
    wgrad_query = transpose_left(normed_in, grad_queries)
    wgrad_key = transpose_left(normed_in, grad_keys)
    wgrad_value = transpose_left(normed_in, grad_values)
    wgrad_gate = transpose_left(normed_in, grad_gate_pre)
    _, first_back = jax.vjp(layer_norm, inputs, first_gain)
    grad_in_norm, wgrad_first = first_back(grad_in)
    grad_tokens = (grad_residual + grad_in_norm).astype(jnp.bfloat16)
    summed = tuple(
        (
            lax.psum_scatter(wgrad_first, SEQ, scatter_dimension=0, tiled=True),
            lax.psum_scatter(wgrad_query, SEQ, scatter_dimension=0, tiled=True),
            lax.psum_scatter(wgrad_key, SEQ, scatter_dimension=0, tiled=True),
            lax.psum_scatter(wgrad_value, SEQ, scatter_dimension=0, tiled=True),
            lax.psum_scatter(wgrad_gate, SEQ, scatter_dimension=0, tiled=True),
            lax.psum_scatter(wgrad_output, SEQ, scatter_dimension=1, tiled=True),
            lax.psum_scatter(wgrad_second, SEQ, scatter_dimension=0, tiled=True),
            lax.psum_scatter(wgrad_gelu, SEQ, scatter_dimension=0, tiled=True),
            lax.psum_scatter(wgrad_linear, SEQ, scatter_dimension=0, tiled=True),
            lax.psum_scatter(wgrad_down, SEQ, scatter_dimension=1, tiled=True),
        )
    )
    return (output_rows, grad_tokens) + summed


def exchange_sum(rows, axis):
    count = lax.axis_size(axis)
    bit = count // 2
    while bit:
        rows = rows + lax.ppermute(rows, axis, [(i, i ^ bit) for i in range(count)])
        bit //= 2
    return rows


CHIP = [(0, 1), (1, 0), (2, 3), (3, 2)]
ACROSS = [(0, 2), (2, 0), (1, 3), (3, 1)]


def of_rows(a, start, size):
    return lax.dynamic_slice_in_dim(a, start, size, 0)


def after(a, *others):
    return lax.optimization_barrier((a, *others))[0]


def head_total(mine, other):
    other = lax.ppermute(other, HEAD, CHIP)
    both = mine + other
    return both + lax.ppermute(both, HEAD, ACROSS)


def other_core(a):
    return lax.ppermute(a, HEAD, CHIP)


def ring_order(count):
    return list(range(0, count, 2)) + list(range(count - 1, 0, -2))


def ring_gather(half, split):
    count = lax.axis_size(SEQ)
    order = ring_order(count)
    up = [(order[i], order[(i + 1) % count]) for i in range(count)]
    down = [(target, source) for source, target in up]
    steps = []
    rising = falling = half
    for hop in range(1, count // 2 + 1):
        if hop == count // 2:
            rising, falling = rising[:split], falling[split:]
        rising, falling = lax.ppermute(rising, SEQ, up), lax.ppermute(falling, SEQ, down)
        others = other_core(rising), other_core(falling)
        if hop == count // 2:
            steps.append([rising, falling, *others])
        else:
            steps.append([rising, others[0], falling, others[1]])
    return steps


def ring_slots():
    count = lax.axis_size(SEQ)
    index = jnp.arange(count, dtype=jnp.int32)

    def position(shard):
        return jnp.where(shard % 2 == 0, shard // 2, count - 1 - shard // 2)

    behind = (position(lax.axis_index(SEQ).astype(jnp.int32)) - position(index)) % count
    steps = jnp.where(behind < count // 2, 2 * behind - 2, 2 * (count - behind) - 1)
    return jnp.where(behind == 0, count - 2, jnp.where(behind == count // 2, count - 1, steps))


def dot_nt(left, right):
    return lax.dot_general(left, right, (((1,), (1,)), ((), ())), preferred_element_type=jnp.float32)


def dot_tn(left, right):
    return lax.dot_general(left, right, (((0,), (0,)), ((), ())), preferred_element_type=jnp.float32)


def dot_nn(left, right):
    return lax.dot_general(left, right, (((1,), (0,)), ((), ())), preferred_element_type=jnp.float32)


def half_split_dot(left, right, dot):
    left_high = left.astype(jnp.bfloat16)
    left_low = (left - left_high.astype(jnp.float32)).astype(jnp.bfloat16)
    return dot(left_high, right) + dot(left_low, right)


def norm_parts(retained):
    centre = jnp.mean(retained, axis=-1, keepdims=True)
    centred = retained - centre
    inverse = lax.rsqrt(jnp.mean(centred * centred, axis=-1, keepdims=True) + eps_norm)
    return centred * inverse, inverse


def norm_start_kernel(core_ref, first_ref, tokens_ref, gain_ref, rates_ref, normed_ref, half_ref, info_ref):
    half = tokens_ref.shape[0] // 2
    for index, core in enumerate((core_ref[0], 1 - core_ref[0])):
        rows = tokens_ref[pl.ds(pl.multiple_of(core * half, half), half), :].astype(jnp.float32)
        normed = (norm_parts(rows)[0] * gain_ref[...]).astype(jnp.bfloat16)
        normed_ref[index * half : (index + 1) * half, :] = normed
        if index == 0:
            half_ref[...] = normed.astype(jnp.float32)
    heads, size = rates_ref.shape
    info_ref[...] = jnp.full(info_ref.shape, first_ref[0], jnp.int32).astype(jnp.float32)
    for head in range(heads):
        info_ref[0:1, head * size : (head + 1) * size] = rates_ref[head : head + 1, :]


def norm_start(core, first_start, tokens, gain, log_decay):
    rows, width = tokens.shape
    vmem, smem = pl.BlockSpec(memory_space=pltpu.VMEM), pl.BlockSpec(memory_space=pltpu.SMEM)
    return pl.pallas_call(
        norm_start_kernel,
        in_specs=[smem, smem, vmem, vmem, vmem],
        out_specs=[vmem, vmem, vmem],
        out_shape=[
            jax.ShapeDtypeStruct((rows, width), jnp.bfloat16),
            jax.ShapeDtypeStruct((rows // 2, width), jnp.float32),
            jax.ShapeDtypeStruct((8, log_decay.size), jnp.float32),
        ],
        compiler_params=pltpu.CompilerParams(vmem_limit_bytes=10 << 20),
        name="norm_start",
    )(core[None], first_start, tokens, gain[None], log_decay)


def gain_part_kernel(core_ref, tokens_ref, mine_ref, other_ref, out_ref):
    half = mine_ref.shape[0]
    total = jnp.zeros(out_ref.shape, jnp.float32)
    for grad_ref, core in ((mine_ref, core_ref[0]), (other_ref, 1 - core_ref[0])):
        rows = tokens_ref[pl.ds(pl.multiple_of(core * half, half), half), :].astype(jnp.float32)
        total = total + jnp.sum(grad_ref[...] * norm_parts(rows)[0], axis=0, keepdims=True)
    out_ref[...] = total


def gain_part(core, tokens, mine, other):
    vmem, smem = pl.BlockSpec(memory_space=pltpu.VMEM), pl.BlockSpec(memory_space=pltpu.SMEM)
    return pl.pallas_call(
        gain_part_kernel,
        in_specs=[smem, vmem, vmem, vmem],
        out_specs=vmem,
        out_shape=jax.ShapeDtypeStruct((1, tokens.shape[1]), jnp.float32),
        cost_estimate=pl.CostEstimate(flops=10 * tokens.size, bytes_accessed=6 * tokens.size, transcendentals=0),
        compiler_params=pltpu.CompilerParams(vmem_limit_bytes=10 << 20),
        name="gain_part",
    )(core[None], tokens, mine, other)


def rows_product_kernel(parts, tiles, pieces, scales, turned, shard_ref, *refs):
    weights = len(tiles)
    part_refs, slab_refs = refs[:parts], refs[parts : 2 * parts]
    weight_refs = refs[2 * parts : 2 * parts + weights]
    outs = refs[len(refs) - sum(pieces) - 2 : len(refs) - 1]
    x = refs[-1]
    step = pl.program_id(0)
    size = x.shape[0] // parts

    @pl.when(step == 0)
    def _():
        for index in range(parts):
            at = slice(index * size, (index + 1) * size)
            x[at, :] = part_refs[index][...].astype(jnp.bfloat16)
            outs[0][at, :] = slab_refs[index][...].astype(jnp.bfloat16)

    start, at = 0, 1
    for weight, count, number, scale in zip(weight_refs, tiles, pieces, scales):

        @pl.when((step >= start) & (step < start + count))
        def _(weight=weight, results=outs[at : at + number], scale=scale):
            found = (dot_nt if turned else dot_nn)(x[...], weight[...])
            if scale != 1.0:
                found = found * scale
            high = found.astype(jnp.bfloat16)
            results[0][...] = high
            if len(results) == 2:
                results[1][...] = (found - high.astype(jnp.float32)).astype(jnp.bfloat16)

        start += count
        at += number


def rows_product(parts, size, weights, pieces, scales, turned, shard, block, total, buffers=None):
    count, width = len(parts), parts[0].shape[1]
    rows = count * size
    tile = 512
    columns = [w.shape[0] if turned else w.shape[1] for w in weights]
    tiles = [c // tile for c in columns]
    starts = [sum(tiles[:i]) for i in range(len(tiles))]
    slab = width // lax.axis_size(SEQ)

    def at(j, start, number):
        return jnp.clip(j - start, 0, number - 1)

    in_specs = [pl.BlockSpec((size, width), lambda j, s: (0, 0)) for _ in parts]
    in_specs += [pl.BlockSpec((size, slab), lambda j, s: (0, s[0])) for _ in parts]
    for start, number in zip(starts, tiles):
        if turned:
            in_specs.append(pl.BlockSpec((tile, width), lambda j, s, a=start, n=number: (at(j, a, n), 0)))
        else:
            in_specs.append(pl.BlockSpec((width, tile), lambda j, s, a=start, n=number: (0, at(j, a, n))))
    out_specs = [pl.BlockSpec((rows, slab), lambda j, s: (block, 0))]
    out_shape = [jax.ShapeDtypeStruct((total, slab), jnp.bfloat16)]
    for start, number, results, c in zip(starts, tiles, pieces, columns):
        out_specs += [pl.BlockSpec((rows, tile), lambda j, s, a=start, n=number: (block, at(j, a, n)))] * results
        out_shape += [jax.ShapeDtypeStruct((total, c), jnp.bfloat16)] * results
    operands = [*parts, *parts, *weights]
    aliases = {}
    if buffers is not None:
        aliases = {1 + len(operands) + i: i for i in range(len(buffers))}
        in_specs += [pl.BlockSpec(memory_space=pl.ANY)] * len(buffers)
        operands += buffers
    return pl.pallas_call(
        functools.partial(rows_product_kernel, count, tiles, pieces, scales, turned),
        grid_spec=pltpu.PrefetchScalarGridSpec(
            num_scalar_prefetch=1,
            grid=(sum(tiles),),
            in_specs=in_specs,
            out_specs=out_specs,
            scratch_shapes=[pltpu.VMEM((rows, width), jnp.bfloat16)],
        ),
        out_shape=out_shape,
        input_output_aliases=aliases,
        cost_estimate=pl.CostEstimate(
            flops=2 * rows * width * sum(columns),
            bytes_accessed=4 * rows * width + 2 * width * sum(columns) + 2 * rows * sum(columns),
            transcendentals=0,
        ),
        compiler_params=pltpu.CompilerParams(vmem_limit_bytes=(40 if turned else 52) << 20),
        name="rows_product",
    )(shard[None], *operands)


def rows_sum_kernel(counts, turned, *refs):
    number = len(counts)
    rows_refs, weight_refs = refs[:number], refs[number : 2 * number]
    mine, other, total = refs[2 * number :]
    step = pl.program_id(0)
    start = 0
    for rows, weight, count in zip(rows_refs, weight_refs, counts):

        @pl.when((step >= start) & (step < start + count))
        def _(rows=rows, weight=weight, start=start):
            found = dot_nt(weight[...], rows[...]) if turned else dot_nn(rows[...], weight[...])
            if start:
                total[...] += found
            else:
                total[...] = jnp.where(step == 0, found, total[...] + found)

        start += count

    @pl.when(step == start - 1)
    def _():
        half = mine.shape[0]
        mine[...] = total[:, :half].T if turned else total[:half, :]
        other[...] = total[:, half:].T if turned else total[half:, :]


def rows_sum(arrays, weights, block, rows, turned):
    tile = 512
    width = weights[0].shape[0] if turned else weights[0].shape[1]
    counts = [a.shape[1] // tile for a in arrays]
    starts = [sum(counts[:i]) for i in range(len(counts))]

    def at(j, start, number):
        return jnp.clip(j - start, 0, number - 1)

    in_specs = [
        pl.BlockSpec((rows, tile), lambda j, a=start, n=number: (block, at(j, a, n)))
        for start, number in zip(starts, counts)
    ]
    for start, number in zip(starts, counts):
        if turned:
            in_specs.append(pl.BlockSpec((width, tile), lambda j, a=start, n=number: (0, at(j, a, n))))
        else:
            in_specs.append(pl.BlockSpec((tile, width), lambda j, a=start, n=number: (at(j, a, n), 0)))
    half = pl.BlockSpec((rows // 2, width), lambda j: (0, 0))
    depth = sum(a.shape[1] for a in arrays)
    return pl.pallas_call(
        functools.partial(rows_sum_kernel, counts, turned),
        grid_spec=pltpu.PrefetchScalarGridSpec(
            num_scalar_prefetch=0,
            grid=(sum(counts),),
            in_specs=in_specs,
            out_specs=[half, half],
            scratch_shapes=[pltpu.VMEM((width, rows) if turned else (rows, width), jnp.float32)],
        ),
        out_shape=[jax.ShapeDtypeStruct((rows // 2, width), jnp.float32)] * 2,
        cost_estimate=pl.CostEstimate(
            flops=2 * rows * width * depth,
            bytes_accessed=2 * (rows + width) * depth + 4 * rows * width,
            transcendentals=0,
        ),
        name="rows_sum",
    )(*arrays, *weights)


def round_rows_kernel(*refs):
    out = refs[-1]
    at = 0
    for part in refs[:-1]:
        size = part.shape[0]
        out[at : at + size, :] = (2.0 * part[...]).astype(jnp.bfloat16)
        at += size


def round_rows(parts):
    vmem = pl.BlockSpec(memory_space=pltpu.VMEM)
    rows, width = sum(part.shape[0] for part in parts), parts[0].shape[1]
    return pl.pallas_call(
        round_rows_kernel,
        in_specs=[vmem] * len(parts),
        out_specs=vmem,
        out_shape=jax.ShapeDtypeStruct((rows, width), jnp.bfloat16),
        cost_estimate=pl.CostEstimate(flops=rows * width, bytes_accessed=6 * rows * width, transcendentals=0),
        compiler_params=pltpu.CompilerParams(vmem_limit_bytes=14 << 20),
        name="round_rows",
    )(*parts)


def causal(first, places):
    size = places.shape[1]
    column = jnp.broadcast_to(places, (size, size))
    row = column.T
    return (row >= column) & ((column >= first) | (row < first)), row


def block_decay(rates, first, seen, row):
    size = rates.shape[1]
    nth = lax.broadcasted_iota(jnp.int32, (size, size), 1).astype(jnp.float32)
    per_row = jnp.sum(jnp.where(nth <= row, rates, 0.0), axis=1, keepdims=True)
    down = jnp.broadcast_to(per_row, (size, size))
    weights = jnp.exp(jnp.where(seen, down - down.T, -jnp.inf))
    place = row[:, :1]
    last = jnp.sum(rates, axis=1, keepdims=True)
    whole = first >= size
    reach = jnp.where(place < first, jnp.exp(per_row), 0.0)
    trail = jnp.where((place >= first) | whole, jnp.exp(last - per_row), 0.0)
    keep = jnp.where(whole, jnp.exp(last), 0.0)
    return weights, reach, trail, keep


def head_lanes(head):
    return slice(head * DK, (head + 1) * DK), slice(head * DV, (head + 1) * DV), slice(head * BLK, (head + 1) * BLK)


def retain_forward_kernel(
    slot_ref, info_ref, places_ref, q_ref, q_rest_ref, k_ref, k_rest_ref, v_ref, gate_ref,
    normed_ref, gated_ref, state_ref, weights_ref, scores_ref, column_ref, state,
):
    @pl.when(pl.program_id(0) == 0)
    def _():
        state[...] = jnp.zeros_like(state)

    first = info_ref[0, 1:2, :1]
    seen, row = causal(first, places_ref[...])
    number = lax.broadcasted_iota(jnp.int32, column_ref.shape[2:], 1)
    for head in range(state.shape[0]):
        key, val, lane = head_lanes(head)
        weights, reach, trail, keep = block_decay(info_ref[0, 0:1, lane], first, seen, row)
        q, k, v = q_ref[:, key], k_ref[:, key], v_ref[:, val]
        held = state[head].astype(jnp.bfloat16)
        state_ref[head, 0] = held
        scores = dot_nt(q, k) + (dot_nt(q_rest_ref[:, key], k) + dot_nt(q, k_rest_ref[:, key]))
        scores = (scores * weights).astype(jnp.bfloat16)
        retained = dot_nn(scores, v) + reach * dot_nn(q, held)
        state[head] = keep * state[head] + dot_tn((k * trail).astype(jnp.bfloat16), v)
        normed, inverse = norm_parts(retained)
        gate = gate_ref[:, val].astype(jnp.float32)
        gated_ref[:, val] = (gate * jax.nn.sigmoid(gate) * normed).astype(jnp.bfloat16)
        normed_ref[:, val] = normed
        weights_ref[head, 0] = weights
        scores_ref[head, 0] = scores
        column_ref[head, 0] = jnp.where(
            number == 0, reach, jnp.where(number == 1, trail, jnp.where(number == 2, inverse, keep))
        )


def retain_backward_kernel(
    slot_ref, q_ref, k_ref, v_ref, gate_ref, normed_ref, state_ref, weights_ref, scores_ref, column_ref, up_ref,
    dq_ref, dk_ref, dv_ref, dgate_ref, beyond,
):
    @pl.when(pl.program_id(0) == 0)
    def _():
        beyond[...] = jnp.zeros_like(beyond)

    for head in range(beyond.shape[0]):
        key, val, _ = head_lanes(head)
        column = column_ref[head, 0]
        reach, trail, inverse, keep = column[:, 0:1], column[:, 1:2], column[:, 2:3], column[0:1, 3:4]
        weights, scores = weights_ref[head, 0], scores_ref[head, 0]
        q, k, v, normed = q_ref[:, key], k_ref[:, key], v_ref[:, val], normed_ref[:, val]
        gate, up = gate_ref[:, val].astype(jnp.float32), up_ref[:, val].astype(jnp.float32)
        sig = jax.nn.sigmoid(gate)
        silu = gate * sig
        dgate_ref[:, val] = (up * normed * (sig + silu * (1.0 - sig))).astype(jnp.bfloat16)
        g = up * silu
        mean_g = jnp.mean(g, axis=-1, keepdims=True)
        mean_gn = jnp.mean(g * normed, axis=-1, keepdims=True)
        grad = (g - mean_g - normed * mean_gn) * inverse
        after_block = beyond[head].astype(jnp.bfloat16)
        dscores = (half_split_dot(grad, v, dot_nt) * weights).astype(jnp.bfloat16)
        grad = grad.astype(jnp.bfloat16)
        q_reach = (q * reach).astype(jnp.bfloat16)
        dq_ref[:, key] = (dot_nn(dscores, k) + reach * dot_nt(grad, state_ref[head, 0])).astype(jnp.bfloat16)
        dk = dot_tn(dscores, q) + trail * dot_nt(v, after_block)
        dk_ref[:, key] = (dk * (1.0 / math.sqrt(DK))).astype(jnp.bfloat16)
        dv_ref[:, val] = (dot_tn(scores, grad) + trail * dot_nn(k, after_block)).astype(jnp.bfloat16)
        beyond[head] = keep * beyond[head] + dot_tn(q_reach, grad)


def retain_specs(heads, blocks, width, reverse):
    at = (lambda b: blocks - 1 - b) if reverse else (lambda b: b)
    info = pl.BlockSpec((1, 8, width), lambda b, slot: (at(b), 0, 0))
    places = pl.BlockSpec((1, BLK), lambda b, slot: (0, 0))
    key = pl.BlockSpec((BLK, heads * DK), lambda b, slot: (slot[at(b)], 0))
    val = pl.BlockSpec((BLK, heads * DV), lambda b, slot: (slot[at(b)], 0))
    held = [
        pl.BlockSpec((heads, 1, up, across), lambda b, slot: (0, at(b), 0, 0))
        for up, across in ((DK, DV), (BLK, BLK), (BLK, BLK), (BLK, 128))
    ]
    return info, places, key, val, held


def retain_forward(slot, info, places, queries_keys, v, gate):
    rows, heads = v.shape[0], v.shape[1] // DV
    blocks = rows // BLK
    info_at, places_at, key, val, held = retain_specs(heads, blocks, info.shape[2], False)
    return pl.pallas_call(
        retain_forward_kernel,
        grid_spec=pltpu.PrefetchScalarGridSpec(
            num_scalar_prefetch=1,
            grid=(blocks,),
            in_specs=[info_at, places_at, key, key, key, key, val, val],
            out_specs=[val, val, *held],
            scratch_shapes=[pltpu.VMEM((heads, DK, DV), jnp.float32)],
        ),
        out_shape=[
            jax.ShapeDtypeStruct((rows, heads * DV), jnp.float32),
            jax.ShapeDtypeStruct((rows, heads * DV), jnp.bfloat16),
            jax.ShapeDtypeStruct((heads, blocks, DK, DV), jnp.bfloat16),
            jax.ShapeDtypeStruct((heads, blocks, BLK, BLK), jnp.float32),
            jax.ShapeDtypeStruct((heads, blocks, BLK, BLK), jnp.bfloat16),
            jax.ShapeDtypeStruct((heads, blocks, BLK, 128), jnp.float32),
        ],
        cost_estimate=pl.CostEstimate(
            flops=2 * heads * rows * (BLK * (3 * DK + DV) + 2 * DK * DV),
            bytes_accessed=rows * heads * (8 * DK + 12 * DV),
            transcendentals=rows * heads * (BLK + DV),
        ),
        name="retain_forward",
    )(slot, info, places, *queries_keys, v, gate)


def retain_backward(slot, queries_keys, v, gate, normed, held, up):
    rows, heads = v.shape[0], v.shape[1] // DV
    blocks = rows // BLK
    _, _, key, val, held_at = retain_specs(heads, blocks, 0, True)
    return pl.pallas_call(
        retain_backward_kernel,
        grid_spec=pltpu.PrefetchScalarGridSpec(
            num_scalar_prefetch=1,
            grid=(blocks,),
            in_specs=[key, key, val, val, val, *held_at, val],
            out_specs=[key, key, val, val],
            scratch_shapes=[pltpu.VMEM((heads, DK, DV), jnp.float32)],
        ),
        out_shape=[
            jax.ShapeDtypeStruct((rows, heads * DK), jnp.bfloat16),
            jax.ShapeDtypeStruct((rows, heads * DK), jnp.bfloat16),
            jax.ShapeDtypeStruct((rows, heads * DV), jnp.bfloat16),
            jax.ShapeDtypeStruct((rows, heads * DV), jnp.bfloat16),
        ],
        cost_estimate=pl.CostEstimate(
            flops=2 * heads * rows * (BLK * (5 * DK + 3 * DV) + 4 * DK * DV),
            bytes_accessed=rows * heads * (12 * DK + 20 * DV),
            transcendentals=rows * heads * (BLK + DV),
        ),
        name="retain_backward",
    )(slot, *queries_keys, v, gate, normed, *held, up)


def norm_grad(grad, gain, centred_unit, inverse):
    e = grad * gain
    mean_e = jnp.mean(e, axis=-1, keepdims=True)
    mean_en = jnp.mean(e * centred_unit, axis=-1, keepdims=True)
    return (e - mean_e - centred_unit * mean_en) * inverse


def local_gather(
    tokens,
    first_gain,
    query_weight,
    key_weight,
    value_weight,
    gate_weight,
    output_weight,
    second_gain,
    gelu_weight,
    linear_weight,
    down_weight,
    log_decay,
    first_start,
    cotangent,
):
    bf16, f32 = jnp.bfloat16, jnp.float32
    shards = lax.axis_size(SEQ)
    shard, group = lax.axis_index(SEQ), lax.axis_index(HEAD)
    rows, width = tokens.shape
    half = rows // 2
    total = shards * rows
    quarter = half // 2
    slab = width // shards
    key_scale = 1.0 / math.sqrt(DK)
    chip, core = (group // 2).astype(jnp.int32), (group % 2).astype(jnp.int32)
    place = shard.astype(jnp.int32)

    def narrow(a):
        return (2.0 * a).astype(bf16)

    def slab_of(a, at):
        return lax.dynamic_slice_in_dim(a, at * slab, slab, 1)

    def in_order(mine, other):
        return jnp.where(core == 0, jnp.concatenate([mine, other]), jnp.concatenate([other, mine]))

    def far_hops():
        return [[(i, (i + hop) % shards) for i in range(shards)] for hop in range(2, shards, 2)]

    def over_steps(own_parts, steps, groups, weights, pieces, scales, turned):
        common = (weights, pieces, scales, turned, place)
        found = rows_product(own_parts, rows // len(own_parts), *common, shards - 2, total)
        for index, group in enumerate(groups):
            parts = [part for step in group for part in steps[step]]
            last = index + 1 == len(groups)
            block = shards - 1 if last else group[0] // len(group)
            found = rows_product(parts, quarter if last else half, *common, block, total, found)
        return found

    normed_own, normed_half, info = norm_start(core, first_start, tokens, first_gain, log_decay)
    came = ring_gather(normed_half, quarter)
    info = info[None]
    for index in range(shards.bit_length() - 1):
        moved = lax.ppermute(info, SEQ, [(i, i ^ (1 << index)) for i in range(shards)])
        upper = (place >> index) & 1 == 1
        info = jnp.concatenate([jnp.where(upper, moved, info), jnp.where(upper, info, moved)], axis=0)
    slot = ring_slots()
    lanes = jnp.arange(half)
    places = jnp.concatenate([core * half + lanes, (1 - core) * half + lanes]).astype(f32)[None]

    cotangent_half = of_rows(cotangent, core * half, half)
    cotangent_own = jnp.concatenate([cotangent_half, of_rows(cotangent, (1 - core) * half, half)], axis=0)
    cotangent_half = cotangent_half.astype(f32)
    token_half = of_rows(tokens, core * half, half).astype(f32)
    first_unit, first_inverse = norm_parts(token_half)

    def far_start(share):
        share = of_rows(share, chip * quarter, quarter)
        return [lax.ppermute(share, SEQ, hop) for hop in far_hops()]

    def far_parts(came):
        parts = []
        for item in came:
            both = [item, lax.ppermute(item, HEAD, ACROSS)]
            parts += both + [other_core(part) for part in both]
        return parts

    cotangent_far = far_start(after(0.5 * cotangent_half, came[-1][0]))
    cotangent_far = far_parts(cotangent_far)
    cotangent_far = round_rows(cotangent_far)

    in_slab, *queries_keys, values, gate_pre = over_steps(
        [normed_own],
        came,
        [[step] for step in range(shards // 2)],
        [query_weight, key_weight, value_weight, gate_weight],
        [2, 2, 1, 1],
        [1.0, key_scale, 1.0, 1.0],
        False,
    )
    normed, gated, *held = retain_forward(slot, info, places, queries_keys, values, gate_pre)

    out_mine, out_other = rows_sum([gated], [output_weight], shards - 2, rows, False)
    residual = token_half + head_total(out_mine, out_other)
    mid_unit, mid_inverse = norm_parts(residual)
    normed_mid_half = 0.5 * (mid_unit * second_gain)
    normed_mid_own = narrow(jnp.concatenate([normed_mid_half, other_core(normed_mid_half)], axis=0))
    mid_far = far_start(normed_mid_half)

    def hidden_mix(pre_gate, up_branch):
        return jax.nn.gelu(pre_gate, approximate=False) * up_branch

    def feed_forward(normed, grad_hidden):
        up_gate = matmul(normed, gelu_weight)
        up_proj = matmul(normed, linear_weight)
        hidden, back = jax.vjp(hidden_mix, up_gate, up_proj)
        grad_up_gate, grad_up = back(grad_hidden)
        return hidden.astype(bf16), grad_up_gate.astype(bf16), grad_up.astype(bf16)

    hidden, grad_up_gate, grad_up = feed_forward(normed_mid_own, transpose_right(cotangent_own, down_weight))

    mid_mine, mid_other = rows_sum([grad_up_gate, grad_up], [gelu_weight, linear_weight], 0, rows, True)
    grad_mid = head_total(mid_mine, mid_other)
    grad_residual = cotangent_half + norm_grad(grad_mid, second_gain, mid_unit, mid_inverse)
    second_part = 0.5 * jnp.sum(grad_mid * mid_unit, axis=0)
    branch_came = ring_gather(grad_residual, quarter)
    steps = list(range(shards // 2))
    branch_slab, grad_gated = over_steps(
        [grad_residual, other_core(grad_residual)],
        branch_came,
        [steps[:2]] + [[step] for step in steps[2:]] if shards > 4 else [[step] for step in steps],
        [output_weight],
        [1],
        [1.0],
        True,
    )

    mid_far = far_parts(mid_far)
    grad_hidden_far = transpose_right(cotangent_far, down_weight)
    normed_mid_far = round_rows(mid_far)
    hidden_far, grad_up_gate_far, grad_up_far = feed_forward(normed_mid_far, grad_hidden_far)

    res_mine, res_other = rows_sum([hidden], [down_weight], 0, rows, False)
    hidden_total = head_total(res_mine, res_other)

    def pair_slab(a):
        return lax.dynamic_slice_in_dim(a, shard // 2 * (2 * slab), 2 * slab, 1)

    def pair_sum(left, right, left_far, right_far, dim):
        found = transpose_left(left, right)
        found = found + transpose_left(left_far, right_far)
        kept = lax.dynamic_slice_in_dim(found, shard % 2 * slab, slab, dim)
        sent = lax.dynamic_slice_in_dim(found, (1 - shard % 2) * slab, slab, dim)
        sent = lax.ppermute(after(sent, branch_came[-1][0]), SEQ, [(i, i ^ 1) for i in range(shards)])
        return kept + sent

    mid_slab, mid_slab_far = pair_slab(normed_mid_own), pair_slab(normed_mid_far)
    wgrad_down = pair_sum(hidden, pair_slab(cotangent_own), hidden_far, pair_slab(cotangent_far), 1)
    wgrad_gelu = pair_sum(mid_slab, grad_up_gate, mid_slab_far, grad_up_gate_far, 0)
    wgrad_linear = pair_sum(mid_slab, grad_up, mid_slab_far, grad_up_far, 0)

    wgrad_output = transpose_left(gated, branch_slab)
    grad_queries, grad_keys, grad_values, grad_gate_pre = retain_backward(
        slot, queries_keys[::2], values, gate_pre, normed, held, grad_gated
    )

    in_mine, in_other = rows_sum(
        [grad_queries, grad_keys, grad_values, grad_gate_pre],
        [query_weight, key_weight, value_weight, gate_weight],
        shards - 2,
        rows,
        True,
    )
    result = 0.5 * (after(residual, in_mine) + hidden_total)
    output_rows = narrow(in_order(result, other_core(result)))
    grad_in = head_total(in_mine, in_other)
    wgrad_query = transpose_left(in_slab, grad_queries)
    wgrad_key = transpose_left(in_slab, grad_keys)
    wgrad_value = transpose_left(in_slab, grad_values)
    wgrad_gate = transpose_left(in_slab, grad_gate_pre)
    first_part = gain_part(core, tokens, in_mine, in_other)
    gains = exchange_sum(jnp.concatenate([first_part, second_part[None]]), SEQ)
    gains = gains + other_core(gains)
    grad_half = 0.5 * (grad_residual + norm_grad(grad_in, first_gain, first_unit, first_inverse))
    grad_tokens = narrow(in_order(grad_half, other_core(grad_half)))
    gains = after(gains, grad_in)
    gains = slab_of(gains + lax.ppermute(gains, HEAD, ACROSS), shard)
    return (
        output_rows,
        grad_tokens,
        gains[0],
        wgrad_query,
        wgrad_key,
        wgrad_value,
        wgrad_gate,
        wgrad_output,
        gains[1],
        wgrad_gelu,
        wgrad_linear,
        wgrad_down,
    )


def local(*arrays):
    tokens = lax.axis_size(SEQ) * arrays[0].shape[0]
    columns = sum(w.shape[1] for w in (*arrays[2:6], *arrays[8:10])) + arrays[6].shape[0] + arrays[10].shape[0]
    shards, groups = lax.axis_size(SEQ), lax.axis_size(HEAD)
    if groups == 4 and shards in (4, 8, 16) and arrays[0].shape[0] == BLK and 4 * tokens <= groups * columns:
        return local_gather(*arrays)
    return local_scatter(*arrays)


def solution(mesh):
    return jax.shard_map(
        local,
        mesh=mesh,
        in_specs=(
            P(SEQ, None),
            P(),
            P(None, HEAD),
            P(None, HEAD),
            P(None, HEAD),
            P(None, HEAD),
            P(HEAD, None),
            P(),
            P(None, HEAD),
            P(None, HEAD),
            P(HEAD, None),
            P(HEAD, SEQ),
            P(SEQ),
            P(SEQ, None),
        ),
        out_specs=(
            P(SEQ, None),
            P(SEQ, None),
            P(SEQ),
            P(SEQ, HEAD),
            P(SEQ, HEAD),
            P(SEQ, HEAD),
            P(SEQ, HEAD),
            P(HEAD, SEQ),
            P(SEQ),
            P(SEQ, HEAD),
            P(SEQ, HEAD),
            P(HEAD, SEQ),
        ),
        check_vma=False,
    )
```

```python
import functools
import math

import jax
import jax.numpy as jnp
from jax import lax
from jax.experimental import pallas as pl
from jax.experimental.pallas import tpu as pltpu
from jax.sharding import PartitionSpec as P


SEQ = "seq"
HEAD = "head"
DK = 256
DV = 512
BLK = 256


maximum_precision = lax.Precision.HIGHEST
eps_norm = 1e-05


def carried_in(part, axis, combine, identity, reverse):
    count = lax.axis_size(axis)
    place = lax.axis_index(axis)
    ahead = count - 1 - place if reverse else place
    gathered = jax.tree.map(lambda a: lax.all_gather(a, axis), part)
    state = jax.tree.map(lambda a, e: jnp.zeros_like(a) + jnp.asarray(e, a.dtype), part, identity)

    def one(hop, state):
        source = count - 1 - hop if reverse else hop
        return combine(
            state, jax.tree.map(lambda a: lax.dynamic_index_in_dim(a, source, 0, False), gathered)
        )

    return lax.fori_loop(0, ahead, one, state)


def matmul(left_side, right_side):
    return jnp.dot(left_side, right_side, preferred_element_type=jnp.float32)


def transpose_left(left_side, right_side):
    return lax.dot_general(
        left_side, right_side, (((0,), (0,)), ((), ())), preferred_element_type=jnp.float32
    )


def transpose_right(left_side, right_side):
    return lax.dot_general(
        left_side, right_side, (((1,), (1,)), ((), ())), preferred_element_type=jnp.float32
    )


def layer_norm(activity, gain_row):
    centre = jnp.mean(activity, axis=-1, keepdims=True)
    centred = activity - centre
    spread = jnp.mean(centred * centred, axis=-1, keepdims=True)
    return centred * lax.rsqrt(spread + eps_norm) * gain_row


def group_norm(activity):
    centre = jnp.mean(activity, axis=-1, keepdims=True)
    centred = activity - centre
    spread = jnp.mean(centred * centred, axis=-1, keepdims=True)
    return centred * lax.rsqrt(spread + eps_norm)


def retain_block(carried, query_slice, key_slice, value_slice, rate_part, flag_part):
    cumulative = jnp.cumsum(rate_part, axis=1)
    started = jnp.cumsum(flag_part)
    block_len = flag_part.shape[0]
    position = jnp.arange(block_len)
    causal_same = (started[:, None] == started[None, :]) & (position[:, None] >= position[None, :])
    log_gap = cumulative[:, :, None] - cumulative[:, None, :]
    weight_matrix = jnp.where(
        causal_same[None], jnp.exp(jnp.where(causal_same[None], log_gap, 0.0)), 0.0
    )
    attention_scores = (
        jnp.einsum("keu,reu->ekr", query_slice, key_slice, precision=maximum_precision)
        * weight_matrix
    )
    within = jnp.einsum("hnm,mhe->nhe", attention_scores, value_slice, precision=maximum_precision)
    before = (started == 0).astype(jnp.float32)
    reach_in = jnp.exp(cumulative) * before[None, :]
    across = jnp.einsum(
        "nhd,hde->nhe", query_slice * reach_in.T[:, :, None], carried, precision=maximum_precision
    )
    last_count = started[-1]
    trailing_weight = (
        jnp.exp(cumulative[:, -1:] - cumulative)
        * (started == last_count).astype(jnp.float32)[None, :]
    )
    keep_factor = jnp.exp(cumulative[:, -1]) * (last_count == 0).astype(jnp.float32)
    zeroed_state = jnp.einsum(
        "ygc,ygs->gcs",
        key_slice * trailing_weight.T[:, :, None],
        value_slice,
        precision=maximum_precision,
    )
    return (keep_factor[:, None, None] * carried + zeroed_state, within + across)


def retain(queries, key_heads, value_heads, log_rates, start_flag, initial):
    block_count = queries.shape[0] // BLK
    head_count = queries.shape[1]
    query_blocks = queries.reshape(block_count, BLK, head_count, queries.shape[2])
    key_blocks = key_heads.reshape(block_count, BLK, head_count, key_heads.shape[2])
    value_blocks = value_heads.reshape(block_count, BLK, head_count, value_heads.shape[2])
    rate_blocks = log_rates.reshape(head_count, block_count, BLK).transpose(1, 0, 2)
    flag_blocks = start_flag.reshape(block_count, BLK)

    def scan_step(carried, block_items):
        return retain_block(carried, *block_items)

    final_state, block_outputs = lax.scan(
        jax.checkpoint(scan_step),
        initial,
        (query_blocks, key_blocks, value_blocks, rate_blocks, flag_blocks),
    )
    return (block_outputs.reshape(block_count * BLK, head_count, value_heads.shape[2]), final_state)


def link_maps(earlier, later):
    return (earlier[0] * later[0], later[0][:, None, None] * earlier[1] + later[1])


def local_scatter(
    tokens,
    first_gain,
    query_weight,
    key_weight,
    value_weight,
    gate_weight,
    output_weight,
    second_gain,
    gelu_weight,
    linear_weight,
    down_weight,
    log_decay,
    first_start,
    cotangent,
):
    token_rows = tokens.shape[0]
    head_count = query_weight.shape[1] // DK
    key_scale = 1.0 / math.sqrt(DK)
    position = jnp.arange(token_rows, dtype=jnp.int32)
    start_flag = (position == first_start[0]).astype(jnp.float32)
    before = (position < first_start[0]).astype(jnp.float32)
    reach_in = jnp.exp(jnp.cumsum(log_decay, axis=1)) * before[None, :]
    shard_keep = jnp.exp(jnp.sum(log_decay, axis=1)) * (first_start[0] == token_rows).astype(
        jnp.float32
    )
    empty_state = jnp.zeros((head_count, DK, DV), jnp.float32)
    inputs = tokens.astype(jnp.float32)
    normed_in = layer_norm(inputs, first_gain).astype(jnp.bfloat16)
    queries = matmul(normed_in, query_weight)
    scaled_keys = matmul(normed_in, key_weight) * key_scale
    values = matmul(normed_in, value_weight)
    gate_pre = matmul(normed_in, gate_weight)
    query_heads = queries.reshape(token_rows, head_count, DK)
    key_heads = scaled_keys.reshape(token_rows, head_count, DK)
    value_heads = values.reshape(token_rows, head_count, DV)
    local_out, local_end = retain(
        query_heads, key_heads, value_heads, log_decay, start_flag, empty_state
    )
    weighted_query = query_heads * reach_in.T[:, :, None]
    incoming = carried_in(
        (shard_keep, local_end), SEQ, link_maps, (jnp.ones_like(shard_keep), empty_state), False
    )[1]
    retained = local_out + jnp.einsum(
        "nhd,hde->nhe", weighted_query, incoming, precision=maximum_precision
    )

    def gate_mix(gate_in, retained_in):
        return jax.nn.silu(gate_in) * group_norm(retained_in).reshape(token_rows, head_count * DV)

    gated_rows = gate_mix(gate_pre, retained).astype(jnp.bfloat16)
    residual = inputs + lax.psum(matmul(gated_rows, output_weight), HEAD)
    normed_mid = layer_norm(residual, second_gain).astype(jnp.bfloat16)
    up_gate = matmul(normed_mid, gelu_weight)
    up_proj = matmul(normed_mid, linear_weight)

    def hidden_mix(pre_gate, up_branch):
        return jax.nn.gelu(pre_gate, approximate=False) * up_branch

    hidden = hidden_mix(up_gate, up_proj).astype(jnp.bfloat16)
    result = residual + lax.psum(matmul(hidden, down_weight), HEAD)
    output_rows = result.astype(jnp.bfloat16)
    grad_hidden = transpose_right(cotangent, down_weight)
    wgrad_down = transpose_left(hidden, cotangent)
    _, hidden_back = jax.vjp(hidden_mix, up_gate, up_proj)
    grad_up_gate, grad_up = hidden_back(grad_hidden)
    grad_up_gate = grad_up_gate.astype(jnp.bfloat16)
    grad_up = grad_up.astype(jnp.bfloat16)
    grad_mid_in = lax.psum(
        transpose_right(grad_up_gate, gelu_weight) + transpose_right(grad_up, linear_weight), HEAD
    )
    wgrad_gelu = transpose_left(normed_mid, grad_up_gate)
    wgrad_linear = transpose_left(normed_mid, grad_up)
    _, second_back = jax.vjp(layer_norm, residual, second_gain)
    grad_mid_norm, wgrad_second = second_back(grad_mid_in)
    grad_residual = cotangent.astype(jnp.float32) + grad_mid_norm
    grad_branch = grad_residual.astype(jnp.bfloat16)
    grad_gated = transpose_right(grad_branch, output_weight)
    wgrad_output = transpose_left(gated_rows, grad_branch)
    _, gate_back = jax.vjp(gate_mix, gate_pre, retained)
    grad_gate_pre, grad_retained = gate_back(grad_gated)
    grad_gate_pre = grad_gate_pre.astype(jnp.bfloat16)
    local_in = jnp.einsum(
        "nhd,nhe->hde", weighted_query, grad_retained, precision=maximum_precision
    )
    beyond = carried_in(
        (shard_keep, local_in), SEQ, link_maps, (jnp.ones_like(shard_keep), empty_state), True
    )[1]

    def local_retain(query_in, key_in, value_in):
        return retain(query_in, key_in, value_in, log_decay, start_flag, incoming)

    _, retain_back = jax.vjp(local_retain, query_heads, key_heads, value_heads)
    grad_q, grad_k, grad_v = retain_back((grad_retained, beyond))
    grad_queries = grad_q.reshape(token_rows, head_count * DK).astype(jnp.bfloat16)
    grad_keys = (grad_k * key_scale).reshape(token_rows, head_count * DK).astype(jnp.bfloat16)
    grad_values = grad_v.reshape(token_rows, head_count * DV).astype(jnp.bfloat16)
    grad_in = lax.psum(
        transpose_right(grad_queries, query_weight)
        + transpose_right(grad_keys, key_weight)
        + transpose_right(grad_values, value_weight)
        + transpose_right(grad_gate_pre, gate_weight),
        HEAD,
    )
    wgrad_query = transpose_left(normed_in, grad_queries)
    wgrad_key = transpose_left(normed_in, grad_keys)
    wgrad_value = transpose_left(normed_in, grad_values)
    wgrad_gate = transpose_left(normed_in, grad_gate_pre)
    _, first_back = jax.vjp(layer_norm, inputs, first_gain)
    grad_in_norm, wgrad_first = first_back(grad_in)
    grad_tokens = (grad_residual + grad_in_norm).astype(jnp.bfloat16)
    summed = tuple(
        (
            lax.psum_scatter(wgrad_first, SEQ, scatter_dimension=0, tiled=True),
            lax.psum_scatter(wgrad_query, SEQ, scatter_dimension=0, tiled=True),
            lax.psum_scatter(wgrad_key, SEQ, scatter_dimension=0, tiled=True),
            lax.psum_scatter(wgrad_value, SEQ, scatter_dimension=0, tiled=True),
            lax.psum_scatter(wgrad_gate, SEQ, scatter_dimension=0, tiled=True),
            lax.psum_scatter(wgrad_output, SEQ, scatter_dimension=1, tiled=True),
            lax.psum_scatter(wgrad_second, SEQ, scatter_dimension=0, tiled=True),
            lax.psum_scatter(wgrad_gelu, SEQ, scatter_dimension=0, tiled=True),
            lax.psum_scatter(wgrad_linear, SEQ, scatter_dimension=0, tiled=True),
            lax.psum_scatter(wgrad_down, SEQ, scatter_dimension=1, tiled=True),
        )
    )
    return (output_rows, grad_tokens) + summed


def exchange_sum(rows, axis):
    count = lax.axis_size(axis)
    bit = count // 2
    while bit:
        rows = rows + lax.ppermute(rows, axis, [(i, i ^ bit) for i in range(count)])
        bit //= 2
    return rows


CHIP = [(0, 1), (1, 0), (2, 3), (3, 2)]
ACROSS = [(0, 2), (2, 0), (1, 3), (3, 1)]


def of_rows(a, start, size):
    return lax.dynamic_slice_in_dim(a, start, size, 0)


def after(a, *others):
    return lax.optimization_barrier((a, *others))[0]


def head_total(mine, other):
    other = lax.ppermute(other, HEAD, CHIP)
    both = mine + other
    return both + lax.ppermute(both, HEAD, ACROSS)


def other_core(a):
    return lax.ppermute(a, HEAD, CHIP)


def ring_order(count):
    return list(range(0, count, 2)) + list(range(count - 1, 0, -2))


def ring_gather(pieces):
    count = lax.axis_size(SEQ)
    order = ring_order(count)
    up = [(order[i], order[(i + 1) % count]) for i in range(count)]
    down = [(target, source) for source, target in up]
    steps = []
    rising, falling = list(pieces), list(pieces)
    for hop in range(1, count // 2 + 1):
        last = hop == count // 2
        if last and len(pieces) == 1:
            middle = pieces[0].shape[0] // 2
            rising, falling = [rising[0][:middle], None], [None, falling[0][middle:]]
        for part in range(len(rising)):
            rising[part] = None if last and part else lax.ppermute(rising[part], SEQ, up)
            falling[part] = None if last and not part else lax.ppermute(falling[part], SEQ, down)
        if last:
            came = [rising[0], falling[1]]
            steps.append(came + [other_core(part) for part in came])
        else:
            steps.append(
                rising + [other_core(part) for part in rising] + falling + [other_core(part) for part in falling]
            )
    return steps


def ring_slots():
    count = lax.axis_size(SEQ)
    index = jnp.arange(count, dtype=jnp.int32)

    def position(shard):
        return jnp.where(shard % 2 == 0, shard // 2, count - 1 - shard // 2)

    behind = (position(lax.axis_index(SEQ).astype(jnp.int32)) - position(index)) % count
    steps = jnp.where(behind < count // 2, 2 * behind - 2, 2 * (count - behind) - 1)
    return jnp.where(behind == 0, count - 2, jnp.where(behind == count // 2, count - 1, steps))


def dot_nt(left, right):
    return lax.dot_general(left, right, (((1,), (1,)), ((), ())), preferred_element_type=jnp.float32)


def dot_tn(left, right):
    return lax.dot_general(left, right, (((0,), (0,)), ((), ())), preferred_element_type=jnp.float32)


def dot_nn(left, right):
    return lax.dot_general(left, right, (((1,), (0,)), ((), ())), preferred_element_type=jnp.float32)


def half_split_dot(left, right, dot):
    left_high = left.astype(jnp.bfloat16)
    left_low = (left - left_high.astype(jnp.float32)).astype(jnp.bfloat16)
    return dot(left_high, right) + dot(left_low, right)


def norm_parts(retained):
    centre = jnp.mean(retained, axis=-1, keepdims=True)
    centred = retained - centre
    inverse = lax.rsqrt(jnp.mean(centred * centred, axis=-1, keepdims=True) + eps_norm)
    return centred * inverse, inverse


def norm_start_kernel(core_ref, first_ref, tokens_ref, gain_ref, rates_ref, normed_ref, first_half_ref, second_half_ref, info_ref):
    half = tokens_ref.shape[0] // 2
    for index, core in enumerate((core_ref[0], 1 - core_ref[0])):
        rows = tokens_ref[pl.ds(pl.multiple_of(core * half, half), half), :].astype(jnp.float32)
        normed = (norm_parts(rows)[0] * gain_ref[...]).astype(jnp.bfloat16)
        normed_ref[index * half : (index + 1) * half, :] = normed
        if index == 0:
            part = first_half_ref.shape[0]
            first_half_ref[...] = normed[:part].astype(jnp.float32)
            second_half_ref[...] = normed[part:].astype(jnp.float32)
    heads, size = rates_ref.shape
    info_ref[...] = jnp.full(info_ref.shape, first_ref[0], jnp.int32).astype(jnp.float32)
    for head in range(heads):
        info_ref[0:1, head * size : (head + 1) * size] = rates_ref[head : head + 1, :]


def norm_start(core, first_start, tokens, gain, log_decay):
    rows, width = tokens.shape
    vmem, smem = pl.BlockSpec(memory_space=pltpu.VMEM), pl.BlockSpec(memory_space=pltpu.SMEM)
    return pl.pallas_call(
        norm_start_kernel,
        in_specs=[smem, smem, vmem, vmem, vmem],
        out_specs=[vmem] * 4,
        out_shape=[
            jax.ShapeDtypeStruct((rows, width), jnp.bfloat16),
            jax.ShapeDtypeStruct((rows // 4, width), jnp.float32),
            jax.ShapeDtypeStruct((rows // 4, width), jnp.float32),
            jax.ShapeDtypeStruct((8, log_decay.size), jnp.float32),
        ],
        compiler_params=pltpu.CompilerParams(vmem_limit_bytes=10 << 20),
        name="norm_start",
    )(core[None], first_start, tokens, gain[None], log_decay)


def gain_part_kernel(core_ref, tokens_ref, mine_ref, other_ref, out_ref):
    half = mine_ref.shape[0]
    total = jnp.zeros(out_ref.shape, jnp.float32)
    for grad_ref, core in ((mine_ref, core_ref[0]), (other_ref, 1 - core_ref[0])):
        rows = tokens_ref[pl.ds(pl.multiple_of(core * half, half), half), :].astype(jnp.float32)
        total = total + jnp.sum(grad_ref[...] * norm_parts(rows)[0], axis=0, keepdims=True)
    out_ref[...] = total


def gain_part(core, tokens, mine, other):
    vmem, smem = pl.BlockSpec(memory_space=pltpu.VMEM), pl.BlockSpec(memory_space=pltpu.SMEM)
    return pl.pallas_call(
        gain_part_kernel,
        in_specs=[smem, vmem, vmem, vmem],
        out_specs=vmem,
        out_shape=jax.ShapeDtypeStruct((1, tokens.shape[1]), jnp.float32),
        cost_estimate=pl.CostEstimate(flops=10 * tokens.size, bytes_accessed=6 * tokens.size, transcendentals=0),
        compiler_params=pltpu.CompilerParams(vmem_limit_bytes=10 << 20),
        name="gain_part",
    )(core[None], tokens, mine, other)


def rows_product_kernel(parts, size, pieces, scales, tile, turned, block, shard_ref, *refs):
    weights = len(pieces)
    results = 1 + sum(pieces)
    part_refs, weight_refs = refs[:parts], refs[parts : parts + weights]
    scratch = refs[len(refs) - 2 * results - parts - weights - 3 :]
    outs, staged, scratch = scratch[:results], scratch[results : 2 * results], scratch[2 * results :]
    held, kept, x, read, written = scratch[:parts], scratch[parts : parts + weights], *scratch[parts + weights :]
    rows = x.shape[0]
    slab = staged[0].shape[1]
    loads = []

    def load(source, target):
        copy = pltpu.make_async_copy(source, target, read.at[len(loads)])
        copy.start()
        loads.append(copy)
        return copy

    arrive = [load(part.at[pl.ds(0, size), :], target) for part, target in zip(part_refs, held)]
    ready = []
    for weight, target in zip(weight_refs, kept):
        for start in range(0, weight.shape[0 if turned else 1], tile):
            at = pl.ds(start, tile)
            if turned:
                ready.append(load(weight.at[at, :], target.at[at, :]))
            else:
                ready.append(load(weight.at[:, at], target.at[:, at]))
    for index, copy in enumerate(arrive):
        copy.wait()
        at = slice(index * size, (index + 1) * size)
        x[at, :] = held[index][...].astype(jnp.bfloat16)
        column = pl.ds(pl.multiple_of(shard_ref[0] * slab, slab), slab)
        staged[0][at, :] = held[index][:, column].astype(jnp.bfloat16)
    stores = []

    def store(index, column):
        target = outs[index].at[pl.ds(block * rows, rows), column]
        copy = pltpu.make_async_copy(staged[index].at[:, column], target, written.at[len(stores)])
        copy.start()
        stores.append(copy)

    store(0, pl.ds(0, slab))
    result, number = 1, 0
    for weight, count, scale in zip(kept, pieces, scales):
        for start in range(0, weight.shape[0 if turned else 1], tile):
            at = slice(start, start + tile)
            ready[number].wait()
            number += 1
            found = dot_nt(x[...], weight[at, :]) if turned else dot_nn(x[...], weight[:, at])
            if scale != 1.0:
                found = found * scale
            high = found.astype(jnp.bfloat16)
            staged[result][:, at] = high
            store(result, pl.ds(start, tile))
            if count == 2:
                staged[result + 1][:, at] = (found - high.astype(jnp.float32)).astype(jnp.bfloat16)
                store(result + 1, pl.ds(start, tile))
        result += count
    for copy in stores:
        copy.wait()


def rows_product(parts, size, weights, pieces, scales, turned, shard, block, total, buffers=None):
    count, width = len(parts), parts[0].shape[1]
    rows = count * size
    tile = 512
    columns = [w.shape[0] if turned else w.shape[1] for w in weights]
    slab = width // lax.axis_size(SEQ)
    widths = [slab] + [c for c, results in zip(columns, pieces) for _ in range(results)]
    operands = [*parts, *weights]
    aliases = {}
    if buffers is not None:
        aliases = {1 + len(operands) + i: i for i in range(len(buffers))}
        operands += buffers
    anywhere = pl.BlockSpec(memory_space=pl.ANY)
    tiles = [c // tile for c in columns]
    return pl.pallas_call(
        functools.partial(rows_product_kernel, count, size, pieces, scales, tile, turned, block),
        grid_spec=pltpu.PrefetchScalarGridSpec(
            num_scalar_prefetch=1,
            grid=(1,),
            in_specs=[anywhere] * len(operands),
            out_specs=[anywhere] * len(widths),
            scratch_shapes=[pltpu.VMEM((rows, c), jnp.bfloat16) for c in widths]
            + [pltpu.VMEM((size, width), part.dtype) for part in parts]
            + [pltpu.VMEM(w.shape, w.dtype) for w in weights]
            + [
                pltpu.VMEM((rows, width), jnp.bfloat16),
                pltpu.SemaphoreType.DMA((count + sum(tiles),)),
                pltpu.SemaphoreType.DMA((1 + sum(a * b for a, b in zip(tiles, pieces)),)),
            ],
        ),
        out_shape=[jax.ShapeDtypeStruct((total, c), jnp.bfloat16) for c in widths],
        input_output_aliases=aliases,
        cost_estimate=pl.CostEstimate(
            flops=2 * rows * width * sum(columns),
            bytes_accessed=4 * rows * width + 2 * width * sum(columns) + 2 * rows * sum(columns),
            transcendentals=0,
        ),
        compiler_params=pltpu.CompilerParams(vmem_limit_bytes=(48 if turned else 52) << 20),
        name="rows_product",
    )(shard[None], *operands)


def rows_sum_kernel(number, tile, turned, *refs):
    rows_refs, weight_refs = refs[:number], refs[number : 2 * number]
    mine, other, total = refs[2 * number : 2 * number + 3]
    held, done = refs[2 * number + 3 : -1], refs[-1]
    pieces = []
    for rows, weight, kept in zip(rows_refs, weight_refs, held):
        for start in range(0, rows.shape[1], tile):
            at = pl.ds(start, tile)
            source, target = (weight.at[:, at], kept.at[:, at]) if turned else (weight.at[at, :], kept.at[at, :])
            copy = pltpu.make_async_copy(source, target, done.at[len(pieces)])
            copy.start()
            pieces.append((copy, rows, kept, slice(start, start + tile)))
    for index, (copy, rows, kept, at) in enumerate(pieces):
        copy.wait()
        if turned:
            found = dot_nt(rows[:, at], kept[:, at])
        else:
            found = dot_nn(rows[:, at], kept[at, :])
        total[...] = total[...] + found if index else found
    half = mine.shape[0]
    mine[...] = total[:half, :]
    other[...] = total[half:, :]


def rows_sum(arrays, weights, block, rows, turned):
    tile = 512
    width = weights[0].shape[0] if turned else weights[0].shape[1]
    half = pl.BlockSpec((rows // 2, width), lambda j: (0, 0))
    depth = sum(a.shape[1] for a in arrays)
    return pl.pallas_call(
        functools.partial(rows_sum_kernel, len(arrays), tile, turned),
        grid_spec=pltpu.PrefetchScalarGridSpec(
            num_scalar_prefetch=0,
            grid=(1,),
            in_specs=[pl.BlockSpec((rows, a.shape[1]), lambda j: (block, 0)) for a in arrays]
            + [pl.BlockSpec(memory_space=pl.ANY)] * len(weights),
            out_specs=[half, half],
            scratch_shapes=[pltpu.VMEM((rows, width), jnp.float32)]
            + [pltpu.VMEM(w.shape, w.dtype) for w in weights]
            + [pltpu.SemaphoreType.DMA((depth // tile,))],
        ),
        out_shape=[jax.ShapeDtypeStruct((rows // 2, width), jnp.float32)] * 2,
        cost_estimate=pl.CostEstimate(
            flops=2 * rows * width * depth,
            bytes_accessed=2 * (rows + width) * depth + 4 * rows * width,
            transcendentals=0,
        ),
        name="rows_sum",
    )(*arrays, *weights)


def round_rows_kernel(*refs):
    out = refs[-1]
    at = 0
    for part in refs[:-1]:
        size = part.shape[0]
        out[at : at + size, :] = (2.0 * part[...]).astype(jnp.bfloat16)
        at += size


def round_rows(parts):
    vmem = pl.BlockSpec(memory_space=pltpu.VMEM)
    rows, width = sum(part.shape[0] for part in parts), parts[0].shape[1]
    return pl.pallas_call(
        round_rows_kernel,
        in_specs=[vmem] * len(parts),
        out_specs=vmem,
        out_shape=jax.ShapeDtypeStruct((rows, width), jnp.bfloat16),
        cost_estimate=pl.CostEstimate(flops=rows * width, bytes_accessed=6 * rows * width, transcendentals=0),
        name="round_rows",
    )(*parts)


def causal(first, places):
    size = places.shape[1]
    column = jnp.broadcast_to(places, (size, size))
    row = column.T
    return (row >= column) & ((column >= first) | (row < first)), row


def block_decay(rates, first, seen, row):
    size = rates.shape[1]
    nth = lax.broadcasted_iota(jnp.int32, (size, size), 1).astype(jnp.float32)
    per_row = jnp.sum(jnp.where(nth <= row, rates, 0.0), axis=1, keepdims=True)
    down = jnp.broadcast_to(per_row, (size, size))
    weights = jnp.exp(jnp.where(seen, down - down.T, -jnp.inf))
    place = row[:, :1]
    last = jnp.sum(rates, axis=1, keepdims=True)
    whole = first >= size
    reach = jnp.where(place < first, jnp.exp(per_row), 0.0)
    trail = jnp.where((place >= first) | whole, jnp.exp(last - per_row), 0.0)
    keep = jnp.where(whole, jnp.exp(last), 0.0)
    return weights, reach, trail, keep


def head_lanes(head):
    return slice(head * DK, (head + 1) * DK), slice(head * DV, (head + 1) * DV), slice(head * BLK, (head + 1) * BLK)


def retain_forward_kernel(
    slot_ref, info_ref, places_ref, q_ref, q_rest_ref, k_ref, k_rest_ref, v_ref, gate_ref,
    normed_ref, gated_ref, state_ref, weights_ref, scores_ref, column_ref, state,
):
    @pl.when(pl.program_id(0) == 0)
    def _():
        state[...] = jnp.zeros_like(state)

    first = info_ref[0, 1:2, :1]
    seen, row = causal(first, places_ref[...])
    number = lax.broadcasted_iota(jnp.int32, column_ref.shape[2:], 1)
    for head in range(state.shape[0]):
        key, val, lane = head_lanes(head)
        weights, reach, trail, keep = block_decay(info_ref[0, 0:1, lane], first, seen, row)
        q, k, v = q_ref[:, key], k_ref[:, key], v_ref[:, val]
        held = state[head].astype(jnp.bfloat16)
        state_ref[head, 0] = held
        scores = dot_nt(q, k) + (dot_nt(q_rest_ref[:, key], k) + dot_nt(q, k_rest_ref[:, key]))
        scores = (scores * weights).astype(jnp.bfloat16)
        retained = dot_nn(scores, v) + reach * dot_nn(q, held)
        state[head] = keep * state[head] + dot_tn((k * trail).astype(jnp.bfloat16), v)
        normed, inverse = norm_parts(retained)
        gate = gate_ref[:, val].astype(jnp.float32)
        gated_ref[:, val] = (gate * jax.nn.sigmoid(gate) * normed).astype(jnp.bfloat16)
        normed_ref[:, val] = normed
        weights_ref[head, 0] = weights
        scores_ref[head, 0] = scores
        column_ref[head, 0] = jnp.where(
            number == 0, reach, jnp.where(number == 1, trail, jnp.where(number == 2, inverse, keep))
        )


def retain_backward_kernel(
    slot_ref, q_ref, k_ref, v_ref, gate_ref, normed_ref, state_ref, weights_ref, scores_ref, column_ref, up_ref,
    dq_ref, dk_ref, dv_ref, dgate_ref, beyond,
):
    @pl.when(pl.program_id(0) == 0)
    def _():
        beyond[...] = jnp.zeros_like(beyond)

    for head in range(beyond.shape[0]):
        key, val, _ = head_lanes(head)
        column = column_ref[head, 0]
        reach, trail, inverse, keep = column[:, 0:1], column[:, 1:2], column[:, 2:3], column[0:1, 3:4]
        weights, scores = weights_ref[head, 0], scores_ref[head, 0]
        q, k, v, normed = q_ref[:, key], k_ref[:, key], v_ref[:, val], normed_ref[:, val]
        gate, up = gate_ref[:, val].astype(jnp.float32), up_ref[:, val].astype(jnp.float32)
        sig = jax.nn.sigmoid(gate)
        silu = gate * sig
        dgate_ref[:, val] = (up * normed * (sig + silu * (1.0 - sig))).astype(jnp.bfloat16)
        g = up * silu
        mean_g = jnp.mean(g, axis=-1, keepdims=True)
        mean_gn = jnp.mean(g * normed, axis=-1, keepdims=True)
        grad = (g - mean_g - normed * mean_gn) * inverse
        after_block = beyond[head].astype(jnp.bfloat16)
        dscores = (half_split_dot(grad, v, dot_nt) * weights).astype(jnp.bfloat16)
        grad = grad.astype(jnp.bfloat16)
        q_reach = (q * reach).astype(jnp.bfloat16)
        dq_ref[:, key] = (dot_nn(dscores, k) + reach * dot_nt(grad, state_ref[head, 0])).astype(jnp.bfloat16)
        dk = dot_tn(dscores, q) + trail * dot_nt(v, after_block)
        dk_ref[:, key] = (dk * (1.0 / math.sqrt(DK))).astype(jnp.bfloat16)
        dv_ref[:, val] = (dot_tn(scores, grad) + trail * dot_nn(k, after_block)).astype(jnp.bfloat16)
        beyond[head] = keep * beyond[head] + dot_tn(q_reach, grad)


def retain_specs(heads, blocks, width, reverse):
    at = (lambda b: blocks - 1 - b) if reverse else (lambda b: b)
    info = pl.BlockSpec((1, 8, width), lambda b, slot: (at(b), 0, 0))
    places = pl.BlockSpec((1, BLK), lambda b, slot: (0, 0))
    key = pl.BlockSpec((BLK, heads * DK), lambda b, slot: (slot[at(b)], 0))
    val = pl.BlockSpec((BLK, heads * DV), lambda b, slot: (slot[at(b)], 0))
    held = [
        pl.BlockSpec((heads, 1, up, across), lambda b, slot: (0, at(b), 0, 0))
        for up, across in ((DK, DV), (BLK, BLK), (BLK, BLK), (BLK, 128))
    ]
    return info, places, key, val, held


def retain_forward(slot, info, places, queries_keys, v, gate):
    rows, heads = v.shape[0], v.shape[1] // DV
    blocks = rows // BLK
    info_at, places_at, key, val, held = retain_specs(heads, blocks, info.shape[2], False)
    return pl.pallas_call(
        retain_forward_kernel,
        grid_spec=pltpu.PrefetchScalarGridSpec(
            num_scalar_prefetch=1,
            grid=(blocks,),
            in_specs=[info_at, places_at, key, key, key, key, val, val],
            out_specs=[val, val, *held],
            scratch_shapes=[pltpu.VMEM((heads, DK, DV), jnp.float32)],
        ),
        out_shape=[
            jax.ShapeDtypeStruct((rows, heads * DV), jnp.float32),
            jax.ShapeDtypeStruct((rows, heads * DV), jnp.bfloat16),
            jax.ShapeDtypeStruct((heads, blocks, DK, DV), jnp.bfloat16),
            jax.ShapeDtypeStruct((heads, blocks, BLK, BLK), jnp.float32),
            jax.ShapeDtypeStruct((heads, blocks, BLK, BLK), jnp.bfloat16),
            jax.ShapeDtypeStruct((heads, blocks, BLK, 128), jnp.float32),
        ],
        cost_estimate=pl.CostEstimate(
            flops=2 * heads * rows * (BLK * (3 * DK + DV) + 2 * DK * DV),
            bytes_accessed=rows * heads * (8 * DK + 12 * DV),
            transcendentals=rows * heads * (BLK + DV),
        ),
        name="retain_forward",
    )(slot, info, places, *queries_keys, v, gate)


def retain_backward(slot, queries_keys, v, gate, normed, held, up):
    rows, heads = v.shape[0], v.shape[1] // DV
    blocks = rows // BLK
    _, _, key, val, held_at = retain_specs(heads, blocks, 0, True)
    return pl.pallas_call(
        retain_backward_kernel,
        grid_spec=pltpu.PrefetchScalarGridSpec(
            num_scalar_prefetch=1,
            grid=(blocks,),
            in_specs=[key, key, val, val, val, *held_at, val],
            out_specs=[key, key, val, val],
            scratch_shapes=[pltpu.VMEM((heads, DK, DV), jnp.float32)],
        ),
        out_shape=[
            jax.ShapeDtypeStruct((rows, heads * DK), jnp.bfloat16),
            jax.ShapeDtypeStruct((rows, heads * DK), jnp.bfloat16),
            jax.ShapeDtypeStruct((rows, heads * DV), jnp.bfloat16),
            jax.ShapeDtypeStruct((rows, heads * DV), jnp.bfloat16),
        ],
        cost_estimate=pl.CostEstimate(
            flops=2 * heads * rows * (BLK * (5 * DK + 3 * DV) + 4 * DK * DV),
            bytes_accessed=rows * heads * (12 * DK + 20 * DV),
            transcendentals=rows * heads * (BLK + DV),
        ),
        name="retain_backward",
    )(slot, *queries_keys, v, gate, normed, *held, up)


def norm_grad(grad, gain, centred_unit, inverse):
    e = grad * gain
    mean_e = jnp.mean(e, axis=-1, keepdims=True)
    mean_en = jnp.mean(e * centred_unit, axis=-1, keepdims=True)
    return (e - mean_e - centred_unit * mean_en) * inverse


def local_gather(
    tokens,
    first_gain,
    query_weight,
    key_weight,
    value_weight,
    gate_weight,
    output_weight,
    second_gain,
    gelu_weight,
    linear_weight,
    down_weight,
    log_decay,
    first_start,
    cotangent,
):
    bf16, f32 = jnp.bfloat16, jnp.float32
    shards = lax.axis_size(SEQ)
    shard, group = lax.axis_index(SEQ), lax.axis_index(HEAD)
    rows, width = tokens.shape
    half = rows // 2
    total = shards * rows
    quarter = half // 2
    slab = width // shards
    key_scale = 1.0 / math.sqrt(DK)
    chip, core = (group // 2).astype(jnp.int32), (group % 2).astype(jnp.int32)
    place = shard.astype(jnp.int32)

    def narrow(a):
        return (2.0 * a).astype(bf16)

    def slab_of(a, at):
        return lax.dynamic_slice_in_dim(a, at * slab, slab, 1)

    def in_order(mine, other):
        return jnp.where(core == 0, jnp.concatenate([mine, other]), jnp.concatenate([other, mine]))

    def far_hops():
        return [[(i, (i + hop) % shards) for i in range(shards)] for hop in range(2, shards, 2)]

    def over_steps(own_parts, steps, groups, weights, pieces, scales, turned):
        common = (weights, pieces, scales, turned, place)
        found = rows_product(own_parts, rows // len(own_parts), *common, shards - 2, total)
        for index, group in enumerate(groups):
            parts = [part for step in group for part in steps[step]]
            last = index + 1 == len(groups)
            block = shards - 1 if last else group[0] // len(group)
            found = rows_product(parts, parts[0].shape[0], *common, block, total, found)
        return found

    normed_own, *normed_half, info = norm_start(core, first_start, tokens, first_gain, log_decay)
    came = ring_gather(normed_half)
    info = info[None]
    for index in range(shards.bit_length() - 1):
        moved = lax.ppermute(info, SEQ, [(i, i ^ (1 << index)) for i in range(shards)])
        upper = (place >> index) & 1 == 1
        info = jnp.concatenate([jnp.where(upper, moved, info), jnp.where(upper, info, moved)], axis=0)
    slot = ring_slots()
    lanes = jnp.arange(half)
    places = jnp.concatenate([core * half + lanes, (1 - core) * half + lanes]).astype(f32)[None]

    cotangent_half = of_rows(cotangent, core * half, half)
    cotangent_own = jnp.concatenate([cotangent_half, of_rows(cotangent, (1 - core) * half, half)], axis=0)
    cotangent_half = cotangent_half.astype(f32)
    token_half = of_rows(tokens, core * half, half).astype(f32)
    first_unit, first_inverse = norm_parts(token_half)

    def far_start(share):
        share = of_rows(share, chip * quarter, quarter)
        return [lax.ppermute(share, SEQ, hop) for hop in far_hops()]

    def far_parts(came):
        parts = []
        for item in came:
            both = [item, lax.ppermute(item, HEAD, ACROSS)]
            parts += both + [other_core(part) for part in both]
        return parts

    cotangent_far = far_start(after(0.5 * cotangent_half, came[-1][1]))
    cotangent_far = far_parts(cotangent_far)
    cotangent_far = round_rows(cotangent_far)

    in_slab, *queries_keys, values, gate_pre = over_steps(
        [normed_own],
        came,
        [[step] for step in range(shards // 2)],
        [query_weight, key_weight, value_weight, gate_weight],
        [2, 2, 1, 1],
        [1.0, key_scale, 1.0, 1.0],
        False,
    )
    normed, gated, *held = retain_forward(slot, info, places, queries_keys, values, gate_pre)

    out_mine, out_other = rows_sum([gated], [output_weight], shards - 2, rows, False)
    residual = token_half + head_total(out_mine, out_other)
    mid_unit, mid_inverse = norm_parts(residual)
    normed_mid_half = 0.5 * (mid_unit * second_gain)
    normed_mid_own = narrow(jnp.concatenate([normed_mid_half, other_core(normed_mid_half)], axis=0))
    mid_far = far_start(normed_mid_half)

    def hidden_mix(pre_gate, up_branch):
        return jax.nn.gelu(pre_gate, approximate=False) * up_branch

    def feed_forward(normed, grad_hidden):
        up_gate = matmul(normed, gelu_weight)
        up_proj = matmul(normed, linear_weight)
        hidden, back = jax.vjp(hidden_mix, up_gate, up_proj)
        grad_up_gate, grad_up = back(grad_hidden)
        return hidden.astype(bf16), grad_up_gate.astype(bf16), grad_up.astype(bf16)

    hidden, grad_up_gate, grad_up = feed_forward(normed_mid_own, transpose_right(cotangent_own, down_weight))

    mid_mine, mid_other = rows_sum([grad_up_gate, grad_up], [gelu_weight, linear_weight], 0, rows, True)
    grad_mid = head_total(mid_mine, mid_other)
    grad_residual = cotangent_half + norm_grad(grad_mid, second_gain, mid_unit, mid_inverse)
    second_part = 0.5 * jnp.sum(grad_mid * mid_unit, axis=0)
    branch_came = ring_gather([grad_residual])
    steps = list(range(shards // 2))
    branch_slab, grad_gated = over_steps(
        [grad_residual, other_core(grad_residual)],
        branch_came,
        [steps[:2]] + [[step] for step in steps[2:]] if shards > 4 else [[step] for step in steps],
        [output_weight],
        [1],
        [1.0],
        True,
    )

    mid_far = far_parts(mid_far)
    grad_hidden_far = transpose_right(cotangent_far, down_weight)
    normed_mid_far = round_rows(mid_far)
    hidden_far, grad_up_gate_far, grad_up_far = feed_forward(normed_mid_far, grad_hidden_far)

    res_mine, res_other = rows_sum([hidden], [down_weight], 0, rows, False)
    hidden_total = head_total(res_mine, after(res_other, branch_came[0][0]))

    def pair_slab(a):
        return lax.dynamic_slice_in_dim(a, shard // 2 * (2 * slab), 2 * slab, 1)

    def pair_sum(left, right, left_far, right_far, dim):
        found = transpose_left(left, right)
        found = found + transpose_left(left_far, right_far)
        kept = lax.dynamic_slice_in_dim(found, shard % 2 * slab, slab, dim)
        sent = lax.dynamic_slice_in_dim(found, (1 - shard % 2) * slab, slab, dim)
        sent = lax.ppermute(after(sent, branch_came[-1][1]), SEQ, [(i, i ^ 1) for i in range(shards)])
        return kept + sent

    mid_slab, mid_slab_far = pair_slab(normed_mid_own), pair_slab(normed_mid_far)
    wgrad_down = pair_sum(hidden, pair_slab(cotangent_own), hidden_far, pair_slab(cotangent_far), 1)
    wgrad_gelu = pair_sum(mid_slab, grad_up_gate, mid_slab_far, grad_up_gate_far, 0)
    wgrad_linear = pair_sum(mid_slab, grad_up, mid_slab_far, grad_up_far, 0)

    wgrad_output = transpose_left(gated, branch_slab)
    grad_queries, grad_keys, grad_values, grad_gate_pre = retain_backward(
        slot, queries_keys[::2], values, gate_pre, normed, held, grad_gated
    )

    in_mine, in_other = rows_sum(
        [grad_queries, grad_keys, grad_values, grad_gate_pre],
        [query_weight, key_weight, value_weight, gate_weight],
        shards - 2,
        rows,
        True,
    )
    result = 0.5 * (after(residual, in_mine) + hidden_total)
    output_rows = narrow(in_order(result, other_core(result)))
    grad_in = head_total(in_mine, in_other)
    wgrad_query = transpose_left(in_slab, grad_queries)
    wgrad_key = transpose_left(in_slab, grad_keys)
    wgrad_value = transpose_left(in_slab, grad_values)
    wgrad_gate = transpose_left(in_slab, grad_gate_pre)
    first_part = gain_part(core, tokens, in_mine, in_other)
    gains = exchange_sum(jnp.concatenate([first_part, second_part[None]]), SEQ)
    gains = gains + other_core(gains)
    grad_half = 0.5 * (grad_residual + norm_grad(grad_in, first_gain, first_unit, first_inverse))
    other_half = other_core(grad_half)
    grad_tokens = narrow(in_order(grad_half, other_half))
    gains = gains + lax.ppermute(after(gains, grad_in), HEAD, ACROSS)
    gains = slab_of(gains, shard)
    return (
        output_rows,
        grad_tokens,
        gains[0],
        wgrad_query,
        wgrad_key,
        wgrad_value,
        wgrad_gate,
        wgrad_output,
        gains[1],
        wgrad_gelu,
        wgrad_linear,
        wgrad_down,
    )


def local(*arrays):
    tokens = lax.axis_size(SEQ) * arrays[0].shape[0]
    columns = sum(w.shape[1] for w in (*arrays[2:6], *arrays[8:10])) + arrays[6].shape[0] + arrays[10].shape[0]
    shards, groups = lax.axis_size(SEQ), lax.axis_size(HEAD)
    if groups == 4 and shards in (4, 8, 16) and arrays[0].shape[0] == BLK and 4 * tokens <= groups * columns:
        return local_gather(*arrays)
    return local_scatter(*arrays)


def solution(mesh):
    return jax.shard_map(
        local,
        mesh=mesh,
        in_specs=(
            P(SEQ, None),
            P(),
            P(None, HEAD),
            P(None, HEAD),
            P(None, HEAD),
            P(None, HEAD),
            P(HEAD, None),
            P(),
            P(None, HEAD),
            P(None, HEAD),
            P(HEAD, None),
            P(HEAD, SEQ),
            P(SEQ),
            P(SEQ, None),
        ),
        out_specs=(
            P(SEQ, None),
            P(SEQ, None),
            P(SEQ),
            P(SEQ, HEAD),
            P(SEQ, HEAD),
            P(SEQ, HEAD),
            P(SEQ, HEAD),
            P(HEAD, SEQ),
            P(SEQ),
            P(SEQ, HEAD),
            P(SEQ, HEAD),
            P(HEAD, SEQ),
        ),
        check_vma=False,
    )
```

```python
import functools
import math

import jax
import jax.numpy as jnp
from jax import lax
from jax.experimental import pallas as pl
from jax.experimental.pallas import tpu as pltpu
from jax.sharding import PartitionSpec as P


SEQ = "seq"
HEAD = "head"
DK = 256
DV = 512
BLK = 256


maximum_precision = lax.Precision.HIGHEST
eps_norm = 1e-05


def carried_in(part, axis, combine, identity, reverse):
    count = lax.axis_size(axis)
    place = lax.axis_index(axis)
    ahead = count - 1 - place if reverse else place
    gathered = jax.tree.map(lambda a: lax.all_gather(a, axis), part)
    state = jax.tree.map(lambda a, e: jnp.zeros_like(a) + jnp.asarray(e, a.dtype), part, identity)

    def one(hop, state):
        source = count - 1 - hop if reverse else hop
        return combine(
            state, jax.tree.map(lambda a: lax.dynamic_index_in_dim(a, source, 0, False), gathered)
        )

    return lax.fori_loop(0, ahead, one, state)


def matmul(left_side, right_side):
    return jnp.dot(left_side, right_side, preferred_element_type=jnp.float32)


def transpose_left(left_side, right_side):
    return lax.dot_general(
        left_side, right_side, (((0,), (0,)), ((), ())), preferred_element_type=jnp.float32
    )


def transpose_right(left_side, right_side):
    return lax.dot_general(
        left_side, right_side, (((1,), (1,)), ((), ())), preferred_element_type=jnp.float32
    )


def layer_norm(activity, gain_row):
    centre = jnp.mean(activity, axis=-1, keepdims=True)
    centred = activity - centre
    spread = jnp.mean(centred * centred, axis=-1, keepdims=True)
    return centred * lax.rsqrt(spread + eps_norm) * gain_row


def group_norm(activity):
    centre = jnp.mean(activity, axis=-1, keepdims=True)
    centred = activity - centre
    spread = jnp.mean(centred * centred, axis=-1, keepdims=True)
    return centred * lax.rsqrt(spread + eps_norm)


def retain_block(carried, query_slice, key_slice, value_slice, rate_part, flag_part):
    cumulative = jnp.cumsum(rate_part, axis=1)
    started = jnp.cumsum(flag_part)
    block_len = flag_part.shape[0]
    position = jnp.arange(block_len)
    causal_same = (started[:, None] == started[None, :]) & (position[:, None] >= position[None, :])
    log_gap = cumulative[:, :, None] - cumulative[:, None, :]
    weight_matrix = jnp.where(
        causal_same[None], jnp.exp(jnp.where(causal_same[None], log_gap, 0.0)), 0.0
    )
    attention_scores = (
        jnp.einsum("keu,reu->ekr", query_slice, key_slice, precision=maximum_precision)
        * weight_matrix
    )
    within = jnp.einsum("hnm,mhe->nhe", attention_scores, value_slice, precision=maximum_precision)
    before = (started == 0).astype(jnp.float32)
    reach_in = jnp.exp(cumulative) * before[None, :]
    across = jnp.einsum(
        "nhd,hde->nhe", query_slice * reach_in.T[:, :, None], carried, precision=maximum_precision
    )
    last_count = started[-1]
    trailing_weight = (
        jnp.exp(cumulative[:, -1:] - cumulative)
        * (started == last_count).astype(jnp.float32)[None, :]
    )
    keep_factor = jnp.exp(cumulative[:, -1]) * (last_count == 0).astype(jnp.float32)
    zeroed_state = jnp.einsum(
        "ygc,ygs->gcs",
        key_slice * trailing_weight.T[:, :, None],
        value_slice,
        precision=maximum_precision,
    )
    return (keep_factor[:, None, None] * carried + zeroed_state, within + across)


def retain(queries, key_heads, value_heads, log_rates, start_flag, initial):
    block_count = queries.shape[0] // BLK
    head_count = queries.shape[1]
    query_blocks = queries.reshape(block_count, BLK, head_count, queries.shape[2])
    key_blocks = key_heads.reshape(block_count, BLK, head_count, key_heads.shape[2])
    value_blocks = value_heads.reshape(block_count, BLK, head_count, value_heads.shape[2])
    rate_blocks = log_rates.reshape(head_count, block_count, BLK).transpose(1, 0, 2)
    flag_blocks = start_flag.reshape(block_count, BLK)

    def scan_step(carried, block_items):
        return retain_block(carried, *block_items)

    final_state, block_outputs = lax.scan(
        jax.checkpoint(scan_step),
        initial,
        (query_blocks, key_blocks, value_blocks, rate_blocks, flag_blocks),
    )
    return (block_outputs.reshape(block_count * BLK, head_count, value_heads.shape[2]), final_state)


def link_maps(earlier, later):
    return (earlier[0] * later[0], later[0][:, None, None] * earlier[1] + later[1])


def local_scatter(
    tokens,
    first_gain,
    query_weight,
    key_weight,
    value_weight,
    gate_weight,
    output_weight,
    second_gain,
    gelu_weight,
    linear_weight,
    down_weight,
    log_decay,
    first_start,
    cotangent,
):
    token_rows = tokens.shape[0]
    head_count = query_weight.shape[1] // DK
    key_scale = 1.0 / math.sqrt(DK)
    position = jnp.arange(token_rows, dtype=jnp.int32)
    start_flag = (position == first_start[0]).astype(jnp.float32)
    before = (position < first_start[0]).astype(jnp.float32)
    reach_in = jnp.exp(jnp.cumsum(log_decay, axis=1)) * before[None, :]
    shard_keep = jnp.exp(jnp.sum(log_decay, axis=1)) * (first_start[0] == token_rows).astype(
        jnp.float32
    )
    empty_state = jnp.zeros((head_count, DK, DV), jnp.float32)
    inputs = tokens.astype(jnp.float32)
    normed_in = layer_norm(inputs, first_gain).astype(jnp.bfloat16)
    queries = matmul(normed_in, query_weight)
    scaled_keys = matmul(normed_in, key_weight) * key_scale
    values = matmul(normed_in, value_weight)
    gate_pre = matmul(normed_in, gate_weight)
    query_heads = queries.reshape(token_rows, head_count, DK)
    key_heads = scaled_keys.reshape(token_rows, head_count, DK)
    value_heads = values.reshape(token_rows, head_count, DV)
    local_out, local_end = retain(
        query_heads, key_heads, value_heads, log_decay, start_flag, empty_state
    )
    weighted_query = query_heads * reach_in.T[:, :, None]
    incoming = carried_in(
        (shard_keep, local_end), SEQ, link_maps, (jnp.ones_like(shard_keep), empty_state), False
    )[1]
    retained = local_out + jnp.einsum(
        "nhd,hde->nhe", weighted_query, incoming, precision=maximum_precision
    )

    def gate_mix(gate_in, retained_in):
        return jax.nn.silu(gate_in) * group_norm(retained_in).reshape(token_rows, head_count * DV)

    gated_rows = gate_mix(gate_pre, retained).astype(jnp.bfloat16)
    residual = inputs + lax.psum(matmul(gated_rows, output_weight), HEAD)
    normed_mid = layer_norm(residual, second_gain).astype(jnp.bfloat16)
    up_gate = matmul(normed_mid, gelu_weight)
    up_proj = matmul(normed_mid, linear_weight)

    def hidden_mix(pre_gate, up_branch):
        return jax.nn.gelu(pre_gate, approximate=False) * up_branch

    hidden = hidden_mix(up_gate, up_proj).astype(jnp.bfloat16)
    result = residual + lax.psum(matmul(hidden, down_weight), HEAD)
    output_rows = result.astype(jnp.bfloat16)
    grad_hidden = transpose_right(cotangent, down_weight)
    wgrad_down = transpose_left(hidden, cotangent)
    _, hidden_back = jax.vjp(hidden_mix, up_gate, up_proj)
    grad_up_gate, grad_up = hidden_back(grad_hidden)
    grad_up_gate = grad_up_gate.astype(jnp.bfloat16)
    grad_up = grad_up.astype(jnp.bfloat16)
    grad_mid_in = lax.psum(
        transpose_right(grad_up_gate, gelu_weight) + transpose_right(grad_up, linear_weight), HEAD
    )
    wgrad_gelu = transpose_left(normed_mid, grad_up_gate)
    wgrad_linear = transpose_left(normed_mid, grad_up)
    _, second_back = jax.vjp(layer_norm, residual, second_gain)
    grad_mid_norm, wgrad_second = second_back(grad_mid_in)
    grad_residual = cotangent.astype(jnp.float32) + grad_mid_norm
    grad_branch = grad_residual.astype(jnp.bfloat16)
    grad_gated = transpose_right(grad_branch, output_weight)
    wgrad_output = transpose_left(gated_rows, grad_branch)
    _, gate_back = jax.vjp(gate_mix, gate_pre, retained)
    grad_gate_pre, grad_retained = gate_back(grad_gated)
    grad_gate_pre = grad_gate_pre.astype(jnp.bfloat16)
    local_in = jnp.einsum(
        "nhd,nhe->hde", weighted_query, grad_retained, precision=maximum_precision
    )
    beyond = carried_in(
        (shard_keep, local_in), SEQ, link_maps, (jnp.ones_like(shard_keep), empty_state), True
    )[1]

    def local_retain(query_in, key_in, value_in):
        return retain(query_in, key_in, value_in, log_decay, start_flag, incoming)

    _, retain_back = jax.vjp(local_retain, query_heads, key_heads, value_heads)
    grad_q, grad_k, grad_v = retain_back((grad_retained, beyond))
    grad_queries = grad_q.reshape(token_rows, head_count * DK).astype(jnp.bfloat16)
    grad_keys = (grad_k * key_scale).reshape(token_rows, head_count * DK).astype(jnp.bfloat16)
    grad_values = grad_v.reshape(token_rows, head_count * DV).astype(jnp.bfloat16)
    grad_in = lax.psum(
        transpose_right(grad_queries, query_weight)
        + transpose_right(grad_keys, key_weight)
        + transpose_right(grad_values, value_weight)
        + transpose_right(grad_gate_pre, gate_weight),
        HEAD,
    )
    wgrad_query = transpose_left(normed_in, grad_queries)
    wgrad_key = transpose_left(normed_in, grad_keys)
    wgrad_value = transpose_left(normed_in, grad_values)
    wgrad_gate = transpose_left(normed_in, grad_gate_pre)
    _, first_back = jax.vjp(layer_norm, inputs, first_gain)
    grad_in_norm, wgrad_first = first_back(grad_in)
    grad_tokens = (grad_residual + grad_in_norm).astype(jnp.bfloat16)
    summed = tuple(
        (
            lax.psum_scatter(wgrad_first, SEQ, scatter_dimension=0, tiled=True),
            lax.psum_scatter(wgrad_query, SEQ, scatter_dimension=0, tiled=True),
            lax.psum_scatter(wgrad_key, SEQ, scatter_dimension=0, tiled=True),
            lax.psum_scatter(wgrad_value, SEQ, scatter_dimension=0, tiled=True),
            lax.psum_scatter(wgrad_gate, SEQ, scatter_dimension=0, tiled=True),
            lax.psum_scatter(wgrad_output, SEQ, scatter_dimension=1, tiled=True),
            lax.psum_scatter(wgrad_second, SEQ, scatter_dimension=0, tiled=True),
            lax.psum_scatter(wgrad_gelu, SEQ, scatter_dimension=0, tiled=True),
            lax.psum_scatter(wgrad_linear, SEQ, scatter_dimension=0, tiled=True),
            lax.psum_scatter(wgrad_down, SEQ, scatter_dimension=1, tiled=True),
        )
    )
    return (output_rows, grad_tokens) + summed


def exchange_sum(rows, axis):
    count = lax.axis_size(axis)
    bit = count // 2
    while bit:
        rows = rows + lax.ppermute(rows, axis, [(i, i ^ bit) for i in range(count)])
        bit //= 2
    return rows


CHIP = [(0, 1), (1, 0), (2, 3), (3, 2)]
ACROSS = [(0, 2), (2, 0), (1, 3), (3, 1)]


def of_rows(a, start, size):
    return lax.dynamic_slice_in_dim(a, start, size, 0)


def after(a, *others):
    return lax.optimization_barrier((a, *others))[0]


def head_total(mine, other):
    other = lax.ppermute(other, HEAD, CHIP)
    both = mine + other
    return both + lax.ppermute(both, HEAD, ACROSS)


def other_core(a):
    return lax.ppermute(a, HEAD, CHIP)


def ring_order(count):
    return list(range(0, count, 2)) + list(range(count - 1, 0, -2))


def ring_gather(pieces):
    count = lax.axis_size(SEQ)
    order = ring_order(count)
    up = [(order[i], order[(i + 1) % count]) for i in range(count)]
    down = [(target, source) for source, target in up]
    steps = []
    rising, falling = list(pieces), list(pieces)
    for hop in range(1, count // 2 + 1):
        last = hop == count // 2
        if last and len(pieces) == 1:
            middle = pieces[0].shape[0] // 2
            rising, falling = [rising[0][:middle], None], [None, falling[0][middle:]]
        for part in range(len(rising)):
            rising[part] = None if last and part else lax.ppermute(rising[part], SEQ, up)
            falling[part] = None if last and not part else lax.ppermute(falling[part], SEQ, down)
        if last:
            came = [rising[0], falling[1]]
            steps.append(came + [other_core(part) for part in came])
        else:
            steps.append(
                rising + [other_core(part) for part in rising] + falling + [other_core(part) for part in falling]
            )
    return steps


def ring_slots():
    count = lax.axis_size(SEQ)
    index = jnp.arange(count, dtype=jnp.int32)

    def position(shard):
        return jnp.where(shard % 2 == 0, shard // 2, count - 1 - shard // 2)

    behind = (position(lax.axis_index(SEQ).astype(jnp.int32)) - position(index)) % count
    steps = jnp.where(behind < count // 2, 2 * behind - 2, 2 * (count - behind) - 1)
    return jnp.where(behind == 0, count - 2, jnp.where(behind == count // 2, count - 1, steps))


def dot_nt(left, right):
    return lax.dot_general(left, right, (((1,), (1,)), ((), ())), preferred_element_type=jnp.float32)


def dot_tn(left, right):
    return lax.dot_general(left, right, (((0,), (0,)), ((), ())), preferred_element_type=jnp.float32)


def dot_nn(left, right):
    return lax.dot_general(left, right, (((1,), (0,)), ((), ())), preferred_element_type=jnp.float32)


def half_split_dot(left, right, dot):
    left_high = left.astype(jnp.bfloat16)
    left_low = (left - left_high.astype(jnp.float32)).astype(jnp.bfloat16)
    return dot(left_high, right) + dot(left_low, right)


def norm_parts(retained):
    centre = jnp.mean(retained, axis=-1, keepdims=True)
    centred = retained - centre
    inverse = lax.rsqrt(jnp.mean(centred * centred, axis=-1, keepdims=True) + eps_norm)
    return centred * inverse, inverse


def norm_start_kernel(core_ref, first_ref, tokens_ref, gain_ref, rates_ref, normed_ref, first_half_ref, second_half_ref, info_ref):
    half = tokens_ref.shape[0] // 2
    for index, core in enumerate((core_ref[0], 1 - core_ref[0])):
        rows = tokens_ref[pl.ds(pl.multiple_of(core * half, half), half), :].astype(jnp.float32)
        normed = (norm_parts(rows)[0] * gain_ref[...]).astype(jnp.bfloat16)
        normed_ref[index * half : (index + 1) * half, :] = normed
        if index == 0:
            part = first_half_ref.shape[0]
            first_half_ref[...] = normed[:part].astype(jnp.float32)
            second_half_ref[...] = normed[part:].astype(jnp.float32)
    heads, size = rates_ref.shape
    info_ref[...] = jnp.full(info_ref.shape, first_ref[0], jnp.int32).astype(jnp.float32)
    for head in range(heads):
        info_ref[0:1, head * size : (head + 1) * size] = rates_ref[head : head + 1, :]


def norm_start(core, first_start, tokens, gain, log_decay):
    rows, width = tokens.shape
    vmem, smem = pl.BlockSpec(memory_space=pltpu.VMEM), pl.BlockSpec(memory_space=pltpu.SMEM)
    return pl.pallas_call(
        norm_start_kernel,
        in_specs=[smem, smem, vmem, vmem, vmem],
        out_specs=[vmem] * 4,
        out_shape=[
            jax.ShapeDtypeStruct((rows, width), jnp.bfloat16),
            jax.ShapeDtypeStruct((rows // 4, width), jnp.float32),
            jax.ShapeDtypeStruct((rows // 4, width), jnp.float32),
            jax.ShapeDtypeStruct((8, log_decay.size), jnp.float32),
        ],
        compiler_params=pltpu.CompilerParams(vmem_limit_bytes=10 << 20),
        name="norm_start",
    )(core[None], first_start, tokens, gain[None], log_decay)


def gain_part_kernel(core_ref, tokens_ref, mine_ref, other_ref, out_ref):
    half = mine_ref.shape[0]
    total = jnp.zeros(out_ref.shape, jnp.float32)
    for grad_ref, core in ((mine_ref, core_ref[0]), (other_ref, 1 - core_ref[0])):
        rows = tokens_ref[pl.ds(pl.multiple_of(core * half, half), half), :].astype(jnp.float32)
        total = total + jnp.sum(grad_ref[...] * norm_parts(rows)[0], axis=0, keepdims=True)
    out_ref[...] = total


def gain_part(core, tokens, mine, other):
    vmem, smem = pl.BlockSpec(memory_space=pltpu.VMEM), pl.BlockSpec(memory_space=pltpu.SMEM)
    return pl.pallas_call(
        gain_part_kernel,
        in_specs=[smem, vmem, vmem, vmem],
        out_specs=vmem,
        out_shape=jax.ShapeDtypeStruct((1, tokens.shape[1]), jnp.float32),
        cost_estimate=pl.CostEstimate(flops=10 * tokens.size, bytes_accessed=6 * tokens.size, transcendentals=0),
        compiler_params=pltpu.CompilerParams(vmem_limit_bytes=10 << 20),
        name="gain_part",
    )(core[None], tokens, mine, other)


def rows_product_kernel(parts, size, pieces, scales, tile, turned, block, shard_ref, *refs):
    weights = len(pieces)
    results = 1 + sum(pieces)
    part_refs, weight_refs = refs[:parts], refs[parts : parts + weights]
    scratch = refs[len(refs) - 2 * results - parts - weights - 3 :]
    outs, staged, scratch = scratch[:results], scratch[results : 2 * results], scratch[2 * results :]
    held, kept, x, read, written = scratch[:parts], scratch[parts : parts + weights], *scratch[parts + weights :]
    rows = x.shape[0]
    slab = staged[0].shape[1]
    loads = []

    def load(source, target):
        copy = pltpu.make_async_copy(source, target, read.at[len(loads)])
        copy.start()
        loads.append(copy)
        return copy

    arrive = [load(part.at[pl.ds(0, size), :], target) for part, target in zip(part_refs, held)]
    ready = []
    for weight, target in zip(weight_refs, kept):
        for start in range(0, weight.shape[0 if turned else 1], tile):
            at = pl.ds(start, tile)
            if turned:
                ready.append(load(weight.at[at, :], target.at[at, :]))
            else:
                ready.append(load(weight.at[:, at], target.at[:, at]))
    for index, copy in enumerate(arrive):
        copy.wait()
        at = slice(index * size, (index + 1) * size)
        x[at, :] = held[index][...].astype(jnp.bfloat16)
        column = pl.ds(pl.multiple_of(shard_ref[0] * slab, slab), slab)
        staged[0][at, :] = held[index][:, column].astype(jnp.bfloat16)
    stores = []

    def store(index, column):
        target = outs[index].at[pl.ds(block * rows, rows), column]
        copy = pltpu.make_async_copy(staged[index].at[:, column], target, written.at[len(stores)])
        copy.start()
        stores.append(copy)

    store(0, pl.ds(0, slab))
    result, number = 1, 0
    for weight, count, scale in zip(kept, pieces, scales):
        for start in range(0, weight.shape[0 if turned else 1], tile):
            at = slice(start, start + tile)
            ready[number].wait()
            number += 1
            found = dot_nt(x[...], weight[at, :]) if turned else dot_nn(x[...], weight[:, at])
            if scale != 1.0:
                found = found * scale
            high = found.astype(jnp.bfloat16)
            staged[result][:, at] = high
            store(result, pl.ds(start, tile))
            if count == 2:
                staged[result + 1][:, at] = (found - high.astype(jnp.float32)).astype(jnp.bfloat16)
                store(result + 1, pl.ds(start, tile))
        result += count
    for copy in stores:
        copy.wait()


def rows_product(parts, size, weights, pieces, scales, turned, shard, block, total, buffers=None):
    count, width = len(parts), parts[0].shape[1]
    rows = count * size
    tile = 512
    columns = [w.shape[0] if turned else w.shape[1] for w in weights]
    slab = width // lax.axis_size(SEQ)
    widths = [slab] + [c for c, results in zip(columns, pieces) for _ in range(results)]
    operands = [*parts, *weights]
    aliases = {}
    if buffers is not None:
        aliases = {1 + len(operands) + i: i for i in range(len(buffers))}
        operands += buffers
    anywhere = pl.BlockSpec(memory_space=pl.ANY)
    tiles = [c // tile for c in columns]
    return pl.pallas_call(
        functools.partial(rows_product_kernel, count, size, pieces, scales, tile, turned, block),
        grid_spec=pltpu.PrefetchScalarGridSpec(
            num_scalar_prefetch=1,
            grid=(1,),
            in_specs=[anywhere] * len(operands),
            out_specs=[anywhere] * len(widths),
            scratch_shapes=[pltpu.VMEM((rows, c), jnp.bfloat16) for c in widths]
            + [pltpu.VMEM((size, width), part.dtype) for part in parts]
            + [pltpu.VMEM(w.shape, w.dtype) for w in weights]
            + [
                pltpu.VMEM((rows, width), jnp.bfloat16),
                pltpu.SemaphoreType.DMA((count + sum(tiles),)),
                pltpu.SemaphoreType.DMA((1 + sum(a * b for a, b in zip(tiles, pieces)),)),
            ],
        ),
        out_shape=[jax.ShapeDtypeStruct((total, c), jnp.bfloat16) for c in widths],
        input_output_aliases=aliases,
        cost_estimate=pl.CostEstimate(
            flops=2 * rows * width * sum(columns),
            bytes_accessed=4 * rows * width + 2 * width * sum(columns) + 2 * rows * sum(columns),
            transcendentals=0,
        ),
        compiler_params=pltpu.CompilerParams(vmem_limit_bytes=(48 if turned else 52) << 20),
        name="rows_product",
    )(shard[None], *operands)


def rows_sum_kernel(number, tile, turned, *refs):
    rows_refs, weight_refs = refs[:number], refs[number : 2 * number]
    mine, other, total = refs[2 * number : 2 * number + 3]
    held, done = refs[2 * number + 3 : -1], refs[-1]
    pieces = []
    for rows, weight, kept in zip(rows_refs, weight_refs, held):
        for start in range(0, rows.shape[1], tile):
            at = pl.ds(start, tile)
            source, target = (weight.at[:, at], kept.at[:, at]) if turned else (weight.at[at, :], kept.at[at, :])
            copy = pltpu.make_async_copy(source, target, done.at[len(pieces)])
            copy.start()
            pieces.append((copy, rows, kept, slice(start, start + tile)))
    for index, (copy, rows, kept, at) in enumerate(pieces):
        copy.wait()
        if turned:
            found = dot_nt(rows[:, at], kept[:, at])
        else:
            found = dot_nn(rows[:, at], kept[at, :])
        total[...] = total[...] + found if index else found
    half = mine.shape[0]
    mine[...] = total[:half, :]
    other[...] = total[half:, :]


def rows_sum(arrays, weights, block, rows, turned):
    tile = 512
    width = weights[0].shape[0] if turned else weights[0].shape[1]
    half = pl.BlockSpec((rows // 2, width), lambda j: (0, 0))
    depth = sum(a.shape[1] for a in arrays)
    return pl.pallas_call(
        functools.partial(rows_sum_kernel, len(arrays), tile, turned),
        grid_spec=pltpu.PrefetchScalarGridSpec(
            num_scalar_prefetch=0,
            grid=(1,),
            in_specs=[pl.BlockSpec((rows, a.shape[1]), lambda j: (block, 0)) for a in arrays]
            + [pl.BlockSpec(memory_space=pl.ANY)] * len(weights),
            out_specs=[half, half],
            scratch_shapes=[pltpu.VMEM((rows, width), jnp.float32)]
            + [pltpu.VMEM(w.shape, w.dtype) for w in weights]
            + [pltpu.SemaphoreType.DMA((depth // tile,))],
        ),
        out_shape=[jax.ShapeDtypeStruct((rows // 2, width), jnp.float32)] * 2,
        cost_estimate=pl.CostEstimate(
            flops=2 * rows * width * depth,
            bytes_accessed=2 * (rows + width) * depth + 4 * rows * width,
            transcendentals=0,
        ),
        name="rows_sum",
    )(*arrays, *weights)


def round_rows_kernel(*refs):
    out = refs[-1]
    at = 0
    for part in refs[:-1]:
        size = part.shape[0]
        out[at : at + size, :] = (2.0 * part[...]).astype(jnp.bfloat16)
        at += size


def round_rows(parts):
    vmem = pl.BlockSpec(memory_space=pltpu.VMEM)
    rows, width = sum(part.shape[0] for part in parts), parts[0].shape[1]
    return pl.pallas_call(
        round_rows_kernel,
        in_specs=[vmem] * len(parts),
        out_specs=vmem,
        out_shape=jax.ShapeDtypeStruct((rows, width), jnp.bfloat16),
        cost_estimate=pl.CostEstimate(flops=rows * width, bytes_accessed=6 * rows * width, transcendentals=0),
        name="round_rows",
    )(*parts)


def causal(first, places):
    size = places.shape[1]
    column = jnp.broadcast_to(places, (size, size))
    row = column.T
    return (row >= column) & ((column >= first) | (row < first)), row


def block_decay(rates, first, seen, row):
    size = rates.shape[1]
    nth = lax.broadcasted_iota(jnp.int32, (size, size), 1).astype(jnp.float32)
    per_row = jnp.sum(jnp.where(nth <= row, rates, 0.0), axis=1, keepdims=True)
    down = jnp.broadcast_to(per_row, (size, size))
    weights = jnp.exp(jnp.where(seen, down - down.T, -jnp.inf))
    place = row[:, :1]
    last = jnp.sum(rates, axis=1, keepdims=True)
    whole = first >= size
    reach = jnp.where(place < first, jnp.exp(per_row), 0.0)
    trail = jnp.where((place >= first) | whole, jnp.exp(last - per_row), 0.0)
    keep = jnp.where(whole, jnp.exp(last), 0.0)
    return weights, reach, trail, keep


def head_lanes(head):
    return slice(head * DK, (head + 1) * DK), slice(head * DV, (head + 1) * DV), slice(head * BLK, (head + 1) * BLK)


def retain_forward_kernel(
    slot_ref, info_ref, places_ref, q_ref, q_rest_ref, k_ref, k_rest_ref, v_ref, gate_ref,
    normed_ref, gated_ref, state_ref, weights_ref, scores_ref, column_ref, state,
):
    @pl.when(pl.program_id(0) == 0)
    def _():
        state[...] = jnp.zeros_like(state)

    first = info_ref[0, 1:2, :1]
    seen, row = causal(first, places_ref[...])
    number = lax.broadcasted_iota(jnp.int32, column_ref.shape[2:], 1)
    for head in range(state.shape[0]):
        key, val, lane = head_lanes(head)
        weights, reach, trail, keep = block_decay(info_ref[0, 0:1, lane], first, seen, row)
        q, k, v = q_ref[:, key], k_ref[:, key], v_ref[:, val]
        held = state[head].astype(jnp.bfloat16)
        state_ref[head, 0] = held
        scores = dot_nt(q, k) + (dot_nt(q_rest_ref[:, key], k) + dot_nt(q, k_rest_ref[:, key]))
        scores = (scores * weights).astype(jnp.bfloat16)
        retained = dot_nn(scores, v) + reach * dot_nn(q, held)
        state[head] = keep * state[head] + dot_tn((k * trail).astype(jnp.bfloat16), v)
        normed, inverse = norm_parts(retained)
        gate = gate_ref[:, val].astype(jnp.float32)
        gated_ref[:, val] = (gate * jax.nn.sigmoid(gate) * normed).astype(jnp.bfloat16)
        normed_ref[:, val] = normed
        weights_ref[head, 0] = weights
        scores_ref[head, 0] = scores
        column_ref[head, 0] = jnp.where(
            number == 0, reach, jnp.where(number == 1, trail, jnp.where(number == 2, inverse, keep))
        )


def retain_backward_kernel(
    slot_ref, q_ref, k_ref, v_ref, gate_ref, normed_ref, state_ref, weights_ref, scores_ref, column_ref, up_ref,
    dq_ref, dk_ref, dv_ref, dgate_ref, beyond,
):
    @pl.when(pl.program_id(0) == 0)
    def _():
        beyond[...] = jnp.zeros_like(beyond)

    for head in range(beyond.shape[0]):
        key, val, _ = head_lanes(head)
        column = column_ref[head, 0]
        reach, trail, inverse, keep = column[:, 0:1], column[:, 1:2], column[:, 2:3], column[0:1, 3:4]
        weights, scores = weights_ref[head, 0], scores_ref[head, 0]
        q, k, v, normed = q_ref[:, key], k_ref[:, key], v_ref[:, val], normed_ref[:, val]
        gate, up = gate_ref[:, val].astype(jnp.float32), up_ref[:, val].astype(jnp.float32)
        sig = jax.nn.sigmoid(gate)
        silu = gate * sig
        dgate_ref[:, val] = (up * normed * (sig + silu * (1.0 - sig))).astype(jnp.bfloat16)
        g = up * silu
        mean_g = jnp.mean(g, axis=-1, keepdims=True)
        mean_gn = jnp.mean(g * normed, axis=-1, keepdims=True)
        grad = (g - mean_g - normed * mean_gn) * inverse
        after_block = beyond[head].astype(jnp.bfloat16)
        dscores = (half_split_dot(grad, v, dot_nt) * weights).astype(jnp.bfloat16)
        grad = grad.astype(jnp.bfloat16)
        q_reach = (q * reach).astype(jnp.bfloat16)
        dq_ref[:, key] = (dot_nn(dscores, k) + reach * dot_nt(grad, state_ref[head, 0])).astype(jnp.bfloat16)
        dk = dot_tn(dscores, q) + trail * dot_nt(v, after_block)
        dk_ref[:, key] = (dk * (1.0 / math.sqrt(DK))).astype(jnp.bfloat16)
        dv_ref[:, val] = (dot_tn(scores, grad) + trail * dot_nn(k, after_block)).astype(jnp.bfloat16)
        beyond[head] = keep * beyond[head] + dot_tn(q_reach, grad)


def retain_specs(heads, blocks, width, reverse):
    at = (lambda b: blocks - 1 - b) if reverse else (lambda b: b)
    info = pl.BlockSpec((1, 8, width), lambda b, slot: (at(b), 0, 0))
    places = pl.BlockSpec((1, BLK), lambda b, slot: (0, 0))
    key = pl.BlockSpec((BLK, heads * DK), lambda b, slot: (slot[at(b)], 0))
    val = pl.BlockSpec((BLK, heads * DV), lambda b, slot: (slot[at(b)], 0))
    held = [
        pl.BlockSpec((heads, 1, up, across), lambda b, slot: (0, at(b), 0, 0))
        for up, across in ((DK, DV), (BLK, BLK), (BLK, BLK), (BLK, 128))
    ]
    return info, places, key, val, held


def retain_forward(slot, info, places, queries_keys, v, gate):
    rows, heads = v.shape[0], v.shape[1] // DV
    blocks = rows // BLK
    info_at, places_at, key, val, held = retain_specs(heads, blocks, info.shape[2], False)
    return pl.pallas_call(
        retain_forward_kernel,
        grid_spec=pltpu.PrefetchScalarGridSpec(
            num_scalar_prefetch=1,
            grid=(blocks,),
            in_specs=[info_at, places_at, key, key, key, key, val, val],
            out_specs=[val, val, *held],
            scratch_shapes=[pltpu.VMEM((heads, DK, DV), jnp.float32)],
        ),
        out_shape=[
            jax.ShapeDtypeStruct((rows, heads * DV), jnp.float32),
            jax.ShapeDtypeStruct((rows, heads * DV), jnp.bfloat16),
            jax.ShapeDtypeStruct((heads, blocks, DK, DV), jnp.bfloat16),
            jax.ShapeDtypeStruct((heads, blocks, BLK, BLK), jnp.float32),
            jax.ShapeDtypeStruct((heads, blocks, BLK, BLK), jnp.bfloat16),
            jax.ShapeDtypeStruct((heads, blocks, BLK, 128), jnp.float32),
        ],
        cost_estimate=pl.CostEstimate(
            flops=2 * heads * rows * (BLK * (3 * DK + DV) + 2 * DK * DV),
            bytes_accessed=rows * heads * (8 * DK + 12 * DV),
            transcendentals=rows * heads * (BLK + DV),
        ),
        name="retain_forward",
    )(slot, info, places, *queries_keys, v, gate)


def retain_backward(slot, queries_keys, v, gate, normed, held, up):
    rows, heads = v.shape[0], v.shape[1] // DV
    blocks = rows // BLK
    _, _, key, val, held_at = retain_specs(heads, blocks, 0, True)
    return pl.pallas_call(
        retain_backward_kernel,
        grid_spec=pltpu.PrefetchScalarGridSpec(
            num_scalar_prefetch=1,
            grid=(blocks,),
            in_specs=[key, key, val, val, val, *held_at, val],
            out_specs=[key, key, val, val],
            scratch_shapes=[pltpu.VMEM((heads, DK, DV), jnp.float32)],
        ),
        out_shape=[
            jax.ShapeDtypeStruct((rows, heads * DK), jnp.bfloat16),
            jax.ShapeDtypeStruct((rows, heads * DK), jnp.bfloat16),
            jax.ShapeDtypeStruct((rows, heads * DV), jnp.bfloat16),
            jax.ShapeDtypeStruct((rows, heads * DV), jnp.bfloat16),
        ],
        cost_estimate=pl.CostEstimate(
            flops=2 * heads * rows * (BLK * (5 * DK + 3 * DV) + 4 * DK * DV),
            bytes_accessed=rows * heads * (12 * DK + 20 * DV),
            transcendentals=rows * heads * (BLK + DV),
        ),
        name="retain_backward",
    )(slot, *queries_keys, v, gate, normed, *held, up)


def norm_grad(grad, gain, centred_unit, inverse):
    e = grad * gain
    mean_e = jnp.mean(e, axis=-1, keepdims=True)
    mean_en = jnp.mean(e * centred_unit, axis=-1, keepdims=True)
    return (e - mean_e - centred_unit * mean_en) * inverse


def local_gather(
    tokens,
    first_gain,
    query_weight,
    key_weight,
    value_weight,
    gate_weight,
    output_weight,
    second_gain,
    gelu_weight,
    linear_weight,
    down_weight,
    log_decay,
    first_start,
    cotangent,
):
    bf16, f32 = jnp.bfloat16, jnp.float32
    shards = lax.axis_size(SEQ)
    shard, group = lax.axis_index(SEQ), lax.axis_index(HEAD)
    rows, width = tokens.shape
    half = rows // 2
    total = shards * rows
    quarter = half // 2
    slab = width // shards
    key_scale = 1.0 / math.sqrt(DK)
    chip, core = (group // 2).astype(jnp.int32), (group % 2).astype(jnp.int32)
    place = shard.astype(jnp.int32)

    def narrow(a):
        return (2.0 * a).astype(bf16)

    def slab_of(a, at):
        return lax.dynamic_slice_in_dim(a, at * slab, slab, 1)

    def in_order(mine, other):
        return jnp.where(core == 0, jnp.concatenate([mine, other]), jnp.concatenate([other, mine]))

    def far_hops():
        return [[(i, (i + hop) % shards) for i in range(shards)] for hop in range(2, shards, 2)]

    def over_steps(own_parts, steps, groups, weights, pieces, scales, turned):
        common = (weights, pieces, scales, turned, place)
        found = rows_product(own_parts, rows // len(own_parts), *common, shards - 2, total)
        for index, group in enumerate(groups):
            parts = [part for step in group for part in steps[step]]
            last = index + 1 == len(groups)
            block = shards - 1 if last else group[0] // len(group)
            found = rows_product(parts, parts[0].shape[0], *common, block, total, found)
        return found

    normed_own, *normed_half, info = norm_start(core, first_start, tokens, first_gain, log_decay)
    came = ring_gather(normed_half)
    info = info[None]
    for index in range(shards.bit_length() - 1):
        moved = lax.ppermute(info, SEQ, [(i, i ^ (1 << index)) for i in range(shards)])
        upper = (place >> index) & 1 == 1
        info = jnp.concatenate([jnp.where(upper, moved, info), jnp.where(upper, info, moved)], axis=0)
    slot = ring_slots()
    lanes = jnp.arange(half)
    places = jnp.concatenate([core * half + lanes, (1 - core) * half + lanes]).astype(f32)[None]

    cotangent_half = of_rows(cotangent, core * half, half)
    cotangent_own = jnp.concatenate([cotangent_half, of_rows(cotangent, (1 - core) * half, half)], axis=0)
    cotangent_half = cotangent_half.astype(f32)
    token_half = of_rows(tokens, core * half, half).astype(f32)
    first_unit, first_inverse = norm_parts(token_half)

    def far_start(share):
        share = of_rows(share, chip * quarter, quarter)
        return [lax.ppermute(share, SEQ, hop) for hop in far_hops()]

    def far_parts(came):
        parts = []
        for item in came:
            both = [item, lax.ppermute(item, HEAD, ACROSS)]
            parts += both + [other_core(part) for part in both]
        return parts

    cotangent_far = far_start(after(0.5 * cotangent_half, came[-1][1]))
    cotangent_far = far_parts(cotangent_far)
    cotangent_far = round_rows(cotangent_far)

    in_slab, *queries_keys, values, gate_pre = over_steps(
        [normed_own],
        came,
        [[step] for step in range(shards // 2)],
        [query_weight, key_weight, value_weight, gate_weight],
        [2, 2, 1, 1],
        [1.0, key_scale, 1.0, 1.0],
        False,
    )
    normed, gated, *held = retain_forward(slot, info, places, queries_keys, values, gate_pre)

    out_mine, out_other = rows_sum([gated], [output_weight], shards - 2, rows, False)
    residual = token_half + head_total(out_mine, out_other)
    mid_unit, mid_inverse = norm_parts(residual)
    normed_mid_half = 0.5 * (mid_unit * second_gain)
    normed_mid_own = narrow(jnp.concatenate([normed_mid_half, other_core(normed_mid_half)], axis=0))
    mid_far = far_start(normed_mid_half)

    def hidden_mix(pre_gate, up_branch):
        return jax.nn.gelu(pre_gate, approximate=False) * up_branch

    def feed_forward(normed, grad_hidden):
        up_gate = matmul(normed, gelu_weight)
        up_proj = matmul(normed, linear_weight)
        hidden, back = jax.vjp(hidden_mix, up_gate, up_proj)
        grad_up_gate, grad_up = back(grad_hidden)
        return hidden.astype(bf16), grad_up_gate.astype(bf16), grad_up.astype(bf16)

    grad_hidden_own = transpose_right(cotangent_own, down_weight)
    hidden, grad_up_gate, grad_up = feed_forward(normed_mid_own, grad_hidden_own)

    mid_mine, mid_other = rows_sum([grad_up_gate, grad_up], [gelu_weight, linear_weight], 0, rows, True)
    grad_mid = head_total(mid_mine, mid_other)
    grad_residual = cotangent_half + norm_grad(grad_mid, second_gain, mid_unit, mid_inverse)
    second_part = 0.5 * jnp.sum(grad_mid * mid_unit, axis=0)
    branch_came = ring_gather([grad_residual])
    steps = list(range(shards // 2))
    branch_slab, grad_gated = over_steps(
        [grad_residual, other_core(grad_residual)],
        branch_came,
        [steps[:2]] + [[step] for step in steps[2:]] if shards > 4 else [[step] for step in steps],
        [output_weight],
        [1],
        [1.0],
        True,
    )

    mid_far = far_parts(mid_far)
    grad_hidden_far = transpose_right(cotangent_far, down_weight)
    normed_mid_far = round_rows(mid_far)
    hidden_far, grad_up_gate_far, grad_up_far = feed_forward(normed_mid_far, grad_hidden_far)

    res_mine, res_other = rows_sum([hidden], [down_weight], 0, rows, False)
    hidden_total = head_total(res_mine, after(res_other, branch_came[0][0]))

    def pair_slab(a):
        return lax.dynamic_slice_in_dim(a, shard // 2 * (2 * slab), 2 * slab, 1)

    def pair_sum(left, right, left_far, right_far, dim):
        found = transpose_left(left, right)
        found = found + transpose_left(left_far, right_far)
        kept = lax.dynamic_slice_in_dim(found, shard % 2 * slab, slab, dim)
        sent = lax.dynamic_slice_in_dim(found, (1 - shard % 2) * slab, slab, dim)
        sent = lax.ppermute(after(sent, branch_came[-2][0]), SEQ, [(i, i ^ 1) for i in range(shards)])
        return kept + sent

    mid_slab, mid_slab_far = pair_slab(normed_mid_own), pair_slab(normed_mid_far)
    wgrad_down = pair_sum(hidden, pair_slab(cotangent_own), hidden_far, pair_slab(cotangent_far), 1)
    wgrad_gelu = pair_sum(mid_slab, grad_up_gate, mid_slab_far, grad_up_gate_far, 0)
    wgrad_linear = pair_sum(mid_slab, grad_up, mid_slab_far, grad_up_far, 0)

    wgrad_output = transpose_left(gated, branch_slab)
    grad_queries, grad_keys, grad_values, grad_gate_pre = retain_backward(
        slot, queries_keys[::2], values, gate_pre, normed, held, grad_gated
    )

    in_mine, in_other = rows_sum(
        [grad_queries, grad_keys, grad_values, grad_gate_pre],
        [query_weight, key_weight, value_weight, gate_weight],
        shards - 2,
        rows,
        True,
    )
    result = 0.5 * (after(residual, in_mine) + hidden_total)
    output_rows = narrow(in_order(result, other_core(result)))
    grad_in = head_total(in_mine, in_other)
    wgrad_query = transpose_left(in_slab, grad_queries)
    wgrad_key = transpose_left(in_slab, grad_keys)
    wgrad_value = transpose_left(in_slab, grad_values)
    wgrad_gate = transpose_left(in_slab, grad_gate_pre)
    first_part = gain_part(core, tokens, in_mine, in_other)
    gains = exchange_sum(jnp.concatenate([first_part, second_part[None]]), SEQ)
    gains = gains + other_core(gains)
    grad_half = 0.5 * (grad_residual + norm_grad(grad_in, first_gain, first_unit, first_inverse))
    other_half = other_core(grad_half)
    grad_tokens = narrow(in_order(grad_half, other_half))
    gains = gains + lax.ppermute(after(gains, grad_in), HEAD, ACROSS)
    gains = slab_of(gains, shard)
    return (
        output_rows,
        grad_tokens,
        gains[0],
        wgrad_query,
        wgrad_key,
        wgrad_value,
        wgrad_gate,
        wgrad_output,
        gains[1],
        wgrad_gelu,
        wgrad_linear,
        wgrad_down,
    )


def local(*arrays):
    tokens = lax.axis_size(SEQ) * arrays[0].shape[0]
    columns = sum(w.shape[1] for w in (*arrays[2:6], *arrays[8:10])) + arrays[6].shape[0] + arrays[10].shape[0]
    shards, groups = lax.axis_size(SEQ), lax.axis_size(HEAD)
    if groups == 4 and shards in (4, 8, 16) and arrays[0].shape[0] == BLK and 4 * tokens <= groups * columns:
        return local_gather(*arrays)
    return local_scatter(*arrays)


def solution(mesh):
    return jax.shard_map(
        local,
        mesh=mesh,
        in_specs=(
            P(SEQ, None),
            P(),
            P(None, HEAD),
            P(None, HEAD),
            P(None, HEAD),
            P(None, HEAD),
            P(HEAD, None),
            P(),
            P(None, HEAD),
            P(None, HEAD),
            P(HEAD, None),
            P(HEAD, SEQ),
            P(SEQ),
            P(SEQ, None),
        ),
        out_specs=(
            P(SEQ, None),
            P(SEQ, None),
            P(SEQ),
            P(SEQ, HEAD),
            P(SEQ, HEAD),
            P(SEQ, HEAD),
            P(SEQ, HEAD),
            P(HEAD, SEQ),
            P(SEQ),
            P(SEQ, HEAD),
            P(SEQ, HEAD),
            P(HEAD, SEQ),
        ),
        check_vma=False,
    )
```
